32 devices in a mesh: fsdp: 4 (over x, core), ctx: 2 (over y), tp: 4 (over z).
Axes of the slice: x: 2, y: 2, z: 4, core: 2. Of those that a mesh axis runs over, the one named last changes fastest.
Arguments:
- tokens: bfloat16 [8, 1024, 768], P('fsdp', 'ctx'), may hold values from -6 to 6
- segments: int32 [8, 1024], P('fsdp', 'ctx'), may hold values from 0 to 3, never falling along the last dimension, each value on 1 to 768 neighbouring positions
- ln_gains: bfloat16 [2, 768], P(None, 'fsdp'), may hold values from 0.5 to 1.5
- ln_biases: bfloat16 [2, 768], P(None, 'fsdp'), may hold values from -1.75 to 1.75
- w_qkv: bfloat16 [3, 768, 768], P(None, 'fsdp', 'tp'), may hold values from -0.21875 to 0.21875
- bias_qv: bfloat16 [2, 12, 64], P(None, 'tp', 'fsdp'), may hold values from -3 to 3
- w_out: bfloat16 [768, 768], P('tp', 'fsdp'), may hold values from -1.25 to 1.25
- out_biases: bfloat16 [2, 768], P(None, 'fsdp'), may hold values from -1.75 to 1.75
- w_up: bfloat16 [768, 3072], P('fsdp', 'tp'), may hold values from -0.21875 to 0.21875
- up_bias: bfloat16 [48, 64], P('tp', 'fsdp'), may hold values from -3 to 3
- w_down: bfloat16 [3072, 768], P('tp', 'fsdp'), may hold values from -0.109375 to 0.109375
- cotangent: bfloat16 [8, 1024, 768], P('fsdp', 'ctx'), may hold values from -6 to 6
Outputs:
- output: bfloat16 [8, 1024, 768], P('fsdp', 'ctx')
- grad_tokens: float32 [8, 1024, 768], P('fsdp', 'ctx')
- grad_ln_gains: float32 [2, 768], P(None, 'fsdp')
- grad_ln_biases: float32 [2, 768], P(None, 'fsdp')
- grad_qkv: float32 [3, 768, 768], P(None, 'fsdp', 'tp')
- grad_bias_qv: float32 [2, 12, 64], P(None, 'tp', 'fsdp')
- grad_out_proj: float32 [768, 768], P('tp', 'fsdp')
- grad_out_biases: float32 [2, 768], P(None, 'fsdp')
- grad_up: float32 [768, 3072], P('fsdp', 'tp')
- grad_up_bias: float32 [48, 64], P('tp', 'fsdp')
- grad_down: float32 [3072, 768], P('tp', 'fsdp')
The draws below stay inside these ranges and needn't reach their ends.
Inputs may be any that keep to these rules, and one draw needn't show every extreme that they name: `segments`: within each sequence the numbers never fall; each document holds 1 to 768 positions, and one document of each sequence exactly that many.
All inputs are finite; a program needn't handle non-finite values.
Results may differ from the reference program's by a relative error of at most 0.017.
Values may be sent and summed in bfloat16 or wider, within the bound.
No kernel may reach another device: no remote copies, remote signals or barrier semaphores. Data moves between devices by JAX's collectives and lax.ppermute only.
A program may use at most 384 MiB of HBM per device.

```python
import math
import jax
import jax.numpy as jnp
import numpy as np
from jax import lax

D = 768
HEADS = 12
HD = 64
FF = 3072
LEN = 1024
DOCS = 4
SEQS = 8


def shard_levels(stream_key, extent, pieces, least, largest):
    level = 1.0
    for dim, parts in pieces:
        draws = jax.random.uniform(jax.random.fold_in(jax.random.fold_in(stream_key, 6), dim), (parts,), jnp.float32, least / len(pieces), largest / len(pieces))
        level = level * jnp.repeat(jnp.exp(draws), extent[dim] // parts).reshape((-1,) + (1,) * (len(extent) - 1 - dim))
    return level


def length_profile(count, total, bound, lean):
    weights = [(1 << 20) // math.isqrt(rank ** lean) + 1 for rank in range(2, count + 1)]
    surplus, holding = total - bound - (count - 1), [1] * (count - 1)
    while surplus > 0:
        candidates = [i for i in range(count - 1) if holding[i] < bound]
        pool, budget = sum([weights[i] for i in candidates]), surplus
        for i in candidates:
            more = min(bound - holding[i], max(1, budget * weights[i] // pool), surplus)
            holding[i] = holding[i] + more
            surplus = surplus - more
    return np.array([bound] + holding)


def ragged_sizes(rng, number_of, total, limit, lean):
    if number_of == 2:
        one = jax.random.randint(rng, (), max(1, total - limit), min(limit, total - 1) + 1)
        return jnp.stack([one, total - one])
    sizes = jnp.asarray(length_profile(number_of, total, limit, lean), jnp.int32)
    couples = (number_of - 1) // 2
    source_of, receiver = sizes[1:1 + 2 * couples:2], sizes[2:2 + 2 * couples:2]
    room = jnp.minimum(source_of - 1, limit - receiver)
    passed = jax.random.randint(jax.random.fold_in(rng, 1), (couples,), 0, 1 << 20) % (room + 1)
    sizes = sizes.at[1:1 + 2 * couples:2].set(source_of - passed).at[2:2 + 2 * couples:2].set(receiver + passed)
    return sizes[jax.random.permutation(jax.random.fold_in(rng, 2), number_of)]


def normal_values(rng, dims, spread, most, cuts=(), held_as=jnp.bfloat16):
    array = jax.random.normal(rng, dims, jnp.float32) * spread
    if len(cuts) > 0:
        array = shard_levels(rng, dims, cuts, -0.22, 0.18) * array
    return jnp.clip(array, min=-most, max=most).astype(held_as)


def setup_inputs(seed: int = 0) -> dict:
    splits = jax.random.split(jax.random.key(seed), 13)
    tokens = normal_values(splits[0], (SEQS, LEN, D), 1.0, 6.0, ((0, 4), (1, 2)))
    segments = jax.vmap(lambda own: jnp.searchsorted(jnp.cumsum(ragged_sizes(own, DOCS, LEN, 3 * LEN // 4, 2)), jnp.arange(LEN), side="right"))(jax.random.split(splits[1], SEQS)).reshape((SEQS, LEN)).astype(jnp.int32)
    ln_gains = jnp.clip(1.0 + 0.1 * jax.random.normal(splits[2], (2, D), jnp.float32), 0.5, 1.5).astype(jnp.bfloat16)
    ln_biases = normal_values(splits[3], (2, D), 0.3, 1.75, ((1, 4),))
    w_qkv = normal_values(splits[4], (3, D, HEADS * HD), D ** -0.5, 0.21875, ((1, 4), (2, 4)))
    bias_qv = normal_values(splits[5], (2, HEADS, HD), 0.5, 3.0, ((1, 4), (2, 4)))
    w_out = normal_values(splits[6], (HEADS * HD, D), (HEADS * HD // 32) ** -0.5, 1.25, ((0, 4), (1, 4)))
    out_biases = normal_values(splits[7], (2, D), 0.3, 1.75, ((1, 4),))
    w_up = normal_values(splits[8], (D, FF), D ** -0.5, 0.21875, ((0, 4), (1, 4)))
    up_bias = normal_values(splits[9], (FF // 64, 64), 0.5, 3.0, ((0, 4), (1, 4)))
    w_down = normal_values(splits[10], (FF, D), FF ** -0.5, 0.109375, ((0, 4), (1, 4)))
    cotangent = normal_values(splits[11], (SEQS, LEN, D), 1.0, 6.0, ((0, 4), (1, 2)))
    return {"tokens": tokens, "segments": segments, "ln_gains": ln_gains, "ln_biases": ln_biases, "w_qkv": w_qkv, "bias_qv": bias_qv, "w_out": w_out, "out_biases": out_biases, "w_up": w_up, "up_bias": up_bias, "w_down": w_down, "cotangent": cotangent}


eps = 1e-05
highest = lax.Precision.HIGHEST

@jax.custom_vjp
def low(v):
    return lax.optimization_barrier(v.astype(jnp.bfloat16)).astype(jnp.float32)

@jax.custom_vjp
def low_back(v):
    return v

def low_keep(v):
    return (low(v), None)

def low_pass(kept, grad):
    return (grad,)

def back_keep(v):
    return (v, None)

def back_low(kept, grad):
    return (low(grad),)
low.defvjp(low_keep, low_pass)
low_back.defvjp(back_keep, back_low)

def layer_norm(values_in, gain, shift):
    average = lax.optimization_barrier(jnp.mean(values_in, axis=-1, keepdims=True))
    centered = values_in - average
    variance = lax.optimization_barrier(jnp.mean(centered * centered, axis=-1, keepdims=True))
    return centered * lax.rsqrt(variance + eps) * gain + shift

def product(left, right):
    return jnp.dot(left, right, precision=highest)

def attention_core(queries, key_rows, values, segment):
    scores = low_back(jnp.einsum('qhd,khd->hqk', queries, key_rows, precision=highest) * 0.125)
    places = jnp.arange(segment.shape[0], dtype=jnp.int32)
    allowed = (segment[:, None] == segment[None, :]) & (places[None, :] <= places[:, None])
    scores = jnp.where(allowed[None], scores, -1e+30)
    row_max = lax.optimization_barrier(jnp.max(scores, axis=-1, keepdims=True))
    exponent = jnp.exp(scores - row_max)
    probability = exponent / lax.optimization_barrier(jnp.sum(exponent, axis=-1, keepdims=True))
    return jnp.einsum('hqk,khd->qhd', low(probability), values, precision=highest)

def forward_sequence(inputs, weights, segment):
    gain_rows, shifts, qkv_proj, qv_bias, out_proj, branch_bias, up_proj, up_shift, down_proj = weights
    length = inputs.shape[0]
    head_shape = (length, HEADS, HD)
    normed = low(layer_norm(inputs, gain_rows[0], shifts[0]))
    queries = low(low_back(product(normed, qkv_proj[0]) + qv_bias[0].reshape(-1)))
    key_rows = low(low_back(product(normed, qkv_proj[1])))
    values = low(low_back(product(normed, qkv_proj[2]) + qv_bias[1].reshape(-1)))
    mixture = attention_core(queries.reshape(head_shape), key_rows.reshape(head_shape), values.reshape(head_shape), segment)
    attended = low(low_back(mixture.reshape(length, HEADS * HD)))
    branch = low_back(product(attended, out_proj) + branch_bias[0])
    hidden = inputs + branch
    normed_two = low(layer_norm(hidden, gain_rows[1], shifts[1]))
    pre_act = low_back(product(normed_two, up_proj) + up_shift.reshape(-1))
    activated = low(low_back(jax.nn.gelu(pre_act, approximate=True)))
    second = low_back(product(activated, down_proj) + branch_bias[1])
    return hidden + second

def reference(tokens, segments, ln_gains, ln_biases, w_qkv, bias_qv, w_out, out_biases, w_up, up_bias, w_down, cotangent):
    params = (ln_gains.astype(jnp.float32), ln_biases.astype(jnp.float32), w_qkv.astype(jnp.float32), bias_qv.astype(jnp.float32), w_out.astype(jnp.float32), out_biases.astype(jnp.float32), w_up.astype(jnp.float32), up_bias.astype(jnp.float32), w_down.astype(jnp.float32))
    token_rows = tokens.astype(jnp.float32)
    cot_rows = cotangent.astype(jnp.float32)

    def one_sequence(running, sequence_item):
        seq_tokens, seq_segment, seq_cot = sequence_item

        def closed(inputs, weights):
            return forward_sequence(inputs, weights, seq_segment)
        output, pullback = jax.vjp(closed, seq_tokens, params)
        grad_inputs, grad_weights = pullback(seq_cot)
        running = tuple((summed + piece_grad for summed, piece_grad in zip(running, grad_weights)))
        return (running, (output, grad_inputs))
    initial = tuple((jnp.zeros(weight.shape, jnp.float32) for weight in params))
    totals, (outputs, grad_inputs) = lax.scan(one_sequence, initial, (token_rows, segments, cot_rows))
    return (outputs.astype(jnp.bfloat16), grad_inputs, totals[0], totals[1], totals[2], totals[3], totals[4], totals[5], totals[6], totals[7], totals[8])
```

```python
import functools
import math

import jax
import jax.numpy as jnp
from jax import lax
from jax.experimental import pallas as pl
from jax.experimental.pallas import tpu as pltpu
from jax.sharding import PartitionSpec as P

HD = 64
QB = 256
eps = 1e-05
masked_score = -1e30
score_scale = 0.125 * math.log2(math.e)
f32 = jnp.float32
bf16 = jnp.bfloat16


def swap(v, axis, bit, size):
    return lax.ppermute(v, axis, [(i, i ^ bit) for i in range(size)])


def dot(a, b):
    return lax.dot_general(a, b, (((1,), (0,)), ((), ())), preferred_element_type=f32)


def turned(v):
    return v.astype(f32).T.astype(v.dtype)


def starts_of(seg):
    start = jnp.zeros(seg.shape, jnp.int32)
    for number in range(3):
        count = jnp.sum((seg == number).astype(jnp.int32), axis=1, keepdims=True)
        start = start + jnp.where(seg > number, count, 0)
    return start


def allowed_block(start, first, width):
    place = lax.broadcasted_iota(jnp.int32, (width, QB), 0)
    allowed = place >= start[:, first : first + QB]
    query = lax.broadcasted_iota(jnp.int32, (width, QB), 1) + first
    return allowed & (place <= query)


def attention_forward(seg_ref, qkv_ref, out_ref, log_ref):
    start = starts_of(seg_ref[...])
    length = qkv_ref.shape[2]
    heads = qkv_ref.shape[1] // HD
    for head in range(heads):
        rows = slice(head * HD, (head + 1) * HD)
        keys = turned(qkv_ref[1, rows, :])
        for first in range(0, length, QB):
            width = first + QB
            cols = slice(first, first + QB)
            scores = dot(keys[:width], qkv_ref[0, rows, cols]) * score_scale
            scores = jnp.where(allowed_block(start, first, width), scores, masked_score)
            top = jnp.max(scores, axis=0, keepdims=True)
            weight = jnp.exp2(scores - top)
            total = jnp.sum(weight, axis=0, keepdims=True)
            mixed = dot(qkv_ref[2, rows, :width], weight.astype(bf16))
            out_ref[rows, cols] = (mixed / total).astype(bf16)
            log_ref[head : head + 1, cols] = top + jnp.log2(total)


def attention_backward(seg_ref, qkv_ref, grad_ref, log_ref, out_ref, key_sum, value_sum):
    start = starts_of(seg_ref[...])
    length = qkv_ref.shape[2]
    width_heads = qkv_ref.shape[1]
    for head in range(width_heads // HD):
        rows = slice(head * HD, (head + 1) * HD)
        keys = turned(qkv_ref[1, rows, :])
        values = turned(qkv_ref[2, rows, :])
        queries = turned(qkv_ref[0, rows, :])
        grads = turned(grad_ref[rows, :])
        key_sum[...] = jnp.zeros_like(key_sum)
        value_sum[...] = jnp.zeros_like(value_sum)
        for first in range(0, length, QB):
            width = first + QB
            cols = slice(first, first + QB)
            scores = dot(keys[:width], qkv_ref[0, rows, cols]) * score_scale
            prob = jnp.exp2(scores - log_ref[head : head + 1, cols])
            prob = jnp.where(allowed_block(start, first, width), prob, 0.0)
            grad_prob = dot(values[:width], grad_ref[rows, cols])
            inner = jnp.sum(prob * grad_prob, axis=0, keepdims=True)
            grad_scores = (prob * (grad_prob - inner) * 0.125).astype(bf16)
            grad_query = dot(qkv_ref[1, rows, :width], grad_scores)
            out_ref[cols, rows] = grad_query.T.astype(bf16)
            key_sum[:width] += dot(grad_scores, queries[cols])
            value_sum[:width] += dot(prob.astype(bf16), grads[cols])
        out_ref[:, width_heads + head * HD : width_heads + (head + 1) * HD] = key_sum[...].astype(bf16)
        out_ref[:, 2 * width_heads + head * HD : 2 * width_heads + (head + 1) * HD] = value_sum[
            ...
        ].astype(bf16)


def normalized(v):
    mean = jnp.mean(v, axis=-1, keepdims=True)
    centered = v - mean
    scale = lax.rsqrt(jnp.mean(centered * centered, axis=-1, keepdims=True) + eps)
    return centered * scale, scale


def norm_back(hat, scale, gain, grad):
    scaled = grad * gain
    first = jnp.mean(scaled, axis=-1, keepdims=True)
    second = jnp.mean(scaled * hat, axis=-1, keepdims=True)
    return scale * (scaled - first - hat * second)


def gelu_pair(u):
    slope = math.sqrt(2 / math.pi)
    bent = jnp.tanh(slope * (u + 0.044715 * u * u * u))
    value = 0.5 * u * (1 + bent)
    rate = 0.5 * (1 + bent) + 0.5 * u * (1 - bent * bent) * slope * (1 + 3 * 0.044715 * u * u)
    return value, rate


def arranged(parts, at):
    low, high = (at & 1) == 1, (at >> 1) == 1
    p0, p1, p2, p3 = parts
    a0, a1 = jnp.where(low, p1, p0), jnp.where(low, p0, p1)
    a2, a3 = jnp.where(low, p3, p2), jnp.where(low, p2, p3)
    return [
        jnp.where(high, a2, a0),
        jnp.where(high, a3, a1),
        jnp.where(high, a0, a2),
        jnp.where(high, a1, a3),
    ]


def pick(v, index, axis):
    return lax.dynamic_index_in_dim(v, index, axis, keepdims=False)


def block(
    tokens,
    segments,
    ln_gains,
    ln_biases,
    w_qkv,
    bias_qv,
    w_out,
    out_biases,
    w_up,
    up_bias,
    w_down,
    cotangent,
    *,
    fsdp,
    ctx,
    tp,
):
    seq_count, half, width = tokens.shape
    part = w_up.shape[0]
    heads_width = w_qkv.shape[2]
    head_count = heads_width // HD
    hidden_part = w_up.shape[1]
    assert ctx == 2 and seq_count == 2 and tp == 4
    f = lax.axis_index("fsdp")
    y = lax.axis_index("ctx")
    z = lax.axis_index("tp")
    piece = half // tp
    pair = z >> 1
    member = z & 1

    def swap_y(v):
        return swap(v, "ctx", 1, ctx)

    def swap_z(v, bit):
        return swap(v, "tp", bit, tp)

    def gather_rows(v):
        if fsdp != 4:
            return lax.all_gather(v, "fsdp", axis=0, tiled=True).reshape((fsdp,) + v.shape)
        far = swap(v, "fsdp", 2, fsdp)
        near = swap(v, "fsdp", 1, fsdp)
        cross = swap(far, "fsdp", 1, fsdp)
        return arranged([v, near, far, cross], f)

    def scatter_rows(g):
        g = g.astype(bf16)
        if fsdp != 4:
            return lax.psum_scatter(g, "fsdp", scatter_dimension=0, tiled=True).astype(f32)
        g = g.reshape(2, 2, part, g.shape[1])
        core, x = f & 1, f >> 1
        kept = pick(g, core, 1)
        got = swap(pick(g, 1 - core, 1), "fsdp", 1, fsdp)
        send = (pick(kept, 1 - x, 0).astype(f32) + pick(got, 1 - x, 0).astype(f32)).astype(bf16)
        own = pick(kept, x, 0).astype(f32) + pick(got, x, 0).astype(f32)
        return own + swap(send, "fsdp", 2, fsdp).astype(f32)

    def sum_y(g):
        g = g.astype(bf16)
        return g.astype(f32) + swap_y(g).astype(f32)

    tok_own = pick(tokens, y, 0)
    tok_got = swap_y(pick(tokens, 1 - y, 0))
    small = jnp.concatenate(
        [
            ln_gains.reshape(-1),
            ln_biases.reshape(-1),
            out_biases.reshape(-1),
            up_bias.reshape(-1),
            bias_qv.reshape(-1),
        ]
    )
    small_rows = -(-small.shape[0] // heads_width)
    small = jnp.pad(small, (0, small_rows * heads_width - small.shape[0]))
    qkv_pack = jnp.concatenate(
        [w_qkv.reshape(3 * part, heads_width), small.reshape(small_rows, heads_width)], axis=0
    )
    packs = gather_rows(qkv_pack)
    cot_rows = lax.dynamic_slice_in_dim(cotangent, pair * 2 * piece, 2 * piece, 1)
    seg_row = jnp.pad(pick(segments, 1 - y, 0).astype(bf16), (0, width - half)).reshape(1, width)
    extra_got = swap_y(jnp.concatenate([pick(cot_rows, 1 - y, 0), seg_row], axis=0))
    up_bias_far = swap_z(up_bias, 2)
    mlp_pack = jnp.concatenate([w_up, w_down.T], axis=0)
    mlp_far = swap_z(mlp_pack, 2)
    out_turned = w_out.T
    out_two = jnp.concatenate([out_turned, swap_z(out_turned, 1)], axis=1)
    out_four = jnp.concatenate([out_two, swap_z(out_two, 2)], axis=1)

    packs = [packs[i] for i in range(fsdp)]
    qkv_proj = jnp.concatenate(
        [p[: 3 * part].reshape(3, part, heads_width) for p in packs], axis=1
    )
    flat = jnp.stack([p[3 * part :].reshape(-1) for p in packs]).astype(f32)
    norms = jnp.moveaxis(flat[:, : 6 * part].reshape(fsdp, 6, part), 0, 1).reshape(6, width)
    gains, shifts, branch_bias = norms[0:2], norms[2:4], norms[4:6]
    base = 6 * part
    bias_rows, bias_cols = up_bias.shape
    up_shift = jnp.moveaxis(
        flat[:, base : base + bias_rows * bias_cols].reshape(fsdp, bias_rows, bias_cols), 0, 1
    ).reshape(-1)
    base = base + bias_rows * bias_cols
    qv_cols = bias_qv.shape[2]
    qv_bias = jnp.moveaxis(
        flat[:, base : base + 2 * head_count * qv_cols].reshape(fsdp, 2, head_count, qv_cols), 0, 2
    ).reshape(2, heads_width)
    up_far = gather_rows(jnp.pad(up_bias_far.reshape(1, -1), ((0, 0), (0, 0))))
    up_shift_far = jnp.moveaxis(
        jnp.stack([up_far[i].reshape(bias_rows, bias_cols) for i in range(fsdp)]), 0, 1
    ).reshape(-1).astype(f32)

    first_half = jnp.where(y == 0, tok_own, tok_got)
    second_half = jnp.where(y == 0, tok_got, tok_own)
    inputs = jnp.concatenate([first_half, second_half], axis=0).astype(f32)
    length = inputs.shape[0]
    seg_own = pick(segments, y, 0).astype(f32)
    seg_got = extra_got[2 * piece, :half].astype(f32)
    seg = jnp.concatenate(
        [jnp.where(y == 0, seg_own, seg_got), jnp.where(y == 0, seg_got, seg_own)]
    ).reshape(1, length).astype(jnp.int32)
    hat, _ = normalized(inputs)
    normed = (hat * gains[0] + shifts[0]).astype(bf16)
    projected = jnp.einsum("cdh,td->cht", qkv_proj, normed, preferred_element_type=f32)
    shift_rows = jnp.stack([qv_bias[0], jnp.zeros_like(qv_bias[0]), qv_bias[1]])
    qkv = (projected + shift_rows[:, :, None]).astype(bf16)
    attended, logs = pl.pallas_call(
        attention_forward,
        out_shape=(
            jax.ShapeDtypeStruct((heads_width, length), bf16),
            jax.ShapeDtypeStruct((head_count, length), f32),
        ),
        name="attention_forward",
    )(seg, qkv)

    def pieces_of(v):
        v = v.reshape(heads_width, 2, tp, piece)
        return [pick(v, z ^ k, 2).reshape(heads_width, 2 * piece) for k in range(tp)]

    att_pieces = pieces_of(attended)
    att_all = jnp.concatenate(
        [att_pieces[0]] + [swap_z(att_pieces[k], k) for k in range(1, tp)], axis=0
    )
    out_proj = jnp.concatenate([v for v in gather_rows(out_four)], axis=0)
    rows_own = lax.dynamic_slice_in_dim(inputs.reshape(2, half, width), z * piece, piece, 1).reshape(
        2 * piece, width
    )
    branch = jnp.einsum("ht,dh->td", att_all, out_proj, preferred_element_type=f32)
    hidden = rows_own + branch + branch_bias[0]
    hat_two, scale_two = normalized(hidden)
    normed_own = (hat_two * gains[1] + shifts[1]).astype(bf16)
    normed_two = jnp.concatenate([normed_own, swap_z(normed_own, 1)], axis=0)

    mlp = []
    for pack, shift in ((mlp_pack, up_shift), (mlp_far, up_shift_far)):
        got = gather_rows(pack)
        up = jnp.concatenate([got[i][:part] for i in range(fsdp)], axis=0)
        down = jnp.concatenate([got[i][part:] for i in range(fsdp)], axis=0)
        mlp.append((up, down, shift))
    cot_own = pick(cot_rows, y, 0)
    cot_got = extra_got[: 2 * piece]
    cot_two = jnp.stack(
        [jnp.where(y == 0, cot_own, cot_got), jnp.where(y == 0, cot_got, cot_own)]
    ).reshape(2, 2, piece, width)
    cot_near = pick(cot_two, member, 1).reshape(2 * piece, width)
    cot_far = pick(cot_two, 1 - member, 1).reshape(2 * piece, width)
    cot_pair = jnp.concatenate([cot_near, cot_far], axis=0)
    acts, grads_pre = [], []
    for up, down, shift in mlp:
        pre = jnp.dot(normed_two, up, preferred_element_type=f32) + shift
        value, rate = gelu_pair(pre)
        acts.append(value.astype(bf16))
        grad_act = jnp.dot(cot_pair, down, preferred_element_type=f32).astype(bf16)
        grads_pre.append((grad_act.astype(f32) * rate).astype(bf16))
    back = sum(
        jnp.einsum("tf,df->td", g, m[0], preferred_element_type=f32)
        for g, m in zip(grads_pre, mlp)
    )
    own_rows = 2 * piece
    grad_normed_two = back[:own_rows] + swap_z(back[own_rows:].astype(bf16), 1).astype(f32)
    cot_own_rows = cot_near.astype(f32)
    grad_hidden = cot_own_rows + norm_back(hat_two, scale_two, gains[1], grad_normed_two)
    grad_branch = grad_hidden.astype(bf16)
    grad_att = jnp.einsum("dh,td->ht", out_proj, grad_branch, preferred_element_type=f32).astype(
        bf16
    )
    grad_att = grad_att.reshape(tp, heads_width, 2, piece)
    grad_parts = [grad_att[0]] + [swap_z(grad_att[k], k) for k in range(1, tp)]
    grad_full = jnp.stack(arranged(grad_parts, z), axis=2).reshape(heads_width, length)

    down_sum = sum(
        jnp.einsum("tf,df->td", a, m[1], preferred_element_type=f32) for a, m in zip(acts, mlp)
    )
    second = down_sum[:own_rows] + swap_z(down_sum[own_rows:].astype(bf16), 1).astype(f32)
    result_rows = (hidden + second + branch_bias[1]).astype(bf16)

    def spread(rows):
        rows = rows.reshape(2, piece, width)
        mine = pick(rows, y, 0)
        other = swap_y(pick(rows, 1 - y, 0))
        both = jnp.stack([jnp.where(y == 0, mine, other), jnp.where(y == 0, other, mine)])
        far = swap_z(both, 2)
        near = swap_z(both, 1)
        cross = swap_z(far, 1)
        return jnp.concatenate(arranged([both, near, far, cross], z), axis=1)

    result = spread(result_rows)

    mlp_grads = []
    for a, g in zip(acts, grads_pre):
        grad_up = jnp.einsum("td,tf->df", normed_two, g, preferred_element_type=f32)
        grad_down = jnp.einsum("td,tf->df", cot_pair, a, preferred_element_type=f32)
        mlp_grads.append((scatter_rows(grad_up), scatter_rows(grad_down)))
    grad_up = sum_y(mlp_grads[0][0] + swap_z(mlp_grads[1][0].astype(bf16), 2).astype(f32))
    grad_down = sum_y(mlp_grads[0][1] + swap_z(mlp_grads[1][1].astype(bf16), 2).astype(f32)).T
    up_sums = [jnp.sum(g.astype(f32), axis=0) for g in grads_pre]
    up_bias_sum = up_sums[0] + swap_z(up_sums[1].reshape(1, -1), 2).reshape(-1)
    grad_out = scatter_rows(
        jnp.einsum("td,ht->dh", grad_branch, att_all, preferred_element_type=f32)
    )
    two = 2 * heads_width
    grad_out = grad_out[:, :two] + swap_z(grad_out[:, two:].astype(bf16), 2).astype(f32)
    grad_out = grad_out[:, :heads_width] + swap_z(
        grad_out[:, heads_width:].astype(bf16), 1
    ).astype(f32)
    grad_out = sum_y(grad_out).T

    grad_qkv_rows = pl.pallas_call(
        attention_backward,
        out_shape=jax.ShapeDtypeStruct((length, 3 * heads_width), bf16),
        scratch_shapes=[pltpu.VMEM((length, HD), f32), pltpu.VMEM((length, HD), f32)],
        name="attention_backward",
    )(seg, qkv, grad_full, logs)
    proj_rows = jnp.moveaxis(qkv_proj, 1, 0).reshape(width, 3 * heads_width)
    normed_grad = jnp.einsum("tc,dc->td", grad_qkv_rows, proj_rows, preferred_element_type=f32)
    normed_grad = normed_grad.reshape(2, tp, piece, width)
    grad_normed = pick(normed_grad, z, 1)
    for k in range(1, tp):
        grad_normed = grad_normed + swap_z(pick(normed_grad, z ^ k, 1).astype(bf16), k).astype(f32)
    grad_normed = grad_normed.reshape(own_rows, width)
    hat_one, scale_one = normalized(rows_own)
    token_rows = grad_hidden + norm_back(hat_one, scale_one, gains[0], grad_normed)
    grad_tokens = spread(token_rows.astype(bf16)).astype(f32)
    grad_qkv = sum_y(
        scatter_rows(jnp.einsum("td,tc->dc", normed, grad_qkv_rows, preferred_element_type=f32))
    )
    grad_qkv = jnp.moveaxis(grad_qkv.reshape(part, 3, heads_width), 1, 0)

    qkv_sums = jnp.sum(grad_qkv_rows.astype(f32), axis=0)
    qv_sums = jnp.concatenate([qkv_sums[:heads_width], qkv_sums[2 * heads_width :]])
    sums = jnp.stack(
        [
            jnp.sum(grad_normed * hat_one, axis=0),
            jnp.sum(grad_normed_two * hat_two, axis=0),
            jnp.sum(grad_normed, axis=0),
            jnp.sum(grad_normed_two, axis=0),
            jnp.sum(grad_branch.astype(f32), axis=0),
            jnp.sum(cot_own_rows, axis=0),
        ]
    )
    sums = sums + swap_z(sums, 1)
    sums = sums + swap_z(sums, 2)
    sums = jnp.concatenate(
        [sums, up_bias_sum.reshape(1, -1), jnp.pad(qv_sums, (0, width - 2 * heads_width))[None]]
    )
    if fsdp == 4:
        sums = sums + swap(sums, "fsdp", 1, fsdp)
        sums = sums + swap(sums, "fsdp", 2, fsdp)
    else:
        sums = lax.psum(sums, "fsdp")
    sums = sums + swap_y(sums)
    norm_sums = pick(sums[:6].reshape(6, fsdp, part), f, 1)
    grad_up_bias = pick(sums[6].reshape(bias_rows, fsdp, bias_cols), f, 1)
    grad_qv = pick(sums[7, : 2 * heads_width].reshape(2, head_count, fsdp, qv_cols), f, 2)
    return (
        result,
        grad_tokens,
        norm_sums[0:2],
        norm_sums[2:4],
        grad_qkv,
        grad_qv,
        grad_out,
        norm_sums[4:6],
        grad_up,
        grad_up_bias,
        grad_down,
    )


def solution(mesh):
    in_specs = (
        P("fsdp", "ctx", None),
        P("fsdp", "ctx"),
        P(None, "fsdp"),
        P(None, "fsdp"),
        P(None, "fsdp", "tp"),
        P(None, "tp", "fsdp"),
        P("tp", "fsdp"),
        P(None, "fsdp"),
        P("fsdp", "tp"),
        P("tp", "fsdp"),
        P("tp", "fsdp"),
        P("fsdp", "ctx", None),
    )
    out_specs = (
        P("fsdp", "ctx", None),
        P("fsdp", "ctx", None),
        P(None, "fsdp"),
        P(None, "fsdp"),
        P(None, "fsdp", "tp"),
        P(None, "tp", "fsdp"),
        P("tp", "fsdp"),
        P(None, "fsdp"),
        P("fsdp", "tp"),
        P("tp", "fsdp"),
        P("tp", "fsdp"),
    )
    local = functools.partial(
        block, fsdp=mesh.shape["fsdp"], ctx=mesh.shape["ctx"], tp=mesh.shape["tp"]
    )
    return jax.shard_map(local, mesh=mesh, in_specs=in_specs, out_specs=out_specs, check_vma=False)
```

```python
import functools
import math

import jax
import jax.numpy as jnp
from jax import lax
from jax.experimental import pallas as pl
from jax.experimental.pallas import tpu as pltpu
from jax.sharding import PartitionSpec as P

HD = 64
QB = 256
eps = 1e-05
masked_score = -1e30
score_scale = 0.125 * math.log2(math.e)
f32 = jnp.float32
bf16 = jnp.bfloat16


def swap(v, axis, bit, size):
    return lax.ppermute(v, axis, [(i, i ^ bit) for i in range(size)])


def dot(a, b):
    return lax.dot_general(a, b, (((1,), (0,)), ((), ())), preferred_element_type=f32)


def turned(v):
    return v.astype(f32).T.astype(v.dtype)


def starts_of(seg):
    start = jnp.zeros(seg.shape, jnp.int32)
    for number in range(3):
        count = jnp.sum((seg == number).astype(jnp.int32), axis=1, keepdims=True)
        start = start + jnp.where(seg > number, count, 0)
    return start


def allowed_block(start, first, width):
    place = lax.broadcasted_iota(jnp.int32, (width, QB), 0)
    allowed = place >= start[:, first : first + QB]
    query = lax.broadcasted_iota(jnp.int32, (width, QB), 1) + first
    return allowed & (place <= query)


def attention_forward(seg_ref, qkv_ref, out_ref, log_ref):
    start = starts_of(seg_ref[...])
    length = qkv_ref.shape[2]
    heads = qkv_ref.shape[1] // HD
    half = length // 2
    for head in range(heads):
        rows = slice(head * HD, (head + 1) * HD)
        keys = turned(qkv_ref[1, rows, :])
        for first in range(0, length, QB):
            width = first + QB
            cols = slice(first, first + QB)
            scores = dot(keys[:width], qkv_ref[0, rows, cols]) * score_scale
            scores = jnp.where(allowed_block(start, first, width), scores, masked_score)
            top = jnp.max(scores, axis=0, keepdims=True)
            weight = jnp.exp2(scores - top)
            total = jnp.sum(weight, axis=0, keepdims=True)
            mixed = dot(qkv_ref[2, rows, :width], weight.astype(bf16))
            low = first % half
            out_ref[first // half, rows, low : low + QB] = (mixed / total).astype(bf16)
            log_ref[head : head + 1, cols] = top + jnp.log2(total)


def attention_backward(at_ref, seg_ref, qkv_ref, g0, g1, g2, g3, log_ref, out_ref, key_sum, value_sum):
    start = starts_of(seg_ref[...])
    at = at_ref[0]
    length = qkv_ref.shape[2]
    width_heads = qkv_ref.shape[1]
    for head in range(width_heads // HD):
        rows = slice(head * HD, (head + 1) * HD)
        keys = turned(qkv_ref[1, rows, :])
        values = turned(qkv_ref[2, rows, :])
        queries = turned(qkv_ref[0, rows, :])
        key_sum[...] = jnp.zeros_like(key_sum)
        value_sum[...] = jnp.zeros_like(value_sum)
        for first in range(0, length, QB):
            width = first + QB
            cols = slice(first, first + QB)
            place = at ^ (first // QB)
            grad = g0[rows, :]
            for k, ref in ((1, g1), (2, g2), (3, g3)):
                grad = jnp.where(place == k, ref[rows, :], grad)
            scores = dot(keys[:width], qkv_ref[0, rows, cols]) * score_scale
            prob = jnp.exp2(scores - log_ref[head : head + 1, cols])
            prob = jnp.where(allowed_block(start, first, width), prob, 0.0)
            grad_prob = dot(values[:width], grad)
            inner = jnp.sum(prob * grad_prob, axis=0, keepdims=True)
            grad_scores = (prob * (grad_prob - inner) * 0.125).astype(bf16)
            grad_query = dot(qkv_ref[1, rows, :width], grad_scores)
            out_ref[cols, rows] = grad_query.T.astype(bf16)
            key_sum[:width] += dot(grad_scores, queries[cols])
            value_sum[:width] += dot(prob.astype(bf16), turned(grad))
        out_ref[:, width_heads + head * HD : width_heads + (head + 1) * HD] = key_sum[...].astype(bf16)
        out_ref[:, 2 * width_heads + head * HD : 2 * width_heads + (head + 1) * HD] = value_sum[
            ...
        ].astype(bf16)


def normalized(v):
    mean = jnp.mean(v, axis=-1, keepdims=True)
    centered = v - mean
    scale = lax.rsqrt(jnp.mean(centered * centered, axis=-1, keepdims=True) + eps)
    return centered * scale, scale


def norm_back(hat, scale, gain, grad):
    scaled = grad * gain
    first = jnp.mean(scaled, axis=-1, keepdims=True)
    second = jnp.mean(scaled * hat, axis=-1, keepdims=True)
    return scale * (scaled - first - hat * second)


def gelu_pair(u):
    slope = math.sqrt(2 / math.pi)
    bent = jnp.tanh(slope * (u + 0.044715 * u * u * u))
    value = 0.5 * u * (1 + bent)
    rate = 0.5 * (1 + bent) + 0.5 * u * (1 - bent * bent) * slope * (1 + 3 * 0.044715 * u * u)
    return value, rate


def arranged(parts, at):
    low, high = (at & 1) == 1, (at >> 1) == 1
    p0, p1, p2, p3 = parts
    a0, a1 = jnp.where(low, p1, p0), jnp.where(low, p0, p1)
    a2, a3 = jnp.where(low, p3, p2), jnp.where(low, p2, p3)
    return [
        jnp.where(high, a2, a0),
        jnp.where(high, a3, a1),
        jnp.where(high, a0, a2),
        jnp.where(high, a1, a3),
    ]


def pick(v, index, axis):
    return lax.dynamic_index_in_dim(v, index, axis, keepdims=False)


def block(
    tokens,
    segments,
    ln_gains,
    ln_biases,
    w_qkv,
    bias_qv,
    w_out,
    out_biases,
    w_up,
    up_bias,
    w_down,
    cotangent,
    *,
    fsdp,
    ctx,
    tp,
):
    seq_count, half, width = tokens.shape
    part = w_up.shape[0]
    heads_width = w_qkv.shape[2]
    head_count = heads_width // HD
    hidden_part = w_up.shape[1]
    length = 2 * half
    piece = half // 2
    assert ctx == 2 and seq_count == 2 and tp == 4
    f = lax.axis_index("fsdp")
    y = lax.axis_index("ctx")
    z = lax.axis_index("tp")
    seq = z >> 1
    member = z & 1
    same = seq == y
    at = 2 * y + member

    def swap_y(v):
        return swap(v, "ctx", 1, ctx)

    def swap_z(v, bit):
        return swap(v, "tp", bit, tp)

    def swap_yz(v, bit):
        pairs = [(a * tp + b, (1 - a) * tp + (b ^ bit)) for a in range(2) for b in range(tp)]
        return lax.ppermute(v, ("ctx", "tp"), pairs)

    def gather_rows(v):
        if fsdp != 4:
            return lax.all_gather(v, "fsdp", axis=0, tiled=True).reshape((fsdp,) + v.shape)
        far = swap(v, "fsdp", 2, fsdp)
        near = swap(v, "fsdp", 1, fsdp)
        cross = swap(far, "fsdp", 1, fsdp)
        return arranged([v, near, far, cross], f)

    def scatter_rows(gs):
        gs = [g.astype(bf16) for g in gs]
        if fsdp != 4:
            return jnp.stack(
                [lax.psum_scatter(g, "fsdp", scatter_dimension=0, tiled=True).astype(f32) for g in gs]
            )
        core, x = f & 1, f >> 1
        send, own = [], []
        for g in gs:
            g = g.reshape(2, 2, part, g.shape[1])
            kept = pick(g, core, 1)
            got = swap(pick(g, 1 - core, 1), "fsdp", 1, fsdp)
            send.append((pick(kept, 1 - x, 0).astype(f32) + pick(got, 1 - x, 0).astype(f32)).astype(bf16))
            own.append(pick(kept, x, 0).astype(f32) + pick(got, x, 0).astype(f32))
        return jnp.stack(own) + swap(jnp.stack(send), "fsdp", 2, fsdp).astype(f32)

    tok_own = pick(tokens, seq, 0)
    seg_own = pick(segments, seq, 0)
    seg_row = jnp.pad(seg_own.astype(bf16), (0, width - half)).reshape(1, width)
    tok_got = swap_y(jnp.concatenate([tok_own, seg_row], axis=0))
    small = jnp.concatenate(
        [
            ln_gains.reshape(-1),
            ln_biases.reshape(-1),
            out_biases.reshape(-1),
            up_bias.reshape(-1),
            bias_qv.reshape(-1),
        ]
    )
    small_rows = -(-small.shape[0] // heads_width)
    small = jnp.pad(small, (0, small_rows * heads_width - small.shape[0]))
    qkv_pack = jnp.concatenate(
        [w_qkv.reshape(3 * part, heads_width), small.reshape(small_rows, heads_width)], axis=0
    )
    qkv_far = swap_z(qkv_pack, 2)
    chosen = jnp.where(same, qkv_pack, qkv_far)
    spare = jnp.where(same, qkv_far[3 * part :], qkv_pack[3 * part :])
    packs = gather_rows(jnp.concatenate([chosen, spare], axis=0))
    mlp_pack = jnp.concatenate([w_up, w_down.T], axis=0)
    mlp_far = swap_z(lax.optimization_barrier((mlp_pack, qkv_far))[0], 2)
    out_turned = w_out.T
    out_two = jnp.concatenate([out_turned, swap_z(out_turned, 1)], axis=1)
    out_far = swap_z(out_two, 2)
    out_four = jnp.concatenate(
        [jnp.where(same, out_two, out_far), jnp.where(same, out_far, out_two)], axis=1
    )

    packs = [packs[i] for i in range(fsdp)]
    qkv_proj = jnp.concatenate(
        [p[: 3 * part].reshape(3, part, heads_width) for p in packs], axis=1
    )
    flat = jnp.stack([p[3 * part :].reshape(2, -1) for p in packs]).astype(f32)
    spare_flat = flat[:, 1]
    flat = flat[:, 0]
    norms = jnp.moveaxis(flat[:, : 6 * part].reshape(fsdp, 6, part), 0, 1).reshape(6, width)
    gains, shifts, branch_bias = norms[0:2], norms[2:4], norms[4:6]
    bias_rows, bias_cols = up_bias.shape

    def up_shift_of(v):
        v = v[:, 6 * part : 6 * part + bias_rows * bias_cols].reshape(fsdp, bias_rows, bias_cols)
        return jnp.moveaxis(v, 0, 1).reshape(-1)

    up_one, up_two = up_shift_of(flat), up_shift_of(spare_flat)
    up_shift = jnp.where(same, up_one, up_two)
    up_shift_far = jnp.where(same, up_two, up_one)
    base = 6 * part + bias_rows * bias_cols
    qv_cols = bias_qv.shape[2]
    qv_bias = jnp.moveaxis(
        flat[:, base : base + 2 * head_count * qv_cols].reshape(fsdp, 2, head_count, qv_cols), 0, 2
    ).reshape(2, heads_width)

    first_half = jnp.where(y == 0, tok_own, tok_got[:half])
    second_half = jnp.where(y == 0, tok_got[:half], tok_own)
    inputs = jnp.concatenate([first_half, second_half], axis=0).astype(f32)
    seg_here = seg_own.astype(f32)
    seg_got = tok_got[half, :half].astype(f32)
    seg = jnp.concatenate(
        [jnp.where(y == 0, seg_here, seg_got), jnp.where(y == 0, seg_got, seg_here)]
    ).reshape(1, length).astype(jnp.int32)
    hat, _ = normalized(inputs)
    normed = (hat * gains[0] + shifts[0]).astype(bf16)
    projected = jnp.einsum("cdh,td->cht", qkv_proj, normed, preferred_element_type=f32)
    shift_rows = jnp.stack([qv_bias[0], jnp.zeros_like(qv_bias[0]), qv_bias[1]])
    qkv = (projected + shift_rows[:, :, None]).astype(bf16)
    attended, logs = pl.pallas_call(
        attention_forward,
        out_shape=(
            jax.ShapeDtypeStruct((2, heads_width, half), bf16),
            jax.ShapeDtypeStruct((head_count, length), f32),
        ),
        name="attention_forward",
    )(seg, qkv)

    att_here, att_there = pick(attended, y, 0), pick(attended, 1 - y, 0)
    att_all = jnp.concatenate(
        [att_here, swap_z(att_here, 1), swap_y(att_there), swap_yz(att_there, 1)], axis=0
    )
    out_proj = jnp.concatenate([v for v in gather_rows(out_four)], axis=0)
    branch = jnp.einsum("ht,dh->td", att_all, out_proj, preferred_element_type=f32)
    hidden = tok_own.astype(f32) + branch + branch_bias[0]
    hat_two, scale_two = normalized(hidden)
    normed_two = (hat_two * gains[1] + shifts[1]).astype(bf16)

    mlp = []
    for pack, shift in ((mlp_pack, up_shift), (mlp_far, up_shift_far)):
        got = gather_rows(pack)
        up = jnp.concatenate([got[i][:part] for i in range(fsdp)], axis=0)
        down = jnp.concatenate([got[i][part:] for i in range(fsdp)], axis=0)
        mlp.append((up, down, shift))
    cot = pick(cotangent, seq, 0)
    acts, grads_pre = [], []
    for up, down, shift in mlp:
        pre = jnp.dot(normed_two, up, preferred_element_type=f32) + shift
        value, rate = gelu_pair(pre)
        acts.append(value.astype(bf16))
        grad_act = jnp.dot(cot, down, preferred_element_type=f32).astype(bf16)
        grads_pre.append((grad_act.astype(f32) * rate).astype(bf16))
    back = sum(
        jnp.einsum("tf,df->td", g, m[0], preferred_element_type=f32)
        for g, m in zip(grads_pre, mlp)
    )

    def mine(v):
        return pick(v.reshape((2, piece) + v.shape[1:]), member, 0)

    def other(v):
        return pick(v.reshape((2, piece) + v.shape[1:]), 1 - member, 0)

    grad_normed_two = mine(back) + swap_z(other(back).astype(bf16), 1).astype(f32)
    hat_two, scale_two, hidden = mine(hat_two), mine(scale_two), mine(hidden)
    cot_rows = mine(cot).astype(f32)
    grad_hidden = cot_rows + norm_back(hat_two, scale_two, gains[1], grad_normed_two)
    grad_branch = grad_hidden.astype(bf16)
    grad_att = jnp.einsum("dh,td->ht", out_proj, grad_branch, preferred_element_type=f32).astype(
        bf16
    ).reshape(4, heads_width, piece)
    grad_parts = [
        grad_att[0],
        swap_z(grad_att[1], 1),
        swap_y(grad_att[2]),
        swap_yz(grad_att[3], 1),
    ]

    vmem = pl.BlockSpec(memory_space=pltpu.VMEM)
    grad_qkv_rows = pl.pallas_call(
        attention_backward,
        out_shape=jax.ShapeDtypeStruct((length, 3 * heads_width), bf16),
        in_specs=[pl.BlockSpec(memory_space=pltpu.SMEM)] + [vmem] * 7,
        scratch_shapes=[pltpu.VMEM((length, HD), f32), pltpu.VMEM((length, HD), f32)],
        name="attention_backward",
    )(at.reshape(1), seg, qkv, *grad_parts, logs)
    proj_rows = jnp.moveaxis(qkv_proj, 1, 0).reshape(width, 3 * heads_width)
    pieces = grad_qkv_rows.reshape(4, piece, 3 * heads_width)

    def normed_grad(k):
        return jnp.einsum(
            "tc,dc->td", pick(pieces, at ^ k, 0), proj_rows, preferred_element_type=f32
        )

    first_got = swap_y(normed_grad(3).astype(bf16))
    second_got = swap_y(normed_grad(2).astype(bf16))
    near_got = swap_z((normed_grad(1) + first_got.astype(f32)).astype(bf16), 1)
    grad_normed = normed_grad(0) + second_got.astype(f32) + near_got.astype(f32)
    rows_own = mine(tok_own).astype(f32)
    hat_one, scale_one = normalized(rows_own)
    token_rows = grad_hidden + norm_back(hat_one, scale_one, gains[0], grad_normed)

    def spread(rows):
        far = swap_z(rows, 2)
        near = swap_z(rows, 1)
        cross = swap_z(far, 1)
        return jnp.concatenate(arranged([rows, near, far, cross], z), axis=0).reshape(
            seq_count, half, width
        )

    grad_tokens = spread(token_rows.astype(bf16)).astype(f32)

    down_sum = sum(
        jnp.einsum("tf,df->td", a, m[1], preferred_element_type=f32) for a, m in zip(acts, mlp)
    )
    second = mine(down_sum) + swap_z(other(down_sum).astype(bf16), 1).astype(f32)
    result = spread((hidden + second + branch_bias[1]).astype(bf16))

    mlp_grads = []
    for a, g in zip(acts, grads_pre):
        grad_up = jnp.einsum("td,tf->df", normed_two, g, preferred_element_type=f32)
        grad_down = jnp.einsum("td,tf->df", cot, a, preferred_element_type=f32)
        mlp_grads.append(scatter_rows([grad_up, grad_down]))
    near_grad, far_grad = [
        pick(v, y, 0) + swap_y(pick(v, 1 - y, 0).astype(bf16)).astype(f32) for v in mlp_grads
    ]
    half_grad = (near_grad + swap_z(far_grad.astype(bf16), 2).astype(f32)).astype(bf16)
    rest_grad = swap_y(half_grad)
    grad_up = jnp.where(y == 0, half_grad, rest_grad).astype(f32)
    grad_down = jnp.where(y == 0, rest_grad, half_grad).astype(f32).T
    up_sums = [jnp.sum(g.astype(f32), axis=0) for g in grads_pre]

    att_own = pick(att_all.reshape(4 * heads_width, 2, piece), member, 1)
    grad_out = scatter_rows(
        [jnp.einsum("td,ht->dh", grad_branch, att_own, preferred_element_type=f32)]
    )[0]
    two = 2 * heads_width
    here, there = grad_out[:, :two], grad_out[:, two:]
    grad_out = jnp.where(same, here, there) + swap_z(
        jnp.where(same, there, here).astype(bf16), 2
    ).astype(f32)
    grad_out = grad_out[:, :heads_width] + swap_z(
        grad_out[:, heads_width:].astype(bf16), 1
    ).astype(f32)
    grad_out = grad_out.astype(bf16)
    grad_out = (grad_out.astype(f32) + swap_y(grad_out).astype(f32)).T

    grad_qkv = scatter_rows(
        [jnp.einsum("td,tc->dc", normed, grad_qkv_rows, preferred_element_type=f32)]
    )[0].astype(bf16)
    grad_qkv = (grad_qkv.astype(f32) + swap_z(grad_qkv, 2).astype(f32)).astype(bf16)
    grad_qkv = jnp.where(same, grad_qkv, swap_y(grad_qkv)).astype(f32)
    grad_qkv = jnp.moveaxis(grad_qkv.reshape(part, 3, heads_width), 1, 0)

    qkv_sums = jnp.sum(grad_qkv_rows.astype(f32), axis=0)
    qv_sums = jnp.concatenate([qkv_sums[:heads_width], qkv_sums[2 * heads_width :]])
    slots = jnp.arange(tp)[:, None]
    sums = jnp.concatenate(
        [
            jnp.stack(
                [
                    jnp.sum(grad_normed * hat_one, axis=0),
                    jnp.sum(grad_normed_two * hat_two, axis=0),
                    jnp.sum(grad_normed, axis=0),
                    jnp.sum(grad_normed_two, axis=0),
                    jnp.sum(grad_branch.astype(f32), axis=0),
                    jnp.sum(cot_rows, axis=0),
                ]
            ),
            jnp.where(slots == z, up_sums[0], 0.0) + jnp.where(slots == (z ^ 2), up_sums[1], 0.0),
            jnp.pad(
                jnp.where(slots == at, qv_sums, 0.0), ((0, 0), (0, width - 2 * heads_width))
            ),
        ]
    )
    sums = sums + swap_z(sums, 1)
    sums = sums + swap_z(sums, 2)
    if fsdp == 4:
        sums = sums + swap(sums, "fsdp", 1, fsdp)
        sums = sums + swap(sums, "fsdp", 2, fsdp)
    else:
        sums = lax.psum(sums, "fsdp")
    sums = sums + swap_y(sums)
    norm_sums = pick(sums[:6].reshape(6, fsdp, part), f, 1)
    up_total = pick(sums[6 : 6 + tp], z, 0)
    grad_up_bias = pick(up_total.reshape(bias_rows, fsdp, bias_cols), f, 1)
    qv_total = pick(sums[6 + tp :, : 2 * heads_width], z, 0)
    grad_qv = pick(qv_total.reshape(2, head_count, fsdp, qv_cols), f, 2)
    return (
        result,
        grad_tokens,
        norm_sums[0:2],
        norm_sums[2:4],
        grad_qkv,
        grad_qv,
        grad_out,
        norm_sums[4:6],
        grad_up,
        grad_up_bias,
        grad_down,
    )


def solution(mesh):
    in_specs = (
        P("fsdp", "ctx", None),
        P("fsdp", "ctx"),
        P(None, "fsdp"),
        P(None, "fsdp"),
        P(None, "fsdp", "tp"),
        P(None, "tp", "fsdp"),
        P("tp", "fsdp"),
        P(None, "fsdp"),
        P("fsdp", "tp"),
        P("tp", "fsdp"),
        P("tp", "fsdp"),
        P("fsdp", "ctx", None),
    )
    out_specs = (
        P("fsdp", "ctx", None),
        P("fsdp", "ctx", None),
        P(None, "fsdp"),
        P(None, "fsdp"),
        P(None, "fsdp", "tp"),
        P(None, "tp", "fsdp"),
        P("tp", "fsdp"),
        P(None, "fsdp"),
        P("fsdp", "tp"),
        P("tp", "fsdp"),
        P("tp", "fsdp"),
    )
    local = functools.partial(
        block, fsdp=mesh.shape["fsdp"], ctx=mesh.shape["ctx"], tp=mesh.shape["tp"]
    )
    return jax.shard_map(local, mesh=mesh, in_specs=in_specs, out_specs=out_specs, check_vma=False)
```

```python
import functools
import math

import jax
import jax.numpy as jnp
from jax import lax
from jax.experimental import pallas as pl
from jax.experimental.pallas import tpu as pltpu
from jax.sharding import PartitionSpec as P

HD = 64
QB = 256
eps = 1e-05
masked_score = -1e30
score_scale = 0.125 * math.log2(math.e)
f32 = jnp.float32
bf16 = jnp.bfloat16


def swap(v, axis, bit, size):
    return lax.ppermute(v, axis, [(i, i ^ bit) for i in range(size)])


def dot(a, b):
    return lax.dot_general(a, b, (((1,), (0,)), ((), ())), preferred_element_type=f32)


def turned(v):
    return v.astype(f32).T.astype(v.dtype)


def starts_of(seg):
    start = jnp.zeros(seg.shape, jnp.int32)
    for number in range(3):
        count = jnp.sum((seg == number).astype(jnp.int32), axis=1, keepdims=True)
        start = start + jnp.where(seg > number, count, 0)
    return start


def allowed_block(start, first, width):
    place = lax.broadcasted_iota(jnp.int32, (width, QB), 0)
    allowed = place >= start[:, first : first + QB]
    query = lax.broadcasted_iota(jnp.int32, (width, QB), 1) + first
    return allowed & (place <= query)


def dot_t(a, b):
    return lax.dot_general(a, b, (((1,), (1,)), ((), ())), preferred_element_type=f32)


def normalized(v):
    mean = jnp.mean(v, axis=-1, keepdims=True)
    centered = v - mean
    scale = lax.rsqrt(jnp.mean(centered * centered, axis=-1, keepdims=True) + eps)
    return centered * scale, scale


def norm_back(hat, scale, gain, grad):
    scaled = grad * gain
    first = jnp.mean(scaled, axis=-1, keepdims=True)
    second = jnp.mean(scaled * hat, axis=-1, keepdims=True)
    return scale * (scaled - first - hat * second)


def gelu_pair(u):
    slope = math.sqrt(2 / math.pi)
    bent = jnp.tanh(slope * (u + 0.044715 * u * u * u))
    value = 0.5 * u * (1 + bent)
    rate = 0.5 * (1 + bent) + 0.5 * u * (1 - bent * bent) * slope * (1 + 3 * 0.044715 * u * u)
    return value, rate


def chosen_part(refs, number, index, f):
    if f is None:
        return refs[number][index]
    place = number ^ f
    value = refs[0][index]
    for k in range(1, len(refs)):
        value = jnp.where(place == k, refs[k][index], value)
    return value


def pack_small(w_ref, gains_ref, biases_ref, out_ref_in, up_ref, qv_ref, pack_ref, rows_ref):
    part = w_ref.shape[1]
    width = w_ref.shape[2]
    for c in range(3):
        pack_ref[:part, c * width : (c + 1) * width] = w_ref[c]
    rows_ref[...] = jnp.zeros_like(rows_ref)
    for k, ref in enumerate((gains_ref, biases_ref, out_ref_in)):
        rows_ref[0:2, k * width : k * width + part] = ref[...].astype(f32)
    up_rows, cols = up_ref.shape
    heads = qv_ref.shape[1]
    for lane in (0, HD):
        rows_ref[2 : 2 + up_rows, lane : lane + cols] = up_ref[...].astype(f32)
    for i in range(2):
        low = 2 + up_rows + i * heads
        rows_ref[low : low + heads, 0:cols] = qv_ref[i].astype(f32)
    pack_ref[part:, :] = rows_ref[...].astype(bf16)


def project(n, ordered, at_ref, own_ref, got_ref, seg_ref, *refs):
    packs = refs[:n]
    rows_ref, turned_ref, att_ref, log_ref, normed_ref, params_ref, w_ref, qv_row = refs[n:]
    y = at_ref[0]
    f = at_ref[1] if ordered else None
    half = own_ref.shape[0]
    length = 2 * half
    width = own_ref.shape[1]
    part = width // n
    columns = w_ref.shape[1]
    group = columns // 3
    heads = group // HD
    small_rows = packs[0].shape[0] - part
    cols = HD // n
    up_rows = width // HD
    params_ref[...] = jnp.zeros_like(params_ref)
    qv_row[...] = jnp.zeros_like(qv_row)
    for p in range(n):
        w_ref[p * part : (p + 1) * part, :] = chosen_part(packs, p, (slice(0, part), slice(None)), f)
        small = chosen_part(packs, p, (slice(part, part + small_rows), slice(None)), f).astype(f32)
        for k in range(3):
            params_ref[2 * k : 2 * k + 2, p * part : (p + 1) * part] = small[
                0:2, k * group : k * group + part
            ]
        for r in range(up_rows):
            low = r * HD + p * cols
            params_ref[6:7, low : low + cols] = small[2 + r : 3 + r, 0:cols]
            params_ref[7:8, low : low + cols] = small[2 + r : 3 + r, HD : HD + cols]
        for i in range(2):
            for h in range(heads):
                low = 2 * i * group + h * HD + p * cols
                r = 2 + up_rows + i * heads + h
                qv_row[0:1, low : low + cols] = small[r : r + 1, 0:cols]
    gain = params_ref[0:1, :]
    shift = params_ref[2:3, :]
    for ref, place in ((own_ref, y), (got_ref, 1 - y)):
        hat, _ = normalized(ref[0:half, :].astype(f32))
        normed_ref[pl.ds(pl.multiple_of(place * half, half), half), :] = (hat * gain + shift).astype(
            bf16
        )
    got_row = got_ref[half : half + 1, 0:half].astype(f32).astype(jnp.int32)
    own_row = seg_ref[...]
    first = y == 0
    seg = jnp.concatenate(
        [jnp.where(first, own_row, got_row), jnp.where(first, got_row, own_row)], axis=1
    )
    for low in range(0, length, QB):
        rows = slice(low, low + QB)
        block_rows = (dot(normed_ref[rows, :], w_ref[...]) + qv_row[...]).astype(bf16)
        rows_ref[rows, :] = block_rows
        turned_ref[:, rows] = turned(block_rows)
    start = starts_of(seg)
    for head in range(heads):
        rows = slice(head * HD, (head + 1) * HD)
        keys = rows_ref[:, group + head * HD : group + (head + 1) * HD]
        for low in range(0, length, QB):
            reach = low + QB
            at_cols = slice(low, reach)
            scores = dot(keys[:reach], turned_ref[rows, at_cols]) * score_scale
            scores = jnp.where(allowed_block(start, low, reach), scores, masked_score)
            top = jnp.max(scores, axis=0, keepdims=True)
            weight = jnp.exp2(scores - top)
            total = jnp.sum(weight, axis=0, keepdims=True)
            mixed = dot(
                turned_ref[2 * group + head * HD : 2 * group + (head + 1) * HD, :reach],
                weight.astype(bf16),
            )
            inside = low % half
            att_ref[low // half, rows, inside : inside + QB] = (mixed / total).astype(bf16)
            log_ref[head : head + 1, at_cols] = top + jnp.log2(total)
    log_ref[heads : heads + 1, :] = start.astype(f32)


def out_project(n, ordered, at_ref, att_ref, z_ref, y_ref, yz_ref, own_ref, params_ref, *refs):
    parts = refs[:n]
    hidden_ref, normed_ref, att_own_ref, out_ref, att_all = refs[n:]
    y, member = at_ref[0], at_ref[2]
    f = at_ref[1] if ordered else None
    group = z_ref.shape[0]
    half, width = own_ref.shape
    part = width // n
    att_all[0:group, :] = att_ref[y]
    for k, ref in enumerate((z_ref, y_ref, yz_ref)):
        att_all[(k + 1) * group : (k + 2) * group, :] = ref[...]
    for p in range(n):
        out_ref[p * part : (p + 1) * part, :] = chosen_part(parts, p, (slice(None), slice(None)), f)
    everything = att_all[...]
    att_own_ref[...] = jnp.where(member == 0, everything[:, : half // 2], everything[:, half // 2 :])
    for low in range(0, half, QB):
        rows = slice(low, low + QB)
        branch = dot_t(turned(everything[:, rows]), out_ref[...])
        hidden = own_ref[rows, :].astype(f32) + branch + params_ref[4:5, :]
        hidden_ref[rows, :] = hidden
        hat, _ = normalized(hidden)
        normed_ref[rows, :] = (hat * params_ref[1:2, :] + params_ref[3:4, :]).astype(bf16)


def feed_forward(n, ordered, last, at_ref, normed_ref, cot_ref, params_ref, *refs):
    ups, downs = refs[:n], refs[n : 2 * n]
    refs = refs[2 * n :]
    if last:
        back_in, down_in, act_ref, pre_ref, back_ref, down_ref, back_send, down_send, sum_ref = refs[:9]
    else:
        act_ref, pre_ref, back_ref, down_ref, sum_ref = refs[:5]
    up_all, down_all = refs[-2:]
    member, same = at_ref[2], at_ref[3]
    f = at_ref[1] if ordered else None
    half, width = normed_ref.shape
    part = width // n
    hidden = up_all.shape[1]
    everything = (slice(None), slice(None))
    for p in range(n):
        up_all[p * part : (p + 1) * part, :] = chosen_part(ups, p, everything, f)
        down_all[p * part : (p + 1) * part, :] = chosen_part(downs, p, everything, f)
    shift = jnp.where(same == (0 if last else 1), params_ref[6:7, :], params_ref[7:8, :])
    sum_ref[...] = jnp.zeros_like(sum_ref)
    for low in range(0, half, QB):
        rows = slice(low, low + QB)
        pre = dot(normed_ref[rows, :], up_all[...]) + shift
        value, rate = gelu_pair(pre)
        act = value.astype(bf16)
        act_ref[rows, :] = act
        down = dot_t(act, down_all[...])
        grad_act = dot(cot_ref[rows, :], down_all[...]).astype(bf16)
        grad = (grad_act.astype(f32) * rate).astype(bf16)
        pre_ref[rows, :] = grad
        sum_ref[0:1, :] += jnp.sum(grad.astype(f32), axis=0, keepdims=True)
        back = dot_t(grad, up_all[...])
        if last:
            back = back + back_in[rows, :]
            down = down + down_in[rows, :]
        back_ref[rows, :] = back
        down_ref[rows, :] = down
    if last:
        other = pl.ds(pl.multiple_of((1 - member) * (half // 2), half // 2), half // 2)
        back_send[...] = back_ref[other, :].astype(bf16)
        down_send[...] = down_ref[other, :].astype(bf16)


def branch_back(
    at_ref, back_ref, got_ref, hidden_ref, cot_ref, out_ref, params_ref,
    grad_ref, branch_ref, g0, g1, g2, g3, sum_ref,
):
    piece = got_ref.shape[0]
    group = g0.shape[0]
    here = pl.ds(pl.multiple_of(at_ref[2] * piece, piece), piece)
    grad_two = back_ref[here, :] + got_ref[...].astype(f32)
    hat, scale = normalized(hidden_ref[here, :])
    cot = cot_ref[here, :].astype(f32)
    grad = cot + norm_back(hat, scale, params_ref[1:2, :], grad_two)
    grad_ref[...] = grad
    low = grad.astype(bf16)
    branch_ref[...] = low
    for k, ref in enumerate((g0, g1, g2, g3)):
        ref[...] = turned(dot(low, out_ref[:, k * group : (k + 1) * group]).astype(bf16))
    sum_ref[...] = jnp.zeros_like(sum_ref)
    sum_ref[0:1, :] = jnp.sum(grad_two * hat, axis=0, keepdims=True)
    sum_ref[1:2, :] = jnp.sum(grad_two, axis=0, keepdims=True)
    sum_ref[2:3, :] = jnp.sum(low.astype(f32), axis=0, keepdims=True)
    sum_ref[3:4, :] = jnp.sum(cot, axis=0, keepdims=True)


def attention_backward(
    at_ref, rows_in, turned_ref, g0, g1, g2, g3, log_ref, w_ref,
    out_ref, n0, n1, n2, n3, sum_ref, key_sum, value_sum,
):
    at = at_ref[4]
    length = rows_in.shape[0]
    group = turned_ref.shape[0] // 3
    heads = group // HD
    piece = n0.shape[0]
    start = log_ref[heads : heads + 1, :].astype(jnp.int32)
    for head in range(heads):
        rows = slice(head * HD, (head + 1) * HD)
        key_cols = slice(group + head * HD, group + (head + 1) * HD)
        value_cols = slice(2 * group + head * HD, 2 * group + (head + 1) * HD)
        keys = rows_in[:, key_cols]
        values = rows_in[:, value_cols]
        key_sum[...] = jnp.zeros_like(key_sum)
        value_sum[...] = jnp.zeros_like(value_sum)
        for low in range(0, length, QB):
            reach = low + QB
            cols = slice(low, reach)
            place = at ^ (low // QB)
            grad = g0[rows, :]
            for k, ref in ((1, g1), (2, g2), (3, g3)):
                grad = jnp.where(place == k, ref[rows, :], grad)
            scores = dot(keys[:reach], turned_ref[rows, cols]) * score_scale
            prob = jnp.exp2(scores - log_ref[head : head + 1, cols])
            prob = jnp.where(allowed_block(start, low, reach), prob, 0.0)
            grad_prob = dot(values[:reach], grad)
            inner = jnp.sum(prob * grad_prob, axis=0, keepdims=True)
            grad_scores = (prob * (grad_prob - inner) * 0.125).astype(bf16)
            grad_query = dot(turned_ref[key_cols, :reach], grad_scores)
            out_ref[cols, rows] = grad_query.T.astype(bf16)
            key_sum[:reach] += dot(grad_scores, rows_in[cols, rows])
            value_sum[:reach] += dot(prob.astype(bf16), turned(grad))
        out_ref[:, key_cols] = key_sum[...].astype(bf16)
        out_ref[:, value_cols] = value_sum[...].astype(bf16)
    for k, ref in ((3, n3), (2, n2), (1, n1), (0, n0)):
        here = pl.ds(pl.multiple_of((at ^ k) * piece, piece), piece)
        ref[...] = dot_t(out_ref[here, :], w_ref[...]).astype(ref.dtype)
    sum_ref[...] = jnp.zeros_like(sum_ref)
    sum_ref[0:1, :] = jnp.sum(out_ref[...].astype(f32), axis=0, keepdims=True)


def token_back(at_ref, n0, second_ref, near_ref, own_ref, params_ref, grad_ref, out_ref, sum_ref):
    piece = n0.shape[0]
    here = pl.ds(pl.multiple_of(at_ref[2] * piece, piece), piece)
    grad_normed = n0[...] + second_ref[...].astype(f32) + near_ref[...].astype(f32)
    hat, scale = normalized(own_ref[here, :].astype(f32))
    rows = grad_ref[...] + norm_back(hat, scale, params_ref[0:1, :], grad_normed)
    out_ref[...] = rows.astype(bf16)
    sum_ref[...] = jnp.zeros_like(sum_ref)
    sum_ref[0:1, :] = jnp.sum(grad_normed * hat, axis=0, keepdims=True)
    sum_ref[1:2, :] = jnp.sum(grad_normed, axis=0, keepdims=True)


def arranged(parts, at):
    low, high = (at & 1) == 1, (at >> 1) == 1
    p0, p1, p2, p3 = parts
    a0, a1 = jnp.where(low, p1, p0), jnp.where(low, p0, p1)
    a2, a3 = jnp.where(low, p3, p2), jnp.where(low, p2, p3)
    return [
        jnp.where(high, a2, a0),
        jnp.where(high, a3, a1),
        jnp.where(high, a0, a2),
        jnp.where(high, a1, a3),
    ]


def pick(v, index, axis):
    return lax.dynamic_index_in_dim(v, index, axis, keepdims=False)


def struct(shape, dtype=bf16):
    return jax.ShapeDtypeStruct(shape, dtype)


def call(body, name, scalars, arrays, outs, scratch=()):
    vmem = pl.BlockSpec(memory_space=pltpu.VMEM)
    specs = [vmem] * len(arrays)
    if scalars is not None:
        specs = [pl.BlockSpec(memory_space=pltpu.SMEM)] + specs
        arrays = (scalars,) + tuple(arrays)
    return pl.pallas_call(
        body, out_shape=outs, in_specs=specs, scratch_shapes=list(scratch), name=name
    )(*arrays)


def block(
    tokens,
    segments,
    ln_gains,
    ln_biases,
    w_qkv,
    bias_qv,
    w_out,
    out_biases,
    w_up,
    up_bias,
    w_down,
    cotangent,
    *,
    fsdp,
    ctx,
    tp,
):
    seq_count, half, width = tokens.shape
    part = w_up.shape[0]
    group = w_qkv.shape[2]
    head_count = group // HD
    hidden_part = w_up.shape[1]
    length = 2 * half
    piece = half // 2
    bias_rows, bias_cols = up_bias.shape
    assert ctx == 2 and seq_count == 2 and tp == 4
    f = lax.axis_index("fsdp")
    y = lax.axis_index("ctx")
    z = lax.axis_index("tp")
    seq = z >> 1
    member = z & 1
    same = seq == y
    at = 2 * y + member
    ordered = fsdp == 4
    scalars = jnp.stack([y, f, member, same.astype(jnp.int32), at]).astype(jnp.int32)

    def after(v, *others):
        return lax.optimization_barrier((v,) + others)[0]

    def swap_y(v):
        return swap(v, "ctx", 1, ctx)

    def swap_z(v, bit):
        return swap(v, "tp", bit, tp)

    def swap_yz(v, bit):
        pairs = [(a * tp + b, (1 - a) * tp + (b ^ bit)) for a in range(2) for b in range(tp)]
        return lax.ppermute(v, ("ctx", "tp"), pairs)

    def gather_parts(v, far=None):
        if not ordered:
            got = lax.all_gather(v, "fsdp", axis=0, tiled=False)
            return [got[i] for i in range(fsdp)]
        if far is None:
            far = swap(v, "fsdp", 2, fsdp)
        near = swap(v, "fsdp", 1, fsdp)
        cross = swap(far, "fsdp", 1, fsdp)
        return [v, near, far, cross]

    def scatter_rows(gs):
        gs = [g.astype(bf16) for g in gs]
        if not ordered:
            return jnp.stack(
                [lax.psum_scatter(g, "fsdp", scatter_dimension=0, tiled=True).astype(f32) for g in gs]
            )
        core, x = f & 1, f >> 1
        send, own = [], []
        for g in gs:
            g = g.reshape(2, 2, part, g.shape[1])
            kept = pick(g, core, 1)
            got = swap(pick(g, 1 - core, 1), "fsdp", 1, fsdp)
            send.append((pick(kept, 1 - x, 0).astype(f32) + pick(got, 1 - x, 0).astype(f32)).astype(bf16))
            own.append(pick(kept, x, 0).astype(f32) + pick(got, x, 0).astype(f32))
        return jnp.stack(own) + swap(jnp.stack(send), "fsdp", 2, fsdp).astype(f32)

    small_rows = 24
    pack = call(
        pack_small,
        "pack_small",
        None,
        (w_qkv, ln_gains, ln_biases, out_biases, up_bias, bias_qv),
        struct((part + small_rows, 3 * group)),
        [pltpu.VMEM((small_rows, 3 * group), f32)],
    )
    pack_far = swap_z(pack, 2)
    tok_own = pick(tokens, seq, 0)
    seg_own = pick(segments, seq, 0)
    seg_row = jnp.pad(seg_own.astype(bf16), (0, width - half)).reshape(1, width)
    tok_got = swap_y(jnp.concatenate([tok_own, seg_row], axis=0))
    down_turned = w_down.T
    near_ups, near_downs = gather_parts(w_up), gather_parts(down_turned)
    place = lax.broadcasted_iota(jnp.int32, pack.shape, 0)
    lane = lax.broadcasted_iota(jnp.int32, pack.shape, 1)
    turned_choice = (place >= part + 2) & (lane >= HD) & (lane < 2 * HD)
    chosen = jnp.where(turned_choice ^ same, pack, pack_far)
    packs = gather_parts(chosen)
    up_far = swap_z(after(w_up, pack_far), 2)
    down_far = swap_z(after(down_turned, pack_far), 2)
    out_turned = w_out.T
    out_two = jnp.concatenate([out_turned, swap_z(out_turned, 1)], axis=1)
    out_far = swap_z(out_two, 2)
    out_four = jnp.concatenate(
        [jnp.where(same, out_two, out_far), jnp.where(same, out_far, out_two)], axis=1
    )
    out_parts = gather_parts(out_four)

    qkv_rows, qkv_turned, attended, logs, normed, params, proj_rows = call(
        functools.partial(project, fsdp, ordered),
        "project",
        scalars,
        (tok_own, tok_got, seg_own.reshape(1, half), *packs),
        (
            struct((length, 3 * group)),
            struct((3 * group, length)),
            struct((2, group, half)),
            struct((head_count + 1, length), f32),
            struct((length, width)),
            struct((8, width), f32),
            struct((width, 3 * group)),
        ),
        [pltpu.VMEM((1, 3 * group), f32)],
    )

    att_here, att_there = pick(attended, y, 0), pick(attended, 1 - y, 0)
    att_y, att_yz, att_z = swap_y(att_there), swap_yz(att_there, 1), swap_z(att_here, 1)
    hidden, normed_two, att_own, out_proj = call(
        functools.partial(out_project, fsdp, ordered),
        "out_project",
        scalars,
        (attended, att_z, att_y, att_yz, tok_own, params, *out_parts),
        (
            struct((half, width), f32),
            struct((half, width)),
            struct((4 * group, piece)),
            struct((width, 4 * group)),
        ),
        [pltpu.VMEM((4 * group, half), bf16)],
    )

    cot = pick(cotangent, seq, 0)
    far_ups, far_downs = gather_parts(up_far), gather_parts(down_far)
    square = pltpu.VMEM((width, hidden_part), bf16)
    rows_f, rows_b = struct((half, width), f32), struct((half, hidden_part))
    half_b, sum_f = struct((piece, width)), struct((8, hidden_part), f32)
    act_one, pre_one, back, down_sum, up_one = call(
        functools.partial(feed_forward, fsdp, ordered, False),
        "feed_forward_near",
        scalars,
        (normed_two, cot, params, *near_ups, *near_downs),
        (rows_b, rows_b, rows_f, rows_f, sum_f),
        [square, square],
    )
    act_two, pre_two, back, down_sum, back_send, down_send, up_two = call(
        functools.partial(feed_forward, fsdp, ordered, True),
        "feed_forward_far",
        scalars,
        (normed_two, cot, params, *far_ups, *far_downs, back, down_sum),
        (rows_b, rows_b, rows_f, rows_f, half_b, half_b, sum_f),
        [square, square],
    )
    back_got = swap_z(back_send, 1)
    grad_hidden, grad_branch, g0, g1, g2, g3, sums_two = call(
        branch_back,
        "branch_back",
        scalars,
        (back, back_got, hidden, cot, out_proj, params),
        (
            struct((piece, width), f32),
            struct((piece, width)),
            *[struct((group, piece))] * 4,
            struct((8, width), f32),
        ),
    )
    g_y, g_yz, g_z = swap_y(g2), swap_yz(g3, 1), swap_z(g1, 1)

    mlp_grads = []
    for a, g in ((act_one, pre_one), (act_two, pre_two)):
        grad_up = jnp.einsum("td,tf->df", normed_two, g, preferred_element_type=f32)
        grad_down = jnp.einsum("td,tf->df", cot, a, preferred_element_type=f32)
        mlp_grads.append(scatter_rows([grad_up, grad_down]))
    down_got = swap_z(down_send, 1)

    grad_rows, n0, n1, n2, n3, qkv_sums = call(
        attention_backward,
        "attention_backward",
        scalars,
        (qkv_rows, qkv_turned, g0, g_z, g_y, g_yz, logs, proj_rows),
        (
            struct((length, 3 * group)),
            struct((piece, width), f32),
            struct((piece, width), f32),
            struct((piece, width)),
            struct((piece, width)),
            struct((8, 3 * group), f32),
        ),
        [pltpu.VMEM((length, HD), f32), pltpu.VMEM((length, HD), f32)],
    )
    first_got = swap_y(n3)
    second_got = swap_y(n2)
    near_got = swap_z((n1 + first_got.astype(f32)).astype(bf16), 1)
    token_rows, sums_one = call(
        token_back,
        "token_back",
        scalars,
        (n0, second_got, near_got, tok_own, params, grad_hidden),
        (struct((piece, width)), struct((8, width), f32)),
    )

    def spread(rows):
        far = swap_z(rows, 2)
        near = swap_z(rows, 1)
        cross = swap_z(far, 1)
        return jnp.concatenate(arranged([rows, near, far, cross], z), axis=0).reshape(
            seq_count, half, width
        )

    grad_tokens = spread(token_rows).astype(f32)

    def mine(v):
        return pick(v.reshape((2, piece) + v.shape[1:]), member, 0)

    second = mine(down_sum) + down_got.astype(f32)
    result = spread((mine(hidden) + second + params[5:6]).astype(bf16))

    near_grad, far_grad = [
        pick(v, y, 0) + swap_y(pick(v, 1 - y, 0).astype(bf16)).astype(f32) for v in mlp_grads
    ]
    half_grad = (near_grad + swap_z(far_grad.astype(bf16), 2).astype(f32)).astype(bf16)
    rest_grad = swap_y(half_grad)
    grad_up = jnp.where(y == 0, half_grad, rest_grad).astype(f32)
    grad_down = jnp.where(y == 0, rest_grad, half_grad).astype(f32).T

    grad_out = scatter_rows(
        [jnp.einsum("td,ht->dh", grad_branch, att_own, preferred_element_type=f32)]
    )[0]
    two = 2 * group
    here, there = grad_out[:, :two], grad_out[:, two:]
    grad_out = jnp.where(same, here, there) + swap_z(
        jnp.where(same, there, here).astype(bf16), 2
    ).astype(f32)
    grad_out = grad_out[:, :group] + swap_z(grad_out[:, group:].astype(bf16), 1).astype(f32)
    grad_out = grad_out.astype(bf16)
    grad_out = (grad_out.astype(f32) + swap_y(grad_out).astype(f32)).T

    grad_qkv = scatter_rows(
        [jnp.einsum("td,tc->dc", normed, grad_rows, preferred_element_type=f32)]
    )[0].astype(bf16)
    grad_qkv = (grad_qkv.astype(f32) + swap_z(grad_qkv, 2).astype(f32)).astype(bf16)
    grad_qkv = jnp.where(same, grad_qkv, swap_y(grad_qkv)).astype(f32)
    grad_qkv = jnp.moveaxis(grad_qkv.reshape(part, 3, group), 1, 0)

    qv_sums = jnp.concatenate([qkv_sums[0:1, :group], qkv_sums[0:1, 2 * group :]], axis=1)
    slots = jnp.arange(tp)[:, None]
    sums = jnp.concatenate(
        [
            sums_one[0:1],
            sums_two[0:1],
            sums_one[1:2],
            sums_two[1:4],
            jnp.where(slots == z, up_one[0:1], 0.0) + jnp.where(slots == (z ^ 2), up_two[0:1], 0.0),
            jnp.pad(jnp.where(slots == at, qv_sums, 0.0), ((0, 0), (0, width - 2 * group))),
        ]
    )
    sums = sums + swap_z(sums, 1)
    sums = sums + swap_z(sums, 2)
    if ordered:
        sums = sums + swap(sums, "fsdp", 1, fsdp)
        sums = sums + swap(sums, "fsdp", 2, fsdp)
    else:
        sums = lax.psum(sums, "fsdp")
    sums = sums + swap_y(sums)
    norm_sums = pick(sums[:6].reshape(6, fsdp, part), f, 1)
    up_total = pick(sums[6 : 6 + tp], z, 0)
    grad_up_bias = pick(up_total.reshape(bias_rows, fsdp, bias_cols), f, 1)
    qv_total = pick(sums[6 + tp :, : 2 * group], z, 0)
    grad_qv = pick(qv_total.reshape(2, head_count, fsdp, bias_cols), f, 2)
    return (
        result,
        grad_tokens,
        norm_sums[0:2],
        norm_sums[2:4],
        grad_qkv,
        grad_qv,
        grad_out,
        norm_sums[4:6],
        grad_up,
        grad_up_bias,
        grad_down,
    )


def solution(mesh):
    in_specs = (
        P("fsdp", "ctx", None),
        P("fsdp", "ctx"),
        P(None, "fsdp"),
        P(None, "fsdp"),
        P(None, "fsdp", "tp"),
        P(None, "tp", "fsdp"),
        P("tp", "fsdp"),
        P(None, "fsdp"),
        P("fsdp", "tp"),
        P("tp", "fsdp"),
        P("tp", "fsdp"),
        P("fsdp", "ctx", None),
    )
    out_specs = (
        P("fsdp", "ctx", None),
        P("fsdp", "ctx", None),
        P(None, "fsdp"),
        P(None, "fsdp"),
        P(None, "fsdp", "tp"),
        P(None, "tp", "fsdp"),
        P("tp", "fsdp"),
        P(None, "fsdp"),
        P("fsdp", "tp"),
        P("tp", "fsdp"),
        P("tp", "fsdp"),
    )
    local = functools.partial(
        block, fsdp=mesh.shape["fsdp"], ctx=mesh.shape["ctx"], tp=mesh.shape["tp"]
    )
    return jax.shard_map(local, mesh=mesh, in_specs=in_specs, out_specs=out_specs, check_vma=False)
```

```python
import functools
import math

import jax
import jax.numpy as jnp
from jax import lax
from jax.experimental import pallas as pl
from jax.experimental.pallas import tpu as pltpu
from jax.sharding import PartitionSpec as P

HD = 64
QB = 256
eps = 1e-05
masked_score = -1e30
score_scale = 0.125 * math.log2(math.e)
f32 = jnp.float32
bf16 = jnp.bfloat16


def swap(v, axis, bit, size):
    return lax.ppermute(v, axis, [(i, i ^ bit) for i in range(size)])


def dot(a, b):
    return lax.dot_general(a, b, (((1,), (0,)), ((), ())), preferred_element_type=f32)


def turned(v):
    return v.astype(f32).T.astype(v.dtype)


def starts_of(seg):
    start = jnp.zeros(seg.shape, jnp.int32)
    for number in range(3):
        count = jnp.sum((seg == number).astype(jnp.int32), axis=1, keepdims=True)
        start = start + jnp.where(seg > number, count, 0)
    return start


def allowed_block(start, first, width):
    place = lax.broadcasted_iota(jnp.int32, (width, QB), 0)
    allowed = place >= start[:, first : first + QB]
    query = lax.broadcasted_iota(jnp.int32, (width, QB), 1) + first
    return allowed & (place <= query)


def dot_t(a, b):
    return lax.dot_general(a, b, (((1,), (1,)), ((), ())), preferred_element_type=f32)


def normalized(v):
    mean = jnp.mean(v, axis=-1, keepdims=True)
    centered = v - mean
    scale = lax.rsqrt(jnp.mean(centered * centered, axis=-1, keepdims=True) + eps)
    return centered * scale, scale


def norm_back(hat, scale, gain, grad):
    scaled = grad * gain
    first = jnp.mean(scaled, axis=-1, keepdims=True)
    second = jnp.mean(scaled * hat, axis=-1, keepdims=True)
    return scale * (scaled - first - hat * second)


def gelu_pair(u):
    slope = math.sqrt(2 / math.pi)
    bent = jnp.tanh(slope * (u + 0.044715 * u * u * u))
    value = 0.5 * u * (1 + bent)
    rate = 0.5 * (1 + bent) + 0.5 * u * (1 - bent * bent) * slope * (1 + 3 * 0.044715 * u * u)
    return value, rate


def chosen_part(refs, number, index, f):
    if f is None:
        return refs[number][index]
    place = number ^ f
    value = refs[0][index]
    for k in range(1, len(refs)):
        value = jnp.where(place == k, refs[k][index], value)
    return value


def pack_small(w_ref, gains_ref, biases_ref, out_ref_in, up_ref, qv_ref, pack_ref, rows_ref):
    part = w_ref.shape[1]
    width = w_ref.shape[2]
    for c in range(3):
        pack_ref[:part, c * width : (c + 1) * width] = w_ref[c]
    rows_ref[...] = jnp.zeros_like(rows_ref)
    for k, ref in enumerate((gains_ref, biases_ref, out_ref_in)):
        rows_ref[0:2, k * width : k * width + part] = ref[...].astype(f32)
    up_rows, cols = up_ref.shape
    heads = qv_ref.shape[0]
    for lane in (0, HD):
        rows_ref[2 : 2 + up_rows, lane : lane + cols] = up_ref[...].astype(f32)
    for i in range(2):
        low = 2 + up_rows + i * heads
        rows_ref[low : low + heads, 0:cols] = qv_ref[:, i, :].astype(f32)
    pack_ref[part:, :] = rows_ref[...].astype(bf16)


def project(n, ordered, at_ref, own_ref, low_ref, high_ref, seg_ref, *refs):
    packs = refs[:n]
    rows_ref, turned_ref, att_ref, log_ref, hat_turned, params_ref, w_ref, qv_row, normed_ref, hat_ref = refs[n:]
    y = at_ref[0]
    f = at_ref[1] if ordered else None
    half = own_ref.shape[0]
    length = 2 * half
    width = own_ref.shape[1]
    part = width // n
    columns = w_ref.shape[1]
    group = columns // 3
    heads = group // HD
    small_rows = packs[0].shape[0] - part
    cols = HD // n
    up_rows = width // HD
    params_ref[...] = jnp.zeros_like(params_ref)
    qv_row[...] = jnp.zeros_like(qv_row)
    for p in range(n):
        w_ref[p * part : (p + 1) * part, :] = chosen_part(packs, p, (slice(0, part), slice(None)), f)
        small = chosen_part(packs, p, (slice(part, part + small_rows), slice(None)), f).astype(f32)
        for k in range(3):
            params_ref[2 * k : 2 * k + 2, p * part : (p + 1) * part] = small[
                0:2, k * group : k * group + part
            ]
        for r in range(up_rows):
            low = r * HD + p * cols
            params_ref[6:7, low : low + cols] = small[2 + r : 3 + r, 0:cols]
            params_ref[7:8, low : low + cols] = small[2 + r : 3 + r, HD : HD + cols]
        for i in range(2):
            for h in range(heads):
                low = 2 * i * group + h * HD + p * cols
                r = 2 + up_rows + i * heads + h
                qv_row[0:1, low : low + cols] = small[r : r + 1, 0:cols]
    gain = params_ref[0:1, :]
    shift = params_ref[2:3, :]
    middle = half // 2
    for rows, place in (
        (own_ref[:middle, :], 2 * y),
        (own_ref[middle:, :], 2 * y + 1),
        (low_ref[:middle, :], 2 - 2 * y),
        (high_ref[...], 3 - 2 * y),
    ):
        hat, _ = normalized(rows.astype(f32))
        here = pl.ds(pl.multiple_of(place * middle, middle), middle)
        hat_ref[here, :] = hat.astype(bf16)
        normed_ref[here, :] = (hat * gain + shift).astype(bf16)
    got_row = low_ref[middle : middle + 1, 0:half].astype(f32).astype(jnp.int32)
    own_row = seg_ref[...]
    first = y == 0
    seg = jnp.concatenate(
        [jnp.where(first, own_row, got_row), jnp.where(first, got_row, own_row)], axis=1
    )
    for low in range(0, length, QB):
        rows = slice(low, low + QB)
        block_rows = (dot(normed_ref[rows, :], w_ref[...]) + qv_row[...]).astype(bf16)
        hat_turned[:, rows] = turned(hat_ref[rows, :])
        rows_ref[rows, :] = block_rows
        turned_ref[:, rows] = turned(block_rows)
    start = starts_of(seg)
    for head in range(heads):
        rows = slice(head * HD, (head + 1) * HD)
        keys = rows_ref[:, group + head * HD : group + (head + 1) * HD]
        for low in range(0, length, QB):
            reach = low + QB
            at_cols = slice(low, reach)
            scores = dot(keys[:reach], turned_ref[rows, at_cols]) * score_scale
            scores = jnp.where(allowed_block(start, low, reach), scores, masked_score)
            top = jnp.max(scores, axis=0, keepdims=True)
            weight = jnp.exp2(scores - top)
            total = jnp.sum(weight, axis=0, keepdims=True)
            mixed = dot(
                turned_ref[2 * group + head * HD : 2 * group + (head + 1) * HD, :reach],
                weight.astype(bf16),
            )
            inside = low % half
            att_ref[low // half, rows, inside : inside + QB] = (mixed / total).astype(bf16)
            log_ref[head : head + 1, at_cols] = top + jnp.log2(total)
    log_ref[heads : heads + 1, :] = start.astype(f32)


def out_project(n, ordered, at_ref, att_ref, z_ref, y_ref, yz_ref, own_ref, params_ref, *refs):
    parts = refs[:n]
    hidden_ref, normed_ref, att_own_ref, out_ref, att_all = refs[n:]
    y, member = at_ref[0], at_ref[2]
    f = at_ref[1] if ordered else None
    group = z_ref.shape[0]
    half, width = own_ref.shape
    part = width // n
    att_all[0:group, :] = att_ref[y]
    for k, ref in enumerate((z_ref, y_ref, yz_ref)):
        att_all[(k + 1) * group : (k + 2) * group, :] = ref[...]
    for p in range(n):
        out_ref[p * part : (p + 1) * part, :] = chosen_part(parts, p, (slice(None), slice(None)), f)
    everything = att_all[...]
    att_own_ref[...] = jnp.where(member == 0, everything[:, : half // 2], everything[:, half // 2 :])
    for low in range(0, half, QB):
        rows = slice(low, low + QB)
        branch = dot_t(turned(everything[:, rows]), out_ref[...])
        hidden = own_ref[rows, :].astype(f32) + branch + params_ref[4:5, :]
        hidden_ref[rows, :] = hidden
        hat, _ = normalized(hidden)
        normed_ref[rows, :] = (hat * params_ref[1:2, :] + params_ref[3:4, :]).astype(bf16)


def feed_near(n, ordered, at_ref, normed_ref, params_ref, *refs):
    parts = refs[:n]
    act_ref, rate_ref, up_all, down_all, down_ref = refs[n:]
    f = at_ref[1] if ordered else None
    half, width = normed_ref.shape
    arrange(parts, f, up_all, down_all)
    shift = jnp.where(at_ref[3] == 1, params_ref[6:7, :], params_ref[7:8, :])
    for low in range(0, half, QB):
        rows = slice(low, low + QB)
        value, rate = gelu_pair(dot(normed_ref[rows, :], up_all[...]) + shift)
        act = value.astype(bf16)
        act_ref[rows, :] = act
        rate_ref[rows, :] = rate
        down_ref[rows, :] = dot_t(act, down_all[...])


def arrange(parts, f, up_all, down_all):
    part = parts[0].shape[0] // 2
    for p in range(len(parts)):
        here = slice(p * part, (p + 1) * part)
        up_all[here, :] = chosen_part(parts, p, (slice(0, part), slice(None)), f)
        down_all[here, :] = chosen_part(parts, p, (slice(part, 2 * part), slice(None)), f)


def feed_far(n, ordered, at_ref, normed_ref, cot_ref, params_ref, rate_one, up_one, down_one, down_in, *refs):
    parts = refs[:n]
    act_two, pre_one, pre_two, back_ref, back_send, down_ref, down_send, sum_ref, up_two, down_two = refs[n:]
    f = at_ref[1] if ordered else None
    member = at_ref[2]
    piece = normed_ref.shape[0] // 2
    arrange(parts, f, up_two, down_two)
    shift = jnp.where(at_ref[3] == 0, params_ref[6:7, :], params_ref[7:8, :])
    sum_ref[...] = jnp.zeros_like(sum_ref)
    for owner, back_out, down_out in ((1 - member, back_send, down_send), (member, back_ref, down_ref)):
        rows = pl.ds(pl.multiple_of(owner * piece, piece), piece)
        value, rate = gelu_pair(dot(normed_ref[rows, :], up_two[...]) + shift)
        act = value.astype(bf16)
        act_two[rows, :] = act
        down_out[...] = (down_in[rows, :] + dot_t(act, down_two[...])).astype(down_out.dtype)
        cot = cot_ref[rows, :]
        back = jnp.zeros((piece, back_ref.shape[1]), f32)
        for k, (slope, up, down, pre) in enumerate(
            ((rate_one[rows, :], up_one, down_one, pre_one), (rate, up_two, down_two, pre_two))
        ):
            grad_act = dot(cot, down[...]).astype(bf16)
            grad = (grad_act.astype(f32) * slope).astype(bf16)
            pre[rows, :] = grad
            sum_ref[k : k + 1, :] += jnp.sum(grad.astype(f32), axis=0, keepdims=True)
            back = back + dot_t(grad, up[...])
        back_out[...] = back.astype(back_out.dtype)


def feed_grads(ordered, at_ref, normed_ref, cot_ref, act_one, pre_one, act_two, pre_two, *refs):
    outs, whole = refs[:-1], refs[-1]
    normed_turned = turned(normed_ref[...])
    cot_turned = turned(cot_ref[...])
    for k, (act, pre) in enumerate(((act_one, pre_one), (act_two, pre_two))):
        for side, (left, right) in enumerate(((normed_turned, pre), (cot_turned, act))):
            whole[...] = dot(left, right[...]).astype(bf16)
            cut_rows(ordered, at_ref[1], whole, [ref.at[2 * k + side] for ref in outs])


def cut_rows(ordered, f, whole, outs):
    if not ordered:
        outs[0][...] = whole[...]
        return
    part = whole.shape[0] // 4
    for ref, core in zip(outs, (f & 1, 1 - (f & 1))):
        for x in range(2):
            ref[x] = whole[pl.ds(pl.multiple_of((2 * x + core) * part, part), part), :]


def core_sum(at_ref, kept_ref, got_ref, own_ref, *sends):
    x = at_ref[1] >> 1
    count = kept_ref.shape[0]
    each = count // len(sends)
    for k in range(count):
        own_ref[k] = kept_ref[k, x].astype(f32) + got_ref[k, x].astype(f32)
        sends[k // each][k % each] = (
            kept_ref[k, 1 - x].astype(f32) + got_ref[k, 1 - x].astype(f32)
        ).astype(bf16)


def x_sum(k, at_ref, own_ref, got_ref, send_ref, kept_ref):
    y = at_ref[0]
    kept_ref[...] = own_ref[2 * k + y] + got_ref[y].astype(f32)
    send_ref[...] = (own_ref[2 * k + 1 - y] + got_ref[1 - y].astype(f32)).astype(bf16)


def branch_back(
    at_ref, back_ref, got_ref, hidden_ref, cot_ref, out_ref, params_ref,
    grad_ref, branch_ref, g0, g1, g2, g3, sum_ref,
):
    piece = got_ref.shape[0]
    group = g0.shape[0]
    here = pl.ds(pl.multiple_of(at_ref[2] * piece, piece), piece)
    grad_two = back_ref[...] + got_ref[...].astype(f32)
    hat, scale = normalized(hidden_ref[here, :])
    cot = cot_ref[here, :].astype(f32)
    grad = cot + norm_back(hat, scale, params_ref[1:2, :], grad_two)
    grad_ref[...] = grad
    low = grad.astype(bf16)
    branch_ref[...] = low
    for k, ref in enumerate((g0, g1, g2, g3)):
        ref[...] = turned(dot(low, out_ref[:, k * group : (k + 1) * group]).astype(bf16))
    sum_ref[...] = jnp.zeros_like(sum_ref)
    sum_ref[0:1, :] = jnp.sum(grad_two * hat, axis=0, keepdims=True)
    sum_ref[1:2, :] = jnp.sum(grad_two, axis=0, keepdims=True)
    sum_ref[2:3, :] = jnp.sum(low.astype(f32), axis=0, keepdims=True)
    sum_ref[3:4, :] = jnp.sum(cot, axis=0, keepdims=True)


def attention_backward(
    ordered, at_ref, rows_in, turned_ref, g0, g1, g2, g3, log_ref, w_ref,
    hat_turned, columns_ref, branch_ref, att_ref, two_ref, up_ref, n0, n1, n2, n3, sum_ref, *refs
):
    outs, (out_ref, whole, key_sum, value_sum) = refs[:-4], refs[-4:]
    at = at_ref[4]
    length = rows_in.shape[0]
    group = turned_ref.shape[0] // 3
    heads = group // HD
    piece = n0.shape[0]
    start = log_ref[heads : heads + 1, :].astype(jnp.int32)
    for head in range(heads):
        rows = slice(head * HD, (head + 1) * HD)
        key_cols = slice(group + head * HD, group + (head + 1) * HD)
        value_cols = slice(2 * group + head * HD, 2 * group + (head + 1) * HD)
        keys = rows_in[:, key_cols]
        values = rows_in[:, value_cols]
        key_sum[...] = jnp.zeros_like(key_sum)
        value_sum[...] = jnp.zeros_like(value_sum)
        for low in range(0, length, QB):
            reach = low + QB
            cols = slice(low, reach)
            place = at ^ (low // QB)
            grad = g0[rows, :]
            for k, ref in ((1, g1), (2, g2), (3, g3)):
                grad = jnp.where(place == k, ref[rows, :], grad)
            scores = dot(keys[:reach], turned_ref[rows, cols]) * score_scale
            prob = jnp.exp2(scores - log_ref[head : head + 1, cols])
            prob = jnp.where(allowed_block(start, low, reach), prob, 0.0)
            grad_prob = dot(values[:reach], grad)
            inner = jnp.sum(prob * grad_prob, axis=0, keepdims=True)
            grad_scores = (prob * (grad_prob - inner) * 0.125).astype(bf16)
            grad_query = dot(turned_ref[key_cols, :reach], grad_scores)
            out_ref[cols, rows] = grad_query.T.astype(bf16)
            key_sum[:reach] += dot(grad_scores, rows_in[cols, rows])
            value_sum[:reach] += dot(prob.astype(bf16), turned(grad))
        out_ref[:, key_cols] = key_sum[...].astype(bf16)
        out_ref[:, value_cols] = value_sum[...].astype(bf16)
    for k, ref in ((3, n3), (2, n2), (1, n1), (0, n0)):
        here = pl.ds(pl.multiple_of((at ^ k) * piece, piece), piece)
        ref[...] = dot_t(out_ref[here, :], w_ref[...]).astype(ref.dtype)
    gain, shift = columns_ref[:, 0:1], columns_ref[:, 2:3]
    rows = out_ref[...]
    row_sum = jnp.sum(rows.astype(f32), axis=0, keepdims=True)
    base = dot(hat_turned[...], rows)
    whole[:, 2 * group : 5 * group] = (gain * base + shift * row_sum).astype(bf16)
    out_grad = dot_t(turned(branch_ref[...]), att_ref[...]).astype(bf16)
    for place, k in ((0, 1), (1, 3), (5, 0), (6, 2)):
        whole[:, place * group : (place + 1) * group] = out_grad[:, k * group : (k + 1) * group]
    cut_rows(ordered, at_ref[1], whole, [ref.at[0] for ref in outs])
    weights = w_ref[...]
    products = (weights.astype(f32) * base).astype(bf16)
    first = dot_t(jnp.ones((8, 3 * group), bf16), products)[0:1]
    high = jnp.broadcast_to(row_sum, (8, 3 * group)).astype(bf16)
    low = (jnp.broadcast_to(row_sum, (8, 3 * group)) - high.astype(f32)).astype(bf16)
    second = (dot_t(high, weights) + dot_t(low, weights))[0:1]
    sum_ref[...] = jnp.zeros_like(sum_ref)
    sum_ref[0:1, :] = first
    sum_ref[1:2, :] = two_ref[0:1, :]
    sum_ref[2:3, :] = second
    sum_ref[3:6, :] = two_ref[1:4, :]
    z = at_ref[5]
    query = row_sum[:, :group]
    value = row_sum[:, 2 * group :]
    for k in range(4):
        row = slice(6 + k, 7 + k)
        sum_ref[row, :] = jnp.where(z == k, up_ref[0:1, :], jnp.where((z ^ 2) == k, up_ref[1:2, :], 0.0))
        row = slice(10 + k, 11 + k)
        sum_ref[row, :group] = jnp.where(at_ref[4] == k, query, 0.0)
        sum_ref[row, group : 2 * group] = jnp.where(at_ref[4] == k, value, 0.0)


def token_back(at_ref, n0, second_ref, near_ref, own_ref, params_ref, grad_ref, out_ref):
    piece = n0.shape[0]
    here = pl.ds(pl.multiple_of(at_ref[2] * piece, piece), piece)
    grad_normed = n0[...].astype(f32) + second_ref[...].astype(f32) + near_ref[...].astype(f32)
    hat, scale = normalized(own_ref[here, :].astype(f32))
    rows = grad_ref[...] + norm_back(hat, scale, params_ref[0:1, :], grad_normed)
    out_ref[...] = rows.astype(bf16)


def place_rows(at_ref, p0, p1, p2, p3, out_ref):
    for k, ref in enumerate((p0, p1, p2, p3)):
        out_ref[at_ref[0] ^ k] = ref[...].astype(out_ref.dtype)


def pick(v, index, axis):
    return lax.dynamic_index_in_dim(v, index, axis, keepdims=False)


def struct(shape, dtype=bf16):
    return jax.ShapeDtypeStruct(shape, dtype)


def call(body, name, scalars, arrays, outs, scratch=(), us=1):
    vmem = pl.BlockSpec(memory_space=pltpu.VMEM)
    specs = [vmem] * len(arrays)
    if scalars is not None:
        specs = [pl.BlockSpec(memory_space=pltpu.SMEM)] + specs
        arrays = (scalars,) + tuple(arrays)
    return pl.pallas_call(
        body, out_shape=outs, in_specs=specs, scratch_shapes=list(scratch), name=name,
        cost_estimate=pl.CostEstimate(flops=0, transcendentals=0, bytes_accessed=us * 3000000),
    )(*arrays)


def block(
    tokens,
    segments,
    ln_gains,
    ln_biases,
    w_qkv,
    bias_qv,
    w_out,
    out_biases,
    w_up,
    up_bias,
    w_down,
    cotangent,
    *,
    fsdp,
    ctx,
    tp,
):
    seq_count, half, width = tokens.shape
    part = w_up.shape[0]
    group = w_qkv.shape[2]
    head_count = group // HD
    hidden_part = w_up.shape[1]
    length = 2 * half
    piece = half // 2
    bias_rows, bias_cols = up_bias.shape
    assert ctx == 2 and seq_count == 2 and tp == 4
    f = lax.axis_index("fsdp")
    y = lax.axis_index("ctx")
    z = lax.axis_index("tp")
    seq = z >> 1
    member = z & 1
    same = seq == y
    at = 2 * y + member
    ordered = fsdp == 4
    scalars = jnp.stack([y, f, member, same.astype(jnp.int32), at, z]).astype(jnp.int32)

    def after(v, *others):
        return lax.optimization_barrier((v,) + others)[0]

    def swap_y(v):
        return swap(v, "ctx", 1, ctx)

    def swap_z(v, bit):
        return swap(v, "tp", bit, tp)

    def swap_yz(v, bit):
        pairs = [(a * tp + b, (1 - a) * tp + (b ^ bit)) for a in range(2) for b in range(tp)]
        return lax.ppermute(v, ("ctx", "tp"), pairs)

    def gather_parts(v, far=None):
        if not ordered:
            got = lax.all_gather(v, "fsdp", axis=0, tiled=False)
            return [got[i] for i in range(fsdp)]
        if far is None:
            far = swap(v, "fsdp", 2, fsdp)
        near = swap(v, "fsdp", 1, fsdp)
        cross = swap(far, "fsdp", 1, fsdp)
        return [v, near, far, cross]

    small_rows = 24
    pack = call(
        pack_small,
        "pack_small",
        None,
        (w_qkv, ln_gains, ln_biases, out_biases, up_bias, jnp.swapaxes(bias_qv, 0, 1)),
        struct((part + small_rows, 3 * group)),
        [pltpu.VMEM((small_rows, 3 * group), f32)],
    )
    pack_far = swap_z(pack, 2)
    out_turned = w_out.T
    out_near = swap_z(after(out_turned, pack), 1)
    tok_own = pick(after(tokens, out_near), seq, 0)
    seg_own = pick(after(segments, out_near), seq, 0)
    seg_row = jnp.pad(seg_own.astype(bf16), (0, width - half)).reshape(1, width)
    tok_low = swap_y(jnp.concatenate([tok_own[:piece], seg_row], axis=0))
    tok_high = swap_y(after(tok_own[piece:], tok_low))
    mlp_pack = jnp.concatenate([after(w_up, pack), w_down.T], axis=0)
    place = lax.broadcasted_iota(jnp.int32, pack.shape, 0)
    lane = lax.broadcasted_iota(jnp.int32, pack.shape, 1)
    turned_choice = (place >= part + 2) & (lane >= HD) & (lane < 2 * HD)
    chosen = jnp.where(turned_choice ^ same, pack, pack_far)
    packs = gather_parts(chosen)
    out_two = jnp.concatenate([out_turned, out_near], axis=1)
    out_far = swap_z(after(out_two, pack_far), 2)
    mlp_far = swap_z(after(mlp_pack, out_far, tok_low), 2)
    near_x = swap(after(mlp_pack, packs[2], out_far), "fsdp", 2, fsdp) if ordered else mlp_pack

    qkv_rows, qkv_turned, attended, logs, hat_turned, params, proj_rows = call(
        functools.partial(project, fsdp, ordered),
        "project",
        scalars,
        (tok_own, tok_low, tok_high, seg_own.reshape(1, half), *packs),
        (
            struct((length, 3 * group)),
            struct((3 * group, length)),
            struct((2, group, half)),
            struct((head_count + 1, length), f32),
            struct((width, length)),
            struct((8, width), f32),
            struct((width, 3 * group)),
        ),
        [pltpu.VMEM((1, 3 * group), f32)] + [pltpu.VMEM((length, width), bf16)] * 2,
        12,
    )

    att_here, att_there = pick(attended, y, 0), pick(attended, 1 - y, 0)
    attended, out_two, out_far = lax.optimization_barrier((attended, out_two, out_far, near_x))[:3]
    out_four = jnp.concatenate(
        [jnp.where(same, out_two, out_far), jnp.where(same, out_far, out_two)], axis=1
    )
    out_x = swap(out_four, "fsdp", 2, fsdp) if ordered else None
    att_y, att_yz, att_z = swap_y(att_there), swap_yz(att_there, 1), swap_z(att_here, 1)
    if ordered:
        out_four, out_x, near_own, near_x = lax.optimization_barrier(
            (out_four, out_x, mlp_pack, near_x, att_z, att_y, att_yz)
        )[:4]
    else:
        near_own = mlp_pack
    out_parts = gather_parts(out_four, out_x)
    near_parts = gather_parts(near_own, near_x)
    hidden, normed_two, att_own, out_proj = call(
        functools.partial(out_project, fsdp, ordered),
        "out_project",
        scalars,
        (attended, att_z, att_y, att_yz, tok_own, params, *out_parts),
        (
            struct((half, width), f32),
            struct((half, width)),
            struct((4 * group, piece)),
            struct((width, 4 * group)),
        ),
        [pltpu.VMEM((4 * group, half), bf16)],
        4,
    )

    cot = pick(cotangent, seq, 0)
    rows_f, rows_b = struct((half, width), f32), struct((half, hidden_part))
    rate_f, square = struct((half, hidden_part), f32), struct((width, hidden_part))
    half_b = struct((piece, width))
    act_one, rate_one, up_one, down_one, down_sum = call(
        functools.partial(feed_near, fsdp, ordered),
        "feed_near",
        scalars,
        (normed_two, params, *near_parts),
        (rows_b, rate_f, square, square, rows_f),
        us=4,
    )
    if ordered:
        far_x = swap(after(mlp_far, att_z, att_y, att_yz), "fsdp", 2, fsdp)
        far_own, far_x = lax.optimization_barrier((mlp_far, far_x, act_one))[:2]
        far_parts = gather_parts(far_own, far_x)
    else:
        far_parts = gather_parts(mlp_far)
    piece_f, sum_f = struct((piece, width), f32), struct((8, hidden_part), f32)
    act_two, pre_one, pre_two, back, back_send, down_own, down_send, up_sums = call(
        functools.partial(feed_far, fsdp, ordered),
        "feed_far",
        scalars,
        (normed_two, cot, params, rate_one, up_one, down_one, down_sum, *far_parts),
        (rows_b, rows_b, rows_b, piece_f, half_b, piece_f, half_b, sum_f),
        [pltpu.VMEM((width, hidden_part), bf16)] * 2,
        us=9,
    )
    back_got = swap_z(back_send, 1)
    cut = (2, part) if ordered else (width,)
    grad_outs = [struct((4,) + cut + (hidden_part,))] * (2 if ordered else 1)
    mlp_grads = call(
        functools.partial(feed_grads, ordered),
        "feed_grads",
        scalars,
        (normed_two, cot, act_one, pre_one, act_two, pre_two),
        tuple(grad_outs),
        [pltpu.VMEM((width, hidden_part), bf16)],
        us=8,
    )

    def scatter(parts, name, count, gate, later):
        if not ordered:
            v = lax.psum_scatter(parts[0], "fsdp", scatter_dimension=1, tiled=True)
            each = v.shape[0] // count
            zeros = [jnp.zeros_like(v[:each])] * count
            return v.astype(f32), zeros, zeros[-1:]
        kept, sent = parts
        got = swap(after(sent, *gate), "fsdp", 1, fsdp)
        shape = kept.shape[:1] + kept.shape[2:]
        each = (shape[0] // count,) + shape[1:]
        kept, *sent = call(
            core_sum, name, scalars, (after(kept, later), got), (struct(shape, f32), *[struct(each)] * count), us=2
        )
        return kept, sent, [swap_x(v) for v in sent[-1:]]

    def swap_x(v, *gate):
        return swap(after(v, *gate), "fsdp", 2, fsdp) if ordered else v

    def mine(v):
        return pick(v.reshape((2, piece) + v.shape[1:]), member, 0)

    def spread(rows, name, dtype, gate=()):
        far = swap_z(rows, 2)
        near = swap_z(rows, 1)
        cross = swap_z(after(far, near, *gate), 1)
        placed = call(
            place_rows, name, z.reshape(1), (rows, near, far, cross), struct((tp, piece, width), dtype)
        )
        return placed.reshape(seq_count, half, width), (near, far), cross

    grad_hidden, grad_branch, g0, g1, g2, g3, sums_two = call(
        branch_back,
        "branch_back",
        scalars,
        (back, back_got, hidden, cot, out_proj, params),
        (
            struct((piece, width), f32),
            struct((piece, width)),
            *[struct((group, piece))] * 4,
            struct((8, width), f32),
        ),
    )
    down_got = swap_z(after(down_send, g0), 1)
    g_y, g_yz, g_z = swap_y(g2), swap_yz(g3, 1), swap_z(g1, 1)
    grads_kept, grads_sent, (far_x,) = scatter(mlp_grads, "core_sum_feed", 2, (g0,), g_y)
    result_rows = (mine(hidden) + down_own + down_got.astype(f32) + params[5:6]).astype(bf16)
    result_rows = after(result_rows, g_y, g_yz, g_z)
    result, result_gate, result_cross = spread(result_rows, "place_result", bf16)
    late_outs = [struct((1,) + cut + (7 * group,))] * (2 if ordered else 1)
    n0, n1, n2, n3, sums, *late = call(
        functools.partial(attention_backward, ordered),
        "attention_backward",
        scalars,
        (
            qkv_rows, qkv_turned, after(g0, result_rows, *grads_sent), g_z, g_y, g_yz, logs, proj_rows,
            hat_turned, params.T, grad_branch, att_own, sums_two, up_sums,
        ),
        (*[struct((piece, width))] * 4, struct((16, width), f32), *late_outs),
        [
            pltpu.VMEM((length, 3 * group), bf16),
            pltpu.VMEM((width, 7 * group), bf16),
            pltpu.VMEM((length, HD), f32),
            pltpu.VMEM((length, HD), f32),
        ],
        us=16,
    )
    first_got = swap_y(after(n3, *result_gate, far_x))
    late_kept, late_sent, _ = scatter(
        late, "core_sum_late", 1, (*result_gate, far_x), first_got
    )
    late_first = late_sent[0]
    halves = (struct((part, hidden_part)), struct((part, hidden_part), f32))
    far_sent, far_kept = call(
        functools.partial(x_sum, 1),
        "x_sum_far",
        scalars,
        (after(grads_kept, first_got), far_x),
        halves,
    )
    share = n1.astype(f32) + first_got.astype(f32)
    near_got = swap_z(share.astype(bf16), 1)
    second_got = swap_y(after(n2, first_got))
    token_rows = call(
        token_back,
        "token_back",
        scalars,
        (after(n0, late_first, far_sent), second_got, near_got, tok_own, params, grad_hidden),
        struct((piece, width)),
        us=3,
    )
    far_got = swap_y(after(far_sent, second_got))
    late_got = swap_x(late_sent[0], first_got)
    near_x_got = swap_x(grads_sent[0], second_got)
    grad_tokens, token_gate, token_cross = spread(
        token_rows, "place_tokens", f32, (result_cross, late_got)
    )
    far_far = swap_z(after((far_kept + far_got.astype(f32)).astype(bf16), *token_gate), 2)
    sums = after(sums, *token_gate, far_got, near_x_got)
    sums = sums + swap_y(sums)
    if ordered:
        sums = sums + swap(sums, "fsdp", 1, fsdp)
        sums = sums + swap(sums, "fsdp", 2, fsdp)
    else:
        sums = lax.psum(sums, "fsdp")
    sums = sums + swap_z(sums, 1)
    sums = sums + swap_z(sums, 2)
    near_sent, near_kept = call(
        functools.partial(x_sum, 0),
        "x_sum_near",
        scalars,
        (after(grads_kept, *token_gate), near_x_got),
        halves,
    )
    half_got = swap_y(after(near_sent, near_got))
    half_grad = (near_kept + half_got.astype(f32) + far_far.astype(f32)).astype(bf16)
    rest_grad = swap_y(half_grad)
    grad_up = jnp.where(y == 0, half_grad, rest_grad).astype(f32)
    grad_down = jnp.where(y == 0, rest_grad, half_grad).astype(f32).T

    late = late_kept[0] + late_got[0].astype(f32)
    out_got = swap_z(after(late[:, : 2 * group].astype(bf16), token_cross), 1).astype(f32)
    grad_qkv = late[:, 2 * group : 5 * group].astype(bf16)
    out_first = late[:, 5 * group : 6 * group] + out_got[:, :group]
    out_second = late[:, 6 * group :] + out_got[:, group:]
    out_here = jnp.where(same, out_first, out_second).astype(bf16)
    out_there = jnp.where(same, out_second, out_first).astype(bf16)
    kept = jnp.concatenate([grad_qkv, out_here], axis=1).astype(f32)
    both = (
        kept + swap_z(jnp.concatenate([grad_qkv, out_there], axis=1), 2).astype(f32)
    ).astype(bf16)
    both_got = swap_y(both)
    grad_qkv = jnp.where(same, both, both_got)[:, : 3 * group].astype(f32)
    grad_qkv = jnp.moveaxis(grad_qkv.reshape(part, 3, group), 1, 0)
    grad_out = (both[:, 3 * group :].astype(f32) + both_got[:, 3 * group :].astype(f32)).T

    norm_sums = pick(sums[:6].reshape(6, fsdp, part), f, 1)
    up_total = pick(sums[6 : 6 + tp], z, 0)
    grad_up_bias = pick(up_total.reshape(bias_rows, fsdp, bias_cols), f, 1)
    qv_total = pick(sums[6 + tp : 6 + 2 * tp, : 2 * group], z, 0)
    grad_qv = pick(qv_total.reshape(2, head_count, fsdp, bias_cols), f, 2)
    return (
        result,
        grad_tokens,
        norm_sums[0:2],
        norm_sums[2:4],
        grad_qkv,
        grad_qv,
        grad_out,
        norm_sums[4:6],
        grad_up,
        grad_up_bias,
        grad_down,
    )


def solution(mesh):
    in_specs = (
        P("fsdp", "ctx", None),
        P("fsdp", "ctx"),
        P(None, "fsdp"),
        P(None, "fsdp"),
        P(None, "fsdp", "tp"),
        P(None, "tp", "fsdp"),
        P("tp", "fsdp"),
        P(None, "fsdp"),
        P("fsdp", "tp"),
        P("tp", "fsdp"),
        P("tp", "fsdp"),
        P("fsdp", "ctx", None),
    )
    out_specs = (
        P("fsdp", "ctx", None),
        P("fsdp", "ctx", None),
        P(None, "fsdp"),
        P(None, "fsdp"),
        P(None, "fsdp", "tp"),
        P(None, "tp", "fsdp"),
        P("tp", "fsdp"),
        P(None, "fsdp"),
        P("fsdp", "tp"),
        P("tp", "fsdp"),
        P("tp", "fsdp"),
    )
    local = functools.partial(
        block, fsdp=mesh.shape["fsdp"], ctx=mesh.shape["ctx"], tp=mesh.shape["tp"]
    )
    return jax.shard_map(local, mesh=mesh, in_specs=in_specs, out_specs=out_specs, check_vma=False)
```

```python
import functools
import math

import jax
import jax.numpy as jnp
from jax import lax
from jax.experimental import pallas as pl
from jax.experimental.pallas import tpu as pltpu
from jax.sharding import PartitionSpec as P

HD = 64
QB = 256
eps = 1e-05
masked_score = -1e30
score_scale = 0.125 * math.log2(math.e)
f32 = jnp.float32
bf16 = jnp.bfloat16


def swap(v, axis, bit, size):
    return lax.ppermute(v, axis, [(i, i ^ bit) for i in range(size)])


def dot(a, b):
    return lax.dot_general(a, b, (((1,), (0,)), ((), ())), preferred_element_type=f32)


def turned(v):
    return v.astype(f32).T.astype(v.dtype)


def starts_of(seg):
    start = jnp.zeros(seg.shape, jnp.int32)
    for number in range(3):
        count = jnp.sum((seg == number).astype(jnp.int32), axis=1, keepdims=True)
        start = start + jnp.where(seg > number, count, 0)
    return start


def allowed_block(start, first, width):
    place = lax.broadcasted_iota(jnp.int32, (width, QB), 0)
    allowed = place >= start[:, first : first + QB]
    query = lax.broadcasted_iota(jnp.int32, (width, QB), 1) + first
    return allowed & (place <= query)


def dot_t(a, b):
    return lax.dot_general(a, b, (((1,), (1,)), ((), ())), preferred_element_type=f32)


def normalized(v):
    mean = jnp.mean(v, axis=-1, keepdims=True)
    centered = v - mean
    scale = lax.rsqrt(jnp.mean(centered * centered, axis=-1, keepdims=True) + eps)
    return centered * scale, scale


def norm_back(hat, scale, gain, grad):
    scaled = grad * gain
    first = jnp.mean(scaled, axis=-1, keepdims=True)
    second = jnp.mean(scaled * hat, axis=-1, keepdims=True)
    return scale * (scaled - first - hat * second)


def gelu_pair(u):
    slope = math.sqrt(2 / math.pi)
    bent = jnp.tanh(slope * (u + 0.044715 * u * u * u))
    value = 0.5 * u * (1 + bent)
    rate = 0.5 * (1 + bent) + 0.5 * u * (1 - bent * bent) * slope * (1 + 3 * 0.044715 * u * u)
    return value, rate


def chosen_part(refs, number, index, f):
    if f is None:
        return refs[number][index]
    place = number ^ f
    value = refs[0][index]
    for k in range(1, len(refs)):
        value = jnp.where(place == k, refs[k][index], value)
    return value


def pack_small(w_ref, gains_ref, biases_ref, out_ref_in, up_ref, qv_ref, pack_ref, rows_ref):
    part = w_ref.shape[1]
    width = w_ref.shape[2]
    for c in range(3):
        pack_ref[:part, c * width : (c + 1) * width] = w_ref[c]
    rows_ref[...] = jnp.zeros_like(rows_ref)
    for k, ref in enumerate((gains_ref, biases_ref, out_ref_in)):
        rows_ref[0:2, k * width : k * width + part] = ref[...].astype(f32)
    up_rows, cols = up_ref.shape
    heads = qv_ref.shape[0]
    for lane in (0, HD):
        rows_ref[2 : 2 + up_rows, lane : lane + cols] = up_ref[...].astype(f32)
    for i in range(2):
        low = 2 + up_rows + i * heads
        rows_ref[low : low + heads, 0:cols] = qv_ref[:, i, :].astype(f32)
    pack_ref[part:, :] = rows_ref[...].astype(bf16)


def project(n, ordered, at_ref, own_ref, low_ref, high_ref, seg_ref, *refs):
    packs = refs[:n]
    rows_ref, turned_ref, att_ref, log_ref, hat_turned, params_ref, w_ref, qv_row, normed_ref, hat_ref = refs[n:]
    y = at_ref[0]
    f = at_ref[1] if ordered else None
    half = own_ref.shape[0]
    length = 2 * half
    width = own_ref.shape[1]
    part = width // n
    columns = w_ref.shape[1]
    group = columns // 3
    heads = group // HD
    small_rows = packs[0].shape[0] - part
    cols = HD // n
    up_rows = width // HD
    params_ref[...] = jnp.zeros_like(params_ref)
    qv_row[...] = jnp.zeros_like(qv_row)
    for p in range(n):
        w_ref[p * part : (p + 1) * part, :] = chosen_part(packs, p, (slice(0, part), slice(None)), f)
        small = chosen_part(packs, p, (slice(part, part + small_rows), slice(None)), f).astype(f32)
        for k in range(3):
            params_ref[2 * k : 2 * k + 2, p * part : (p + 1) * part] = small[
                0:2, k * group : k * group + part
            ]
        for r in range(up_rows):
            low = r * HD + p * cols
            params_ref[6:7, low : low + cols] = small[2 + r : 3 + r, 0:cols]
            params_ref[7:8, low : low + cols] = small[2 + r : 3 + r, HD : HD + cols]
        for i in range(2):
            for h in range(heads):
                low = 2 * i * group + h * HD + p * cols
                r = 2 + up_rows + i * heads + h
                qv_row[0:1, low : low + cols] = small[r : r + 1, 0:cols]
    gain = params_ref[0:1, :]
    shift = params_ref[2:3, :]
    middle = half // 2
    for rows, place in (
        (own_ref[:middle, :], 2 * y),
        (own_ref[middle:, :], 2 * y + 1),
        (low_ref[:middle, :], 2 - 2 * y),
        (high_ref[...], 3 - 2 * y),
    ):
        hat, _ = normalized(rows.astype(f32))
        here = pl.ds(pl.multiple_of(place * middle, middle), middle)
        hat_ref[here, :] = hat.astype(bf16)
        normed_ref[here, :] = (hat * gain + shift).astype(bf16)
    got_row = low_ref[middle : middle + 1, 0:half].astype(f32).astype(jnp.int32)
    own_row = seg_ref[...]
    first = y == 0
    seg = jnp.concatenate(
        [jnp.where(first, own_row, got_row), jnp.where(first, got_row, own_row)], axis=1
    )
    for low in range(0, length, QB):
        rows = slice(low, low + QB)
        block_rows = (dot(normed_ref[rows, :], w_ref[...]) + qv_row[...]).astype(bf16)
        hat_turned[:, rows] = turned(hat_ref[rows, :])
        rows_ref[rows, :] = block_rows
        turned_ref[:, rows] = turned(block_rows)
    start = starts_of(seg)
    for head in range(heads):
        rows = slice(head * HD, (head + 1) * HD)
        keys = rows_ref[:, group + head * HD : group + (head + 1) * HD]
        for low in range(0, length, QB):
            reach = low + QB
            at_cols = slice(low, reach)
            scores = dot(keys[:reach], turned_ref[rows, at_cols]) * score_scale
            scores = jnp.where(allowed_block(start, low, reach), scores, masked_score)
            top = jnp.max(scores, axis=0, keepdims=True)
            weight = jnp.exp2(scores - top)
            total = jnp.sum(weight, axis=0, keepdims=True)
            mixed = dot(
                turned_ref[2 * group + head * HD : 2 * group + (head + 1) * HD, :reach],
                weight.astype(bf16),
            )
            inside = low % half
            att_ref[low // half, rows, inside : inside + QB] = (mixed / total).astype(bf16)
            log_ref[head : head + 1, at_cols] = top + jnp.log2(total)
    log_ref[heads : heads + 1, :] = start.astype(f32)


def out_project(n, ordered, at_ref, att_ref, z_ref, y_ref, yz_ref, own_ref, params_ref, *refs):
    parts = refs[:n]
    hidden_ref, normed_ref, att_own_ref, out_ref, att_all = refs[n:]
    y, member = at_ref[0], at_ref[2]
    f = at_ref[1] if ordered else None
    group = z_ref.shape[0]
    half, width = own_ref.shape
    part = width // n
    att_all[0:group, :] = att_ref[y]
    for k, ref in enumerate((z_ref, y_ref, yz_ref)):
        att_all[(k + 1) * group : (k + 2) * group, :] = ref[...]
    for p in range(n):
        out_ref[p * part : (p + 1) * part, :] = chosen_part(parts, p, (slice(None), slice(None)), f)
    everything = att_all[...]
    att_own_ref[...] = jnp.where(member == 0, everything[:, : half // 2], everything[:, half // 2 :])
    for low in range(0, half, QB):
        rows = slice(low, low + QB)
        branch = dot_t(turned(everything[:, rows]), out_ref[...])
        hidden = own_ref[rows, :].astype(f32) + branch + params_ref[4:5, :]
        hidden_ref[rows, :] = hidden
        hat, _ = normalized(hidden)
        normed_ref[rows, :] = (hat * params_ref[1:2, :] + params_ref[3:4, :]).astype(bf16)


def feed_near(n, ordered, at_ref, normed_ref, params_ref, *refs):
    parts = refs[:n]
    act_ref, rate_ref, up_all, down_all, down_ref = refs[n:]
    f = at_ref[1] if ordered else None
    half, width = normed_ref.shape
    arrange(parts, f, up_all, down_all)
    shift = jnp.where(at_ref[3] == 1, params_ref[6:7, :], params_ref[7:8, :])
    for low in range(0, half, QB):
        rows = slice(low, low + QB)
        value, rate = gelu_pair(dot(normed_ref[rows, :], up_all[...]) + shift)
        act = value.astype(bf16)
        act_ref[rows, :] = act
        rate_ref[rows, :] = rate
        down_ref[rows, :] = dot_t(act, down_all[...])


def arrange(parts, f, up_all, down_all):
    part = parts[0].shape[0] // 2
    for p in range(len(parts)):
        here = slice(p * part, (p + 1) * part)
        up_all[here, :] = chosen_part(parts, p, (slice(0, part), slice(None)), f)
        down_all[here, :] = chosen_part(parts, p, (slice(part, 2 * part), slice(None)), f)


def feed_far(n, ordered, at_ref, normed_ref, cot_ref, params_ref, rate_one, up_one, down_one, down_in, *refs):
    parts = refs[:n]
    act_two, pre_one, pre_two, back_ref, back_send, down_ref, down_send, sum_ref, up_two, down_two = refs[n:]
    f = at_ref[1] if ordered else None
    member = at_ref[2]
    piece = normed_ref.shape[0] // 2
    arrange(parts, f, up_two, down_two)
    shift = jnp.where(at_ref[3] == 0, params_ref[6:7, :], params_ref[7:8, :])
    sum_ref[...] = jnp.zeros_like(sum_ref)
    for owner, back_out, down_out in ((1 - member, back_send, down_send), (member, back_ref, down_ref)):
        rows = pl.ds(pl.multiple_of(owner * piece, piece), piece)
        value, rate = gelu_pair(dot(normed_ref[rows, :], up_two[...]) + shift)
        act = value.astype(bf16)
        act_two[rows, :] = act
        down_out[...] = (down_in[rows, :] + dot_t(act, down_two[...])).astype(down_out.dtype)
        cot = cot_ref[rows, :]
        back = jnp.zeros((piece, back_ref.shape[1]), f32)
        for k, (slope, up, down, pre) in enumerate(
            ((rate_one[rows, :], up_one, down_one, pre_one), (rate, up_two, down_two, pre_two))
        ):
            grad_act = dot(cot, down[...]).astype(bf16)
            grad = (grad_act.astype(f32) * slope).astype(bf16)
            pre[rows, :] = grad
            sum_ref[k : k + 1, :] += jnp.sum(grad.astype(f32), axis=0, keepdims=True)
            back = back + dot_t(grad, up[...])
        back_out[...] = back.astype(back_out.dtype)


def feed_grads(ordered, at_ref, normed_ref, cot_ref, act_one, pre_one, act_two, pre_two, *refs):
    outs, whole = refs[:-1], refs[-1]
    normed_turned = turned(normed_ref[...])
    cot_turned = turned(cot_ref[...])
    for k, (act, pre) in enumerate(((act_one, pre_one), (act_two, pre_two))):
        for side, (left, right) in enumerate(((normed_turned, pre), (cot_turned, act))):
            whole[...] = dot(left, right[...]).astype(bf16)
            cut_rows(ordered, at_ref[1], whole, [ref.at[2 * k + side] for ref in outs])


def cut_rows(ordered, f, whole, outs):
    if not ordered:
        outs[0][...] = whole[...]
        return
    part = whole.shape[0] // 4
    for ref, core in zip(outs, (f & 1, 1 - (f & 1))):
        for x in range(2):
            ref[x] = whole[pl.ds(pl.multiple_of((2 * x + core) * part, part), part), :]


def core_sum(at_ref, kept_ref, got_ref, own_ref, *sends):
    x = at_ref[1] >> 1
    count = kept_ref.shape[0]
    each = count // len(sends)
    for k in range(count):
        own_ref[k] = kept_ref[k, x].astype(f32) + got_ref[k, x].astype(f32)
        sends[k // each][k % each] = (
            kept_ref[k, 1 - x].astype(f32) + got_ref[k, 1 - x].astype(f32)
        ).astype(bf16)


def x_sum(k, at_ref, own_ref, got_ref, send_ref, kept_ref):
    y = at_ref[0]
    kept_ref[...] = own_ref[2 * k + y] + got_ref[y].astype(f32)
    send_ref[...] = (own_ref[2 * k + 1 - y] + got_ref[1 - y].astype(f32)).astype(bf16)


def branch_back(
    at_ref, back_ref, got_ref, hidden_ref, cot_ref, out_ref, params_ref,
    grad_ref, branch_ref, g0, g1, g2, g3, sum_ref,
):
    piece = got_ref.shape[0]
    group = g0.shape[0]
    here = pl.ds(pl.multiple_of(at_ref[2] * piece, piece), piece)
    grad_two = back_ref[...] + got_ref[...].astype(f32)
    hat, scale = normalized(hidden_ref[here, :])
    cot = cot_ref[here, :].astype(f32)
    grad = cot + norm_back(hat, scale, params_ref[1:2, :], grad_two)
    grad_ref[...] = grad
    low = grad.astype(bf16)
    branch_ref[...] = low
    for k, ref in enumerate((g0, g1, g2, g3)):
        ref[...] = turned(dot(low, out_ref[:, k * group : (k + 1) * group]).astype(bf16))
    sum_ref[...] = jnp.zeros_like(sum_ref)
    sum_ref[0:1, :] = jnp.sum(grad_two * hat, axis=0, keepdims=True)
    sum_ref[1:2, :] = jnp.sum(grad_two, axis=0, keepdims=True)
    sum_ref[2:3, :] = jnp.sum(low.astype(f32), axis=0, keepdims=True)
    sum_ref[3:4, :] = jnp.sum(cot, axis=0, keepdims=True)


def attention_backward(
    ordered, at_ref, rows_in, turned_ref, g0, g1, g2, g3, log_ref, w_ref,
    hat_turned, columns_ref, branch_ref, att_ref, two_ref, up_ref, n0, n1, n2, n3, sum_ref, *refs
):
    outs, (out_ref, whole, key_sum, value_sum) = refs[:-4], refs[-4:]
    at = at_ref[4]
    length = rows_in.shape[0]
    group = turned_ref.shape[0] // 3
    heads = group // HD
    piece = n0.shape[0]
    start = log_ref[heads : heads + 1, :].astype(jnp.int32)
    for head in range(heads):
        rows = slice(head * HD, (head + 1) * HD)
        key_cols = slice(group + head * HD, group + (head + 1) * HD)
        value_cols = slice(2 * group + head * HD, 2 * group + (head + 1) * HD)
        keys = rows_in[:, key_cols]
        values = rows_in[:, value_cols]
        key_sum[...] = jnp.zeros_like(key_sum)
        value_sum[...] = jnp.zeros_like(value_sum)
        for low in range(0, length, QB):
            reach = low + QB
            cols = slice(low, reach)
            place = at ^ (low // QB)
            grad = g0[rows, :]
            for k, ref in ((1, g1), (2, g2), (3, g3)):
                grad = jnp.where(place == k, ref[rows, :], grad)
            scores = dot(keys[:reach], turned_ref[rows, cols]) * score_scale
            prob = jnp.exp2(scores - log_ref[head : head + 1, cols])
            prob = jnp.where(allowed_block(start, low, reach), prob, 0.0)
            grad_prob = dot(values[:reach], grad)
            inner = jnp.sum(prob * grad_prob, axis=0, keepdims=True)
            grad_scores = (prob * (grad_prob - inner) * 0.125).astype(bf16)
            grad_query = dot(turned_ref[key_cols, :reach], grad_scores)
            out_ref[cols, rows] = grad_query.T.astype(bf16)
            key_sum[:reach] += dot(grad_scores, rows_in[cols, rows])
            value_sum[:reach] += dot(prob.astype(bf16), turned(grad))
        out_ref[:, key_cols] = key_sum[...].astype(bf16)
        out_ref[:, value_cols] = value_sum[...].astype(bf16)
    for k, ref in ((3, n3), (2, n2), (1, n1), (0, n0)):
        here = pl.ds(pl.multiple_of((at ^ k) * piece, piece), piece)
        ref[...] = dot_t(out_ref[here, :], w_ref[...]).astype(ref.dtype)
    gain, shift = columns_ref[:, 0:1], columns_ref[:, 2:3]
    rows = out_ref[...]
    row_sum = jnp.sum(rows.astype(f32), axis=0, keepdims=True)
    base = dot(hat_turned[...], rows)
    whole[:, 2 * group : 5 * group] = (gain * base + shift * row_sum).astype(bf16)
    out_grad = dot_t(turned(branch_ref[...]), att_ref[...]).astype(bf16)
    for place, k in ((0, 1), (1, 3), (5, 0), (6, 2)):
        whole[:, place * group : (place + 1) * group] = out_grad[:, k * group : (k + 1) * group]
    cut_rows(ordered, at_ref[1], whole, [ref.at[0] for ref in outs])
    weights = w_ref[...]
    products = (weights.astype(f32) * base).astype(bf16)
    first = dot_t(jnp.ones((8, 3 * group), bf16), products)[0:1]
    high = jnp.broadcast_to(row_sum, (8, 3 * group)).astype(bf16)
    low = (jnp.broadcast_to(row_sum, (8, 3 * group)) - high.astype(f32)).astype(bf16)
    second = (dot_t(high, weights) + dot_t(low, weights))[0:1]
    sum_ref[...] = jnp.zeros_like(sum_ref)
    sum_ref[0:1, :] = first
    sum_ref[1:2, :] = two_ref[0:1, :]
    sum_ref[2:3, :] = second
    sum_ref[3:6, :] = two_ref[1:4, :]
    z = at_ref[5]
    query = row_sum[:, :group]
    value = row_sum[:, 2 * group :]
    for k in range(4):
        row = slice(6 + k, 7 + k)
        sum_ref[row, :] = jnp.where(z == k, up_ref[0:1, :], jnp.where((z ^ 2) == k, up_ref[1:2, :], 0.0))
        row = slice(10 + k, 11 + k)
        sum_ref[row, :group] = jnp.where(at_ref[4] == k, query, 0.0)
        sum_ref[row, group : 2 * group] = jnp.where(at_ref[4] == k, value, 0.0)


def token_back(at_ref, n0, second_ref, near_ref, own_ref, params_ref, grad_ref, out_ref):
    piece = n0.shape[0]
    here = pl.ds(pl.multiple_of(at_ref[2] * piece, piece), piece)
    grad_normed = n0[...].astype(f32) + second_ref[...].astype(f32) + near_ref[...].astype(f32)
    hat, scale = normalized(own_ref[here, :].astype(f32))
    rows = grad_ref[...] + norm_back(hat, scale, params_ref[0:1, :], grad_normed)
    out_ref[...] = rows.astype(bf16)


def place_rows(at_ref, p0, p1, p2, p3, out_ref):
    for k, ref in enumerate((p0, p1, p2, p3)):
        out_ref[at_ref[0] ^ k] = ref[...].astype(out_ref.dtype)


def pick(v, index, axis):
    return lax.dynamic_index_in_dim(v, index, axis, keepdims=False)


def struct(shape, dtype=bf16):
    return jax.ShapeDtypeStruct(shape, dtype)


def call(body, name, scalars, arrays, outs, scratch=(), us=1):
    vmem = pl.BlockSpec(memory_space=pltpu.VMEM)
    specs = [vmem] * len(arrays)
    if scalars is not None:
        specs = [pl.BlockSpec(memory_space=pltpu.SMEM)] + specs
        arrays = (scalars,) + tuple(arrays)
    return pl.pallas_call(
        body, out_shape=outs, in_specs=specs, scratch_shapes=list(scratch), name=name,
        cost_estimate=pl.CostEstimate(flops=0, transcendentals=0, bytes_accessed=us * 3000000),
    )(*arrays)


def block(
    tokens,
    segments,
    ln_gains,
    ln_biases,
    w_qkv,
    bias_qv,
    w_out,
    out_biases,
    w_up,
    up_bias,
    w_down,
    cotangent,
    *,
    fsdp,
    ctx,
    tp,
):
    seq_count, half, width = tokens.shape
    part = w_up.shape[0]
    group = w_qkv.shape[2]
    head_count = group // HD
    hidden_part = w_up.shape[1]
    length = 2 * half
    piece = half // 2
    bias_rows, bias_cols = up_bias.shape
    assert ctx == 2 and seq_count == 2 and tp == 4
    f = lax.axis_index("fsdp")
    y = lax.axis_index("ctx")
    z = lax.axis_index("tp")
    seq = z >> 1
    member = z & 1
    same = seq == y
    at = 2 * y + member
    ordered = fsdp == 4
    scalars = jnp.stack([y, f, member, same.astype(jnp.int32), at, z]).astype(jnp.int32)

    def after(v, *others):
        return lax.optimization_barrier((v,) + others)[0]

    def swap_y(v):
        return swap(v, "ctx", 1, ctx)

    def swap_z(v, bit):
        return swap(v, "tp", bit, tp)

    def swap_yz(v, bit):
        pairs = [(a * tp + b, (1 - a) * tp + (b ^ bit)) for a in range(2) for b in range(tp)]
        return lax.ppermute(v, ("ctx", "tp"), pairs)

    def gather_parts(v, far=None):
        if not ordered:
            got = lax.all_gather(v, "fsdp", axis=0, tiled=False)
            return [got[i] for i in range(fsdp)]
        if far is None:
            far = swap(v, "fsdp", 2, fsdp)
        near = swap(v, "fsdp", 1, fsdp)
        cross = swap(far, "fsdp", 1, fsdp)
        return [v, near, far, cross]

    small_rows = 24
    pack = call(
        pack_small,
        "pack_small",
        None,
        (w_qkv, ln_gains, ln_biases, out_biases, up_bias, jnp.swapaxes(bias_qv, 0, 1)),
        struct((part + small_rows, 3 * group)),
        [pltpu.VMEM((small_rows, 3 * group), f32)],
    )
    pack_far = swap_z(pack, 2)
    out_turned = w_out.T
    out_near = swap_z(after(out_turned, pack), 1)
    tok_own = pick(after(tokens, out_near), seq, 0)
    seg_own = pick(after(segments, out_near), seq, 0)
    seg_row = jnp.pad(seg_own.astype(bf16), (0, width - half)).reshape(1, width)
    tok_low = swap_y(jnp.concatenate([tok_own[:piece], seg_row], axis=0))
    tok_high = swap_y(after(tok_own[piece:], tok_low))
    mlp_pack = jnp.concatenate([after(w_up, pack), w_down.T], axis=0)
    place = lax.broadcasted_iota(jnp.int32, pack.shape, 0)
    lane = lax.broadcasted_iota(jnp.int32, pack.shape, 1)
    turned_choice = (place >= part + 2) & (lane >= HD) & (lane < 2 * HD)
    chosen = jnp.where(turned_choice ^ same, pack, pack_far)
    packs = gather_parts(chosen)
    out_two = jnp.concatenate([out_turned, out_near], axis=1)
    out_far = swap_z(after(out_two, pack_far), 2)
    mlp_far = swap_z(after(mlp_pack, out_far, tok_low), 2)
    near_x = swap(after(mlp_pack, packs[2], out_far), "fsdp", 2, fsdp) if ordered else mlp_pack

    qkv_rows, qkv_turned, attended, logs, hat_turned, params, proj_rows = call(
        functools.partial(project, fsdp, ordered),
        "project",
        scalars,
        (tok_own, tok_low, tok_high, seg_own.reshape(1, half), *packs),
        (
            struct((length, 3 * group)),
            struct((3 * group, length)),
            struct((2, group, half)),
            struct((head_count + 1, length), f32),
            struct((width, length)),
            struct((8, width), f32),
            struct((width, 3 * group)),
        ),
        [pltpu.VMEM((1, 3 * group), f32)] + [pltpu.VMEM((length, width), bf16)] * 2,
        12,
    )

    att_here, att_there = pick(attended, y, 0), pick(attended, 1 - y, 0)
    attended, out_two, out_far = lax.optimization_barrier((attended, out_two, out_far, near_x))[:3]
    out_four = jnp.concatenate(
        [jnp.where(same, out_two, out_far), jnp.where(same, out_far, out_two)], axis=1
    )
    out_x = swap(out_four, "fsdp", 2, fsdp) if ordered else None
    att_y, att_yz, att_z = swap_y(att_there), swap_yz(att_there, 1), swap_z(att_here, 1)
    if ordered:
        out_four, out_x, near_own, near_x = lax.optimization_barrier(
            (out_four, out_x, mlp_pack, near_x, att_z, att_y, att_yz)
        )[:4]
    else:
        near_own = mlp_pack
    out_parts = gather_parts(out_four, out_x)
    near_parts = gather_parts(near_own, near_x)
    hidden, normed_two, att_own, out_proj = call(
        functools.partial(out_project, fsdp, ordered),
        "out_project",
        scalars,
        (attended, att_z, att_y, att_yz, tok_own, params, *out_parts),
        (
            struct((half, width), f32),
            struct((half, width)),
            struct((4 * group, piece)),
            struct((width, 4 * group)),
        ),
        [pltpu.VMEM((4 * group, half), bf16)],
        4,
    )

    cot = pick(cotangent, seq, 0)
    rows_f, rows_b = struct((half, width), f32), struct((half, hidden_part))
    rate_f, square = struct((half, hidden_part), f32), struct((width, hidden_part))
    half_b = struct((piece, width))
    act_one, rate_one, up_one, down_one, down_sum = call(
        functools.partial(feed_near, fsdp, ordered),
        "feed_near",
        scalars,
        (normed_two, params, *near_parts),
        (rows_b, rate_f, square, square, rows_f),
        us=4,
    )
    if ordered:
        far_x = swap(after(mlp_far, att_z, att_y, att_yz), "fsdp", 2, fsdp)
        far_own, far_x = lax.optimization_barrier((mlp_far, far_x, act_one))[:2]
        far_parts = gather_parts(far_own, far_x)
    else:
        far_parts = gather_parts(mlp_far)
    piece_f, sum_f = struct((piece, width), f32), struct((8, hidden_part), f32)
    act_two, pre_one, pre_two, back, back_send, down_own, down_send, up_sums = call(
        functools.partial(feed_far, fsdp, ordered),
        "feed_far",
        scalars,
        (normed_two, cot, params, rate_one, up_one, down_one, down_sum, *far_parts),
        (rows_b, rows_b, rows_b, piece_f, half_b, piece_f, half_b, sum_f),
        [pltpu.VMEM((width, hidden_part), bf16)] * 2,
        us=9,
    )
    back_got = swap_z(back_send, 1)
    cut = (2, part) if ordered else (width,)
    grad_outs = [struct((4,) + cut + (hidden_part,))] * (2 if ordered else 1)
    mlp_grads = call(
        functools.partial(feed_grads, ordered),
        "feed_grads",
        scalars,
        (normed_two, cot, act_one, pre_one, act_two, pre_two),
        tuple(grad_outs),
        [pltpu.VMEM((width, hidden_part), bf16)],
        us=8,
    )

    def scatter(parts, name, count, gate, later):
        if not ordered:
            v = lax.psum_scatter(parts[0], "fsdp", scatter_dimension=1, tiled=True)
            each = v.shape[0] // count
            zeros = [jnp.zeros_like(v[:each])] * count
            return v.astype(f32), zeros, zeros[-1:]
        kept, sent = parts
        got = swap(after(sent, *gate), "fsdp", 1, fsdp)
        shape = kept.shape[:1] + kept.shape[2:]
        each = (shape[0] // count,) + shape[1:]
        kept, *sent = call(
            core_sum, name, scalars, (after(kept, later), got), (struct(shape, f32), *[struct(each)] * count), us=2
        )
        return kept, sent, [swap_x(v) for v in sent[-1:]]

    def swap_x(v, *gate):
        return swap(after(v, *gate), "fsdp", 2, fsdp) if ordered else v

    def mine(v):
        return pick(v.reshape((2, piece) + v.shape[1:]), member, 0)

    def spread(rows, name, dtype, gate=()):
        far = swap_z(rows, 2)
        near = swap_z(rows, 1)
        cross = swap_z(after(far, near, *gate), 1)
        placed = call(
            place_rows, name, z.reshape(1), (rows, near, far, cross), struct((tp, piece, width), dtype)
        )
        return placed.reshape(seq_count, half, width), (near, far), cross

    grad_hidden, grad_branch, g0, g1, g2, g3, sums_two = call(
        branch_back,
        "branch_back",
        scalars,
        (back, back_got, hidden, cot, out_proj, params),
        (
            struct((piece, width), f32),
            struct((piece, width)),
            *[struct((group, piece))] * 4,
            struct((8, width), f32),
        ),
    )
    down_got = swap_z(after(down_send, g0), 1)
    g_y, g_yz, g_z = swap_y(g2), swap_yz(g3, 1), swap_z(g1, 1)
    grads_kept, grads_sent, (far_x,) = scatter(mlp_grads, "core_sum_feed", 2, (g0,), g_y)
    result_rows = (mine(hidden) + down_own + down_got.astype(f32) + params[5:6]).astype(bf16)
    result_rows = after(result_rows, g_y, g_yz, g_z)
    result, result_gate, result_cross = spread(result_rows, "place_result", bf16)
    late_outs = [struct((1,) + cut + (7 * group,))] * (2 if ordered else 1)
    n0, n1, n2, n3, sums, *late = call(
        functools.partial(attention_backward, ordered),
        "attention_backward",
        scalars,
        (
            qkv_rows, qkv_turned, after(g0, result_rows, *grads_sent), g_z, g_y, g_yz, logs, proj_rows,
            hat_turned, params.T, grad_branch, att_own, sums_two, up_sums,
        ),
        (*[struct((piece, width))] * 4, struct((16, width), f32), *late_outs),
        [
            pltpu.VMEM((length, 3 * group), bf16),
            pltpu.VMEM((width, 7 * group), bf16),
            pltpu.VMEM((length, HD), f32),
            pltpu.VMEM((length, HD), f32),
        ],
        us=16,
    )
    first_got = swap_y(after(n3, *result_gate, far_x))
    late_kept, late_sent, _ = scatter(
        late, "core_sum_late", 1, (*result_gate, far_x), first_got
    )
    late_first = late_sent[0]
    halves = (struct((part, hidden_part)), struct((part, hidden_part), f32))
    far_sent, far_kept = call(
        functools.partial(x_sum, 1),
        "x_sum_far",
        scalars,
        (after(grads_kept, first_got), far_x),
        halves,
    )
    share = n1.astype(f32) + first_got.astype(f32)
    near_got = swap_z(share.astype(bf16), 1)
    second_got = swap_y(after(n2, first_got))
    token_rows = call(
        token_back,
        "token_back",
        scalars,
        (after(n0, late_first, far_sent), second_got, near_got, tok_own, params, grad_hidden),
        struct((piece, width)),
        us=3,
    )
    far_got = swap_y(after(far_sent, second_got))
    late_got = swap_x(late_sent[0], first_got)
    near_x_got = swap_x(grads_sent[0], second_got)
    far_far = swap_z(after((far_kept + far_got.astype(f32)).astype(bf16), token_rows), 2)
    grad_tokens, token_gate, token_cross = spread(
        token_rows, "place_tokens", f32, (result_cross, late_got, far_far)
    )
    sums = after(sums, *token_gate, far_got, near_x_got)
    sums = sums + swap_y(sums)
    if ordered:
        sums = sums + swap(sums, "fsdp", 1, fsdp)
        sums = sums + swap(sums, "fsdp", 2, fsdp)
    else:
        sums = lax.psum(sums, "fsdp")
    near_sent, near_kept = call(
        functools.partial(x_sum, 0),
        "x_sum_near",
        scalars,
        (after(grads_kept, *token_gate), near_x_got),
        halves,
    )
    half_got = swap_y(after(near_sent, near_got))
    half_grad = (near_kept + half_got.astype(f32) + far_far.astype(f32)).astype(bf16)
    rest_grad = swap_y(half_grad)
    grad_up = jnp.where(y == 0, half_grad, rest_grad).astype(f32)
    grad_down = jnp.where(y == 0, rest_grad, half_grad).astype(f32).T

    late = late_kept[0] + late_got[0].astype(f32)
    out_got = swap_z(after(late[:, : 2 * group].astype(bf16), *token_gate), 1).astype(f32)
    grad_qkv = late[:, 2 * group : 5 * group].astype(bf16)
    out_first = late[:, 5 * group : 6 * group] + out_got[:, :group]
    out_second = late[:, 6 * group :] + out_got[:, group:]
    out_here = jnp.where(same, out_first, out_second).astype(bf16)
    out_there = jnp.where(same, out_second, out_first).astype(bf16)
    kept = jnp.concatenate([grad_qkv, out_here], axis=1).astype(f32)
    both = (
        kept + swap_z(jnp.concatenate([grad_qkv, out_there], axis=1), 2).astype(f32)
    ).astype(bf16)
    both_got = swap_y(both)
    grad_qkv = jnp.where(same, both, both_got)[:, : 3 * group].astype(f32)
    grad_qkv = jnp.moveaxis(grad_qkv.reshape(part, 3, group), 1, 0)
    grad_out = (both[:, 3 * group :].astype(f32) + both_got[:, 3 * group :].astype(f32)).T

    sums = after(sums, out_got, token_cross)
    sums = sums + swap_z(sums, 1)
    sums = sums + swap_z(sums, 2)
    norm_sums = pick(sums[:6].reshape(6, fsdp, part), f, 1)
    up_total = pick(sums[6 : 6 + tp], z, 0)
    grad_up_bias = pick(up_total.reshape(bias_rows, fsdp, bias_cols), f, 1)
    qv_total = pick(sums[6 + tp : 6 + 2 * tp, : 2 * group], z, 0)
    grad_qv = pick(qv_total.reshape(2, head_count, fsdp, bias_cols), f, 2)
    return (
        result,
        grad_tokens,
        norm_sums[0:2],
        norm_sums[2:4],
        grad_qkv,
        grad_qv,
        grad_out,
        norm_sums[4:6],
        grad_up,
        grad_up_bias,
        grad_down,
    )


def solution(mesh):
    in_specs = (
        P("fsdp", "ctx", None),
        P("fsdp", "ctx"),
        P(None, "fsdp"),
        P(None, "fsdp"),
        P(None, "fsdp", "tp"),
        P(None, "tp", "fsdp"),
        P("tp", "fsdp"),
        P(None, "fsdp"),
        P("fsdp", "tp"),
        P("tp", "fsdp"),
        P("tp", "fsdp"),
        P("fsdp", "ctx", None),
    )
    out_specs = (
        P("fsdp", "ctx", None),
        P("fsdp", "ctx", None),
        P(None, "fsdp"),
        P(None, "fsdp"),
        P(None, "fsdp", "tp"),
        P(None, "tp", "fsdp"),
        P("tp", "fsdp"),
        P(None, "fsdp"),
        P("fsdp", "tp"),
        P("tp", "fsdp"),
        P("tp", "fsdp"),
    )
    local = functools.partial(
        block, fsdp=mesh.shape["fsdp"], ctx=mesh.shape["ctx"], tp=mesh.shape["tp"]
    )
    return jax.shard_map(local, mesh=mesh, in_specs=in_specs, out_specs=out_specs, check_vma=False)
```

```python
import functools
import math

import jax
import jax.numpy as jnp
from jax import lax
from jax.experimental import pallas as pl
from jax.experimental.pallas import tpu as pltpu
from jax.sharding import PartitionSpec as P

HD = 64
QB = 256
eps = 1e-05
masked_score = -1e30
score_scale = 0.125 * math.log2(math.e)
f32 = jnp.float32
bf16 = jnp.bfloat16


def swap(v, axis, bit, size):
    return lax.ppermute(v, axis, [(i, i ^ bit) for i in range(size)])


def dot(a, b):
    return lax.dot_general(a, b, (((1,), (0,)), ((), ())), preferred_element_type=f32)


def turned(v):
    return v.astype(f32).T.astype(v.dtype)


def starts_of(seg):
    start = jnp.zeros(seg.shape, jnp.int32)
    for number in range(3):
        count = jnp.sum((seg == number).astype(jnp.int32), axis=1, keepdims=True)
        start = start + jnp.where(seg > number, count, 0)
    return start


def allowed_block(start, first, width):
    place = lax.broadcasted_iota(jnp.int32, (width, QB), 0)
    allowed = place >= start[:, first : first + QB]
    query = lax.broadcasted_iota(jnp.int32, (width, QB), 1) + first
    return allowed & (place <= query)


def dot_t(a, b):
    return lax.dot_general(a, b, (((1,), (1,)), ((), ())), preferred_element_type=f32)


def normalized(v):
    mean = jnp.mean(v, axis=-1, keepdims=True)
    centered = v - mean
    scale = lax.rsqrt(jnp.mean(centered * centered, axis=-1, keepdims=True) + eps)
    return centered * scale, scale


def norm_back(hat, scale, gain, grad):
    scaled = grad * gain
    first = jnp.mean(scaled, axis=-1, keepdims=True)
    second = jnp.mean(scaled * hat, axis=-1, keepdims=True)
    return scale * (scaled - first - hat * second)


def gelu_pair(u):
    slope = math.sqrt(2 / math.pi)
    bent = jnp.tanh(slope * (u + 0.044715 * u * u * u))
    value = 0.5 * u * (1 + bent)
    rate = 0.5 * (1 + bent) + 0.5 * u * (1 - bent * bent) * slope * (1 + 3 * 0.044715 * u * u)
    return value, rate


def chosen_part(refs, number, index, f):
    if f is None:
        return refs[number][index]
    place = number ^ f
    value = refs[0][index]
    for k in range(1, len(refs)):
        value = jnp.where(place == k, refs[k][index], value)
    return value


def pack_small(w_ref, gains_ref, biases_ref, out_ref_in, up_ref, qv_ref, pack_ref, rows_ref):
    part = w_ref.shape[1]
    width = w_ref.shape[2]
    for c in range(3):
        pack_ref[:part, c * width : (c + 1) * width] = w_ref[c]
    rows_ref[...] = jnp.zeros_like(rows_ref)
    for k, ref in enumerate((gains_ref, biases_ref, out_ref_in)):
        rows_ref[0:2, k * width : k * width + part] = ref[...].astype(f32)
    up_rows, cols = up_ref.shape
    heads = qv_ref.shape[0]
    for lane in (0, HD):
        rows_ref[2 : 2 + up_rows, lane : lane + cols] = up_ref[...].astype(f32)
    for i in range(2):
        low = 2 + up_rows + i * heads
        rows_ref[low : low + heads, 0:cols] = qv_ref[:, i, :].astype(f32)
    pack_ref[part:, :] = rows_ref[...].astype(bf16)


def project(n, ordered, at_ref, own_ref, low_ref, high_ref, seg_ref, *refs):
    packs = refs[:n]
    rows_ref, turned_ref, att_ref, log_ref, hat_turned, params_ref, w_ref, qv_row, normed_ref, hat_ref = refs[n:]
    y = at_ref[0]
    f = at_ref[1] if ordered else None
    half = own_ref.shape[0]
    length = 2 * half
    width = own_ref.shape[1]
    part = width // n
    columns = w_ref.shape[1]
    group = columns // 3
    heads = group // HD
    small_rows = packs[0].shape[0] - part
    cols = HD // n
    up_rows = width // HD
    params_ref[...] = jnp.zeros_like(params_ref)
    qv_row[...] = jnp.zeros_like(qv_row)
    for p in range(n):
        w_ref[p * part : (p + 1) * part, :] = chosen_part(packs, p, (slice(0, part), slice(None)), f)
        small = chosen_part(packs, p, (slice(part, part + small_rows), slice(None)), f).astype(f32)
        for k in range(3):
            params_ref[2 * k : 2 * k + 2, p * part : (p + 1) * part] = small[
                0:2, k * group : k * group + part
            ]
        for r in range(up_rows):
            low = r * HD + p * cols
            params_ref[6:7, low : low + cols] = small[2 + r : 3 + r, 0:cols]
            params_ref[7:8, low : low + cols] = small[2 + r : 3 + r, HD : HD + cols]
        for i in range(2):
            for h in range(heads):
                low = 2 * i * group + h * HD + p * cols
                r = 2 + up_rows + i * heads + h
                qv_row[0:1, low : low + cols] = small[r : r + 1, 0:cols]
    gain = params_ref[0:1, :]
    shift = params_ref[2:3, :]
    middle = half // 2
    for rows, place in (
        (own_ref[:middle, :], 2 * y),
        (own_ref[middle:, :], 2 * y + 1),
        (low_ref[:middle, :], 2 - 2 * y),
        (high_ref[...], 3 - 2 * y),
    ):
        hat, _ = normalized(rows.astype(f32))
        here = pl.ds(pl.multiple_of(place * middle, middle), middle)
        hat_ref[here, :] = hat.astype(bf16)
        normed_ref[here, :] = (hat * gain + shift).astype(bf16)
    got_row = low_ref[middle : middle + 1, 0:half].astype(f32).astype(jnp.int32)
    own_row = seg_ref[...]
    first = y == 0
    seg = jnp.concatenate(
        [jnp.where(first, own_row, got_row), jnp.where(first, got_row, own_row)], axis=1
    )
    for low in range(0, length, QB):
        rows = slice(low, low + QB)
        block_rows = (dot(normed_ref[rows, :], w_ref[...]) + qv_row[...]).astype(bf16)
        hat_turned[:, rows] = turned(hat_ref[rows, :])
        rows_ref[rows, :] = block_rows
        turned_ref[:, rows] = turned(block_rows)
    start = starts_of(seg)
    for head in range(heads):
        rows = slice(head * HD, (head + 1) * HD)
        keys = rows_ref[:, group + head * HD : group + (head + 1) * HD]
        for low in range(0, length, QB):
            reach = low + QB
            at_cols = slice(low, reach)
            scores = dot(keys[:reach], turned_ref[rows, at_cols]) * score_scale
            scores = jnp.where(allowed_block(start, low, reach), scores, masked_score)
            top = jnp.max(scores, axis=0, keepdims=True)
            weight = jnp.exp2(scores - top)
            total = jnp.sum(weight, axis=0, keepdims=True)
            mixed = dot(
                turned_ref[2 * group + head * HD : 2 * group + (head + 1) * HD, :reach],
                weight.astype(bf16),
            )
            inside = low % half
            att_ref[low // half, rows, inside : inside + QB] = (mixed / total).astype(bf16)
            log_ref[head : head + 1, at_cols] = top + jnp.log2(total)
    log_ref[heads : heads + 1, :] = start.astype(f32)


def out_project(n, ordered, at_ref, att_ref, z_ref, y_ref, yz_ref, own_ref, params_ref, *refs):
    parts = refs[:n]
    hidden_ref, normed_ref, att_own_ref, out_ref, att_all = refs[n:]
    y, member = at_ref[0], at_ref[2]
    f = at_ref[1] if ordered else None
    group = z_ref.shape[0]
    half, width = own_ref.shape
    part = width // n
    att_all[0:group, :] = att_ref[y]
    for k, ref in enumerate((z_ref, y_ref, yz_ref)):
        att_all[(k + 1) * group : (k + 2) * group, :] = ref[...]
    for p in range(n):
        out_ref[p * part : (p + 1) * part, :] = chosen_part(parts, p, (slice(None), slice(None)), f)
    everything = att_all[...]
    att_own_ref[...] = jnp.where(member == 0, everything[:, : half // 2], everything[:, half // 2 :])
    for low in range(0, half, QB):
        rows = slice(low, low + QB)
        branch = dot_t(turned(everything[:, rows]), out_ref[...])
        hidden = own_ref[rows, :].astype(f32) + branch + params_ref[4:5, :]
        hidden_ref[rows, :] = hidden
        hat, _ = normalized(hidden)
        normed_ref[rows, :] = (hat * params_ref[1:2, :] + params_ref[3:4, :]).astype(bf16)


def feed_near(n, ordered, at_ref, normed_ref, params_ref, *refs):
    parts = refs[:n]
    act_ref, rate_ref, up_all, down_all, down_ref = refs[n:]
    f = at_ref[1] if ordered else None
    half, width = normed_ref.shape
    arrange(parts, f, up_all, down_all)
    shift = jnp.where(at_ref[3] == 1, params_ref[6:7, :], params_ref[7:8, :])
    for low in range(0, half, QB):
        rows = slice(low, low + QB)
        value, rate = gelu_pair(dot(normed_ref[rows, :], up_all[...]) + shift)
        act = value.astype(bf16)
        act_ref[rows, :] = act
        rate_ref[rows, :] = rate
        down_ref[rows, :] = dot_t(act, down_all[...])


def arrange(parts, f, up_all, down_all):
    part = parts[0].shape[0] // 2
    for p in range(len(parts)):
        here = slice(p * part, (p + 1) * part)
        up_all[here, :] = chosen_part(parts, p, (slice(0, part), slice(None)), f)
        down_all[here, :] = chosen_part(parts, p, (slice(part, 2 * part), slice(None)), f)


def feed_far(n, ordered, at_ref, normed_ref, cot_ref, params_ref, rate_one, up_one, down_one, down_in, *refs):
    parts = refs[:n]
    act_two, pre_one, pre_two, back_ref, back_send, down_ref, down_send, sum_ref, up_two, down_two = refs[n:]
    f = at_ref[1] if ordered else None
    member = at_ref[2]
    piece = normed_ref.shape[0] // 2
    arrange(parts, f, up_two, down_two)
    shift = jnp.where(at_ref[3] == 0, params_ref[6:7, :], params_ref[7:8, :])
    sum_ref[...] = jnp.zeros_like(sum_ref)
    for owner, back_out, down_out in ((1 - member, back_send, down_send), (member, back_ref, down_ref)):
        rows = pl.ds(pl.multiple_of(owner * piece, piece), piece)
        value, rate = gelu_pair(dot(normed_ref[rows, :], up_two[...]) + shift)
        act = value.astype(bf16)
        act_two[rows, :] = act
        down_out[...] = (down_in[rows, :] + dot_t(act, down_two[...])).astype(down_out.dtype)
        cot = cot_ref[rows, :]
        back = jnp.zeros((piece, back_ref.shape[1]), f32)
        for k, (slope, up, down, pre) in enumerate(
            ((rate_one[rows, :], up_one, down_one, pre_one), (rate, up_two, down_two, pre_two))
        ):
            grad_act = dot(cot, down[...]).astype(bf16)
            grad = (grad_act.astype(f32) * slope).astype(bf16)
            pre[rows, :] = grad
            sum_ref[k : k + 1, :] += jnp.sum(grad.astype(f32), axis=0, keepdims=True)
            back = back + dot_t(grad, up[...])
        back_out[...] = back.astype(back_out.dtype)


def feed_grads(ordered, at_ref, normed_ref, cot_ref, act_one, pre_one, act_two, pre_two, *refs):
    outs, whole = refs[:-1], refs[-1]
    normed_turned = turned(normed_ref[...])
    cot_turned = turned(cot_ref[...])
    for k, (act, pre) in enumerate(((act_one, pre_one), (act_two, pre_two))):
        for side, (left, right) in enumerate(((normed_turned, pre), (cot_turned, act))):
            whole[...] = dot(left, right[...]).astype(bf16)
            cut_rows(ordered, at_ref[1], whole, [ref.at[2 * k + side] for ref in outs])


def cut_rows(ordered, f, whole, outs):
    if not ordered:
        outs[0][...] = whole[...]
        return
    part = whole.shape[0] // 4
    for ref, core in zip(outs, (f & 1, 1 - (f & 1))):
        for x in range(2):
            ref[x] = whole[pl.ds(pl.multiple_of((2 * x + core) * part, part), part), :]


def core_sum(at_ref, kept_ref, got_ref, own_ref, *sends):
    x = at_ref[1] >> 1
    count = kept_ref.shape[0]
    each = count // len(sends)
    for k in range(count):
        own_ref[k] = kept_ref[k, x].astype(f32) + got_ref[k, x].astype(f32)
        sends[k // each][k % each] = (
            kept_ref[k, 1 - x].astype(f32) + got_ref[k, 1 - x].astype(f32)
        ).astype(bf16)


def x_sum(k, at_ref, own_ref, got_ref, send_ref, kept_ref):
    y = at_ref[0]
    kept_ref[...] = own_ref[2 * k + y] + got_ref[y].astype(f32)
    send_ref[...] = (own_ref[2 * k + 1 - y] + got_ref[1 - y].astype(f32)).astype(bf16)


def branch_back(
    at_ref, back_ref, got_ref, hidden_ref, cot_ref, out_ref, params_ref,
    grad_ref, branch_ref, g0, g1, g2, g3, sum_ref,
):
    piece = got_ref.shape[0]
    group = g0.shape[0]
    here = pl.ds(pl.multiple_of(at_ref[2] * piece, piece), piece)
    grad_two = back_ref[...] + got_ref[...].astype(f32)
    hat, scale = normalized(hidden_ref[here, :])
    cot = cot_ref[here, :].astype(f32)
    grad = cot + norm_back(hat, scale, params_ref[1:2, :], grad_two)
    grad_ref[...] = grad
    low = grad.astype(bf16)
    branch_ref[...] = low
    for k, ref in enumerate((g0, g1, g2, g3)):
        ref[...] = turned(dot(low, out_ref[:, k * group : (k + 1) * group]).astype(bf16))
    sum_ref[...] = jnp.zeros_like(sum_ref)
    sum_ref[0:1, :] = jnp.sum(grad_two * hat, axis=0, keepdims=True)
    sum_ref[1:2, :] = jnp.sum(grad_two, axis=0, keepdims=True)
    sum_ref[2:3, :] = jnp.sum(low.astype(f32), axis=0, keepdims=True)
    sum_ref[3:4, :] = jnp.sum(cot, axis=0, keepdims=True)


def attention_backward(
    ordered, at_ref, rows_in, turned_ref, g0, g1, g2, g3, log_ref, w_ref,
    hat_turned, columns_ref, branch_ref, att_ref, two_ref, up_ref, n0, n1, n2, n3, sum_ref, *refs
):
    outs, (out_ref, whole, key_sum, value_sum) = refs[:-4], refs[-4:]
    at = at_ref[4]
    length = rows_in.shape[0]
    group = turned_ref.shape[0] // 3
    heads = group // HD
    piece = n0.shape[0]
    start = log_ref[heads : heads + 1, :].astype(jnp.int32)
    for head in range(heads):
        rows = slice(head * HD, (head + 1) * HD)
        key_cols = slice(group + head * HD, group + (head + 1) * HD)
        value_cols = slice(2 * group + head * HD, 2 * group + (head + 1) * HD)
        keys = rows_in[:, key_cols]
        values = rows_in[:, value_cols]
        key_sum[...] = jnp.zeros_like(key_sum)
        value_sum[...] = jnp.zeros_like(value_sum)
        for low in range(0, length, QB):
            reach = low + QB
            cols = slice(low, reach)
            place = at ^ (low // QB)
            grad = g0[rows, :]
            for k, ref in ((1, g1), (2, g2), (3, g3)):
                grad = jnp.where(place == k, ref[rows, :], grad)
            scores = dot(keys[:reach], turned_ref[rows, cols]) * score_scale
            prob = jnp.exp2(scores - log_ref[head : head + 1, cols])
            prob = jnp.where(allowed_block(start, low, reach), prob, 0.0)
            grad_prob = dot(values[:reach], grad)
            inner = jnp.sum(prob * grad_prob, axis=0, keepdims=True)
            grad_scores = (prob * (grad_prob - inner) * 0.125).astype(bf16)
            grad_query = dot(turned_ref[key_cols, :reach], grad_scores)
            out_ref[cols, rows] = grad_query.T.astype(bf16)
            key_sum[:reach] += dot(grad_scores, rows_in[cols, rows])
            value_sum[:reach] += dot(prob.astype(bf16), turned(grad))
        out_ref[:, key_cols] = key_sum[...].astype(bf16)
        out_ref[:, value_cols] = value_sum[...].astype(bf16)
    for k, ref in ((3, n3), (2, n2), (1, n1), (0, n0)):
        here = pl.ds(pl.multiple_of((at ^ k) * piece, piece), piece)
        ref[...] = dot_t(out_ref[here, :], w_ref[...]).astype(ref.dtype)
    gain, shift = columns_ref[:, 0:1], columns_ref[:, 2:3]
    rows = out_ref[...]
    row_sum = jnp.sum(rows.astype(f32), axis=0, keepdims=True)
    base = dot(hat_turned[...], rows)
    whole[:, 2 * group : 5 * group] = (gain * base + shift * row_sum).astype(bf16)
    out_grad = dot_t(turned(branch_ref[...]), att_ref[...]).astype(bf16)
    for place, k in ((0, 1), (1, 3), (5, 0), (6, 2)):
        whole[:, place * group : (place + 1) * group] = out_grad[:, k * group : (k + 1) * group]
    cut_rows(ordered, at_ref[1], whole, [ref.at[0] for ref in outs])
    weights = w_ref[...]
    products = (weights.astype(f32) * base).astype(bf16)
    first = dot_t(jnp.ones((8, 3 * group), bf16), products)[0:1]
    high = jnp.broadcast_to(row_sum, (8, 3 * group)).astype(bf16)
    low = (jnp.broadcast_to(row_sum, (8, 3 * group)) - high.astype(f32)).astype(bf16)
    second = (dot_t(high, weights) + dot_t(low, weights))[0:1]
    sum_ref[...] = jnp.zeros_like(sum_ref)
    sum_ref[0:1, :] = first
    sum_ref[1:2, :] = two_ref[0:1, :]
    sum_ref[2:3, :] = second
    sum_ref[3:6, :] = two_ref[1:4, :]
    z = at_ref[5]
    query = row_sum[:, :group]
    value = row_sum[:, 2 * group :]
    for k in range(4):
        row = slice(6 + k, 7 + k)
        sum_ref[row, :] = jnp.where(z == k, up_ref[0:1, :], jnp.where((z ^ 2) == k, up_ref[1:2, :], 0.0))
        row = slice(10 + k, 11 + k)
        sum_ref[row, :group] = jnp.where(at_ref[4] == k, query, 0.0)
        sum_ref[row, group : 2 * group] = jnp.where(at_ref[4] == k, value, 0.0)


def token_back(at_ref, n0, second_ref, near_ref, own_ref, params_ref, grad_ref, out_ref):
    piece = n0.shape[0]
    here = pl.ds(pl.multiple_of(at_ref[2] * piece, piece), piece)
    grad_normed = n0[...].astype(f32) + second_ref[...].astype(f32) + near_ref[...].astype(f32)
    hat, scale = normalized(own_ref[here, :].astype(f32))
    rows = grad_ref[...] + norm_back(hat, scale, params_ref[0:1, :], grad_normed)
    out_ref[...] = rows.astype(bf16)


def place_rows(at_ref, p0, p1, p2, p3, out_ref):
    for k, ref in enumerate((p0, p1, p2, p3)):
        out_ref[at_ref[0] ^ k] = ref[...].astype(out_ref.dtype)


def pick(v, index, axis):
    return lax.dynamic_index_in_dim(v, index, axis, keepdims=False)


def struct(shape, dtype=bf16):
    return jax.ShapeDtypeStruct(shape, dtype)


def call(body, name, scalars, arrays, outs, scratch=(), us=1):
    vmem = pl.BlockSpec(memory_space=pltpu.VMEM)
    specs = [vmem] * len(arrays)
    if scalars is not None:
        specs = [pl.BlockSpec(memory_space=pltpu.SMEM)] + specs
        arrays = (scalars,) + tuple(arrays)
    return pl.pallas_call(
        body, out_shape=outs, in_specs=specs, scratch_shapes=list(scratch), name=name,
        cost_estimate=pl.CostEstimate(flops=0, transcendentals=0, bytes_accessed=us * 3000000),
    )(*arrays)


def block(
    tokens,
    segments,
    ln_gains,
    ln_biases,
    w_qkv,
    bias_qv,
    w_out,
    out_biases,
    w_up,
    up_bias,
    w_down,
    cotangent,
    *,
    fsdp,
    ctx,
    tp,
):
    seq_count, half, width = tokens.shape
    part = w_up.shape[0]
    group = w_qkv.shape[2]
    head_count = group // HD
    hidden_part = w_up.shape[1]
    length = 2 * half
    piece = half // 2
    bias_rows, bias_cols = up_bias.shape
    assert ctx == 2 and seq_count == 2 and tp == 4
    f = lax.axis_index("fsdp")
    y = lax.axis_index("ctx")
    z = lax.axis_index("tp")
    seq = z >> 1
    member = z & 1
    same = seq == y
    at = 2 * y + member
    ordered = fsdp == 4
    scalars = jnp.stack([y, f, member, same.astype(jnp.int32), at, z]).astype(jnp.int32)

    def after(v, *others):
        return lax.optimization_barrier((v,) + others)[0]

    def swap_y(v):
        return swap(v, "ctx", 1, ctx)

    def swap_z(v, bit):
        return swap(v, "tp", bit, tp)

    def swap_yz(v, bit):
        pairs = [(a * tp + b, (1 - a) * tp + (b ^ bit)) for a in range(2) for b in range(tp)]
        return lax.ppermute(v, ("ctx", "tp"), pairs)

    def gather_parts(v, far=None):
        if not ordered:
            got = lax.all_gather(v, "fsdp", axis=0, tiled=False)
            return [got[i] for i in range(fsdp)]
        if far is None:
            far = swap(v, "fsdp", 2, fsdp)
        near = swap(v, "fsdp", 1, fsdp)
        cross = swap(far, "fsdp", 1, fsdp)
        return [v, near, far, cross]

    small_rows = 24
    pack = call(
        pack_small,
        "pack_small",
        None,
        (w_qkv, ln_gains, ln_biases, out_biases, up_bias, jnp.swapaxes(bias_qv, 0, 1)),
        struct((part + small_rows, 3 * group)),
        [pltpu.VMEM((small_rows, 3 * group), f32)],
    )
    pack_far = swap_z(pack, 2)
    out_turned = w_out.T
    out_near = swap_z(after(out_turned, pack), 1)
    tok_own = pick(after(tokens, out_near), seq, 0)
    seg_own = pick(after(segments, out_near), seq, 0)
    seg_row = jnp.pad(seg_own.astype(bf16), (0, width - half)).reshape(1, width)
    tok_low = swap_y(jnp.concatenate([tok_own[:piece], seg_row], axis=0))
    tok_high = swap_y(after(tok_own[piece:], tok_low))
    mlp_pack = jnp.concatenate([after(w_up, pack), w_down.T], axis=0)
    place = lax.broadcasted_iota(jnp.int32, pack.shape, 0)
    lane = lax.broadcasted_iota(jnp.int32, pack.shape, 1)
    turned_choice = (place >= part + 2) & (lane >= HD) & (lane < 2 * HD)
    chosen = jnp.where(turned_choice ^ same, pack, pack_far)
    packs = gather_parts(chosen)
    out_two = jnp.concatenate([out_turned, out_near], axis=1)
    out_far = swap_z(after(out_two, pack_far), 2)
    mlp_far = swap_z(after(mlp_pack, out_far, tok_low), 2)
    near_x = swap(after(mlp_pack, packs[2], out_far), "fsdp", 2, fsdp) if ordered else mlp_pack

    qkv_rows, qkv_turned, attended, logs, hat_turned, params, proj_rows = call(
        functools.partial(project, fsdp, ordered),
        "project",
        scalars,
        (tok_own, tok_low, tok_high, seg_own.reshape(1, half), *packs),
        (
            struct((length, 3 * group)),
            struct((3 * group, length)),
            struct((2, group, half)),
            struct((head_count + 1, length), f32),
            struct((width, length)),
            struct((8, width), f32),
            struct((width, 3 * group)),
        ),
        [pltpu.VMEM((1, 3 * group), f32)] + [pltpu.VMEM((length, width), bf16)] * 2,
        12,
    )

    att_here, att_there = pick(attended, y, 0), pick(attended, 1 - y, 0)
    attended, out_two, out_far = lax.optimization_barrier((attended, out_two, out_far, near_x))[:3]
    out_four = jnp.concatenate(
        [jnp.where(same, out_two, out_far), jnp.where(same, out_far, out_two)], axis=1
    )
    out_x = swap(out_four, "fsdp", 2, fsdp) if ordered else None
    att_y, att_yz, att_z = swap_y(att_there), swap_yz(att_there, 1), swap_z(att_here, 1)
    if ordered:
        out_four, out_x, near_own, near_x = lax.optimization_barrier(
            (out_four, out_x, mlp_pack, near_x, att_z, att_y, att_yz)
        )[:4]
    else:
        near_own = mlp_pack
    out_parts = gather_parts(out_four, out_x)
    near_parts = gather_parts(near_own, near_x)
    hidden, normed_two, att_own, out_proj = call(
        functools.partial(out_project, fsdp, ordered),
        "out_project",
        scalars,
        (attended, att_z, att_y, att_yz, tok_own, params, *out_parts),
        (
            struct((half, width), f32),
            struct((half, width)),
            struct((4 * group, piece)),
            struct((width, 4 * group)),
        ),
        [pltpu.VMEM((4 * group, half), bf16)],
        4,
    )

    cot = pick(cotangent, seq, 0)
    rows_f, rows_b = struct((half, width), f32), struct((half, hidden_part))
    rate_f, square = struct((half, hidden_part), f32), struct((width, hidden_part))
    half_b = struct((piece, width))
    act_one, rate_one, up_one, down_one, down_sum = call(
        functools.partial(feed_near, fsdp, ordered),
        "feed_near",
        scalars,
        (normed_two, params, *near_parts),
        (rows_b, rate_f, square, square, rows_f),
        us=4,
    )
    if ordered:
        far_x = swap(after(mlp_far, att_z, att_y, att_yz), "fsdp", 2, fsdp)
        far_own, far_x = lax.optimization_barrier((mlp_far, far_x, act_one))[:2]
        far_parts = gather_parts(far_own, far_x)
    else:
        far_parts = gather_parts(mlp_far)
    piece_f, sum_f = struct((piece, width), f32), struct((8, hidden_part), f32)
    act_two, pre_one, pre_two, back, back_send, down_own, down_send, up_sums = call(
        functools.partial(feed_far, fsdp, ordered),
        "feed_far",
        scalars,
        (normed_two, cot, params, rate_one, up_one, down_one, down_sum, *far_parts),
        (rows_b, rows_b, rows_b, piece_f, half_b, piece_f, half_b, sum_f),
        [pltpu.VMEM((width, hidden_part), bf16)] * 2,
        us=9,
    )
    back_got = swap_z(back_send, 1)
    cut = (2, part) if ordered else (width,)
    grad_outs = [struct((4,) + cut + (hidden_part,))] * (2 if ordered else 1)
    mlp_grads = call(
        functools.partial(feed_grads, ordered),
        "feed_grads",
        scalars,
        (normed_two, cot, act_one, pre_one, act_two, pre_two),
        tuple(grad_outs),
        [pltpu.VMEM((width, hidden_part), bf16)],
        us=8,
    )

    def scatter(parts, name, count, gate, later):
        if not ordered:
            v = lax.psum_scatter(parts[0], "fsdp", scatter_dimension=1, tiled=True)
            each = v.shape[0] // count
            zeros = [jnp.zeros_like(v[:each])] * count
            return v.astype(f32), zeros, zeros[-1:]
        kept, sent = parts
        got = swap(after(sent, *gate), "fsdp", 1, fsdp)
        shape = kept.shape[:1] + kept.shape[2:]
        each = (shape[0] // count,) + shape[1:]
        kept, *sent = call(
            core_sum, name, scalars, (after(kept, later), got), (struct(shape, f32), *[struct(each)] * count), us=2
        )
        return kept, sent, [swap_x(v) for v in sent[-1:]]

    def swap_x(v, *gate):
        return swap(after(v, *gate), "fsdp", 2, fsdp) if ordered else v

    def mine(v):
        return pick(v.reshape((2, piece) + v.shape[1:]), member, 0)

    def spread(rows, dtype, gate=()):
        far = swap_z(rows, 2)
        near = swap_z(rows, 1)
        cross = swap_z(after(far, near, *gate), 1)

        def placed(name, *others):
            parts = (after(rows, *others), near, far, cross)
            return call(
                place_rows, name, z.reshape(1), parts, struct((tp, piece, width), dtype)
            ).reshape(seq_count, half, width)

        return placed, (near, far), cross

    grad_hidden, grad_branch, g0, g1, g2, g3, sums_two = call(
        branch_back,
        "branch_back",
        scalars,
        (back, back_got, hidden, cot, out_proj, params),
        (
            struct((piece, width), f32),
            struct((piece, width)),
            *[struct((group, piece))] * 4,
            struct((8, width), f32),
        ),
    )
    down_got = swap_z(after(down_send, g0), 1)
    g_y, g_yz, g_z = swap_y(g2), swap_yz(g3, 1), swap_z(g1, 1)
    grads_kept, grads_sent, (far_x,) = scatter(mlp_grads, "core_sum_feed", 2, (g0,), g_y)
    result_rows = (mine(hidden) + down_own + down_got.astype(f32) + params[5:6]).astype(bf16)
    result_rows = after(result_rows, g_y, g_yz, g_z)
    place_result, result_gate, result_cross = spread(result_rows, bf16)
    late_outs = [struct((1,) + cut + (7 * group,))] * (2 if ordered else 1)
    n0, n1, n2, n3, sums, *late = call(
        functools.partial(attention_backward, ordered),
        "attention_backward",
        scalars,
        (
            qkv_rows, qkv_turned, after(g0, result_rows, *grads_sent), g_z, g_y, g_yz, logs, proj_rows,
            hat_turned, params.T, grad_branch, att_own, sums_two, up_sums,
        ),
        (*[struct((piece, width))] * 4, struct((16, width), f32), *late_outs),
        [
            pltpu.VMEM((length, 3 * group), bf16),
            pltpu.VMEM((width, 7 * group), bf16),
            pltpu.VMEM((length, HD), f32),
            pltpu.VMEM((length, HD), f32),
        ],
        us=16,
    )
    first_got = swap_y(after(n3, *result_gate, far_x))
    late_kept, late_sent, _ = scatter(
        late, "core_sum_late", 1, (*result_gate, far_x), first_got
    )
    late_first = late_sent[0]
    halves = (struct((part, hidden_part)), struct((part, hidden_part), f32))
    far_sent, far_kept = call(
        functools.partial(x_sum, 1),
        "x_sum_far",
        scalars,
        (after(grads_kept, first_got), far_x),
        halves,
    )
    share = n1.astype(f32) + first_got.astype(f32)
    near_got = swap_z(after(share.astype(bf16), result_cross), 1)
    second_got = swap_y(after(n2, first_got))
    token_rows = call(
        token_back,
        "token_back",
        scalars,
        (after(n0, late_first, far_sent), second_got, near_got, tok_own, params, grad_hidden),
        struct((piece, width)),
        us=3,
    )
    far_got = swap_y(after(far_sent, second_got))
    late_got = swap_x(late_sent[0], first_got)
    near_x_got = swap_x(grads_sent[0], second_got)
    far_far = swap_z(after((far_kept + far_got.astype(f32)).astype(bf16), token_rows), 2)
    place_tokens, token_gate, token_cross = spread(
        token_rows, f32, (late_got, far_far)
    )
    sums = after(sums, *token_gate, far_got, near_x_got)
    sums = sums + swap_y(sums)
    if ordered:
        sums = sums + swap(sums, "fsdp", 1, fsdp)
        sums = sums + swap(sums, "fsdp", 2, fsdp)
    else:
        sums = lax.psum(sums, "fsdp")
    near_sent, near_kept = call(
        functools.partial(x_sum, 0),
        "x_sum_near",
        scalars,
        (after(grads_kept, *token_gate), near_x_got),
        halves,
    )
    half_got = swap_y(after(near_sent, near_got))
    half_grad = (near_kept + half_got.astype(f32) + far_far.astype(f32)).astype(bf16)
    rest_grad = swap_y(half_grad)
    grad_up = jnp.where(y == 0, half_grad, rest_grad).astype(f32)
    grad_down = jnp.where(y == 0, rest_grad, half_grad).astype(f32).T

    late = late_kept[0] + late_got[0].astype(f32)
    out_got = swap_z(after(late[:, : 2 * group].astype(bf16), *token_gate), 1).astype(f32)
    grad_qkv = late[:, 2 * group : 5 * group].astype(bf16)
    out_first = late[:, 5 * group : 6 * group] + out_got[:, :group]
    out_second = late[:, 6 * group :] + out_got[:, group:]
    out_here = jnp.where(same, out_first, out_second).astype(bf16)
    out_there = jnp.where(same, out_second, out_first).astype(bf16)
    kept = jnp.concatenate([grad_qkv, out_here], axis=1).astype(f32)
    both = (
        kept + swap_z(jnp.concatenate([grad_qkv, out_there], axis=1), 2).astype(f32)
    ).astype(bf16)
    both_got = swap_y(both)
    result = place_result("place_result", token_rows)
    grad_tokens = place_tokens("place_tokens", both)
    grad_qkv = jnp.where(same, both, both_got)[:, : 3 * group].astype(f32)
    grad_qkv = jnp.moveaxis(grad_qkv.reshape(part, 3, group), 1, 0)
    grad_out = (both[:, 3 * group :].astype(f32) + both_got[:, 3 * group :].astype(f32)).T

    sums = after(sums, out_got, token_cross)
    sums = sums + swap_z(sums, 1)
    sums = sums + swap_z(sums, 2)
    norm_sums = pick(sums[:6].reshape(6, fsdp, part), f, 1)
    up_total = pick(sums[6 : 6 + tp], z, 0)
    grad_up_bias = pick(up_total.reshape(bias_rows, fsdp, bias_cols), f, 1)
    qv_total = pick(sums[6 + tp : 6 + 2 * tp, : 2 * group], z, 0)
    grad_qv = pick(qv_total.reshape(2, head_count, fsdp, bias_cols), f, 2)
    return (
        result,
        grad_tokens,
        norm_sums[0:2],
        norm_sums[2:4],
        grad_qkv,
        grad_qv,
        grad_out,
        norm_sums[4:6],
        grad_up,
        grad_up_bias,
        grad_down,
    )


def solution(mesh):
    in_specs = (
        P("fsdp", "ctx", None),
        P("fsdp", "ctx"),
        P(None, "fsdp"),
        P(None, "fsdp"),
        P(None, "fsdp", "tp"),
        P(None, "tp", "fsdp"),
        P("tp", "fsdp"),
        P(None, "fsdp"),
        P("fsdp", "tp"),
        P("tp", "fsdp"),
        P("tp", "fsdp"),
        P("fsdp", "ctx", None),
    )
    out_specs = (
        P("fsdp", "ctx", None),
        P("fsdp", "ctx", None),
        P(None, "fsdp"),
        P(None, "fsdp"),
        P(None, "fsdp", "tp"),
        P(None, "tp", "fsdp"),
        P("tp", "fsdp"),
        P(None, "fsdp"),
        P("fsdp", "tp"),
        P("tp", "fsdp"),
        P("tp", "fsdp"),
    )
    local = functools.partial(
        block, fsdp=mesh.shape["fsdp"], ctx=mesh.shape["ctx"], tp=mesh.shape["tp"]
    )
    return jax.shard_map(local, mesh=mesh, in_specs=in_specs, out_specs=out_specs, check_vma=False)
```

```python
import functools
import math

import jax
import jax.numpy as jnp
from jax import lax
from jax.experimental import pallas as pl
from jax.experimental.pallas import tpu as pltpu
from jax.sharding import PartitionSpec as P

HD = 64
QB = 256
eps = 1e-05
masked_score = -1e30
score_scale = 0.125 * math.log2(math.e)
f32 = jnp.float32
bf16 = jnp.bfloat16


def swap(v, axis, bit, size):
    return lax.ppermute(v, axis, [(i, i ^ bit) for i in range(size)])


def dot(a, b):
    return lax.dot_general(a, b, (((1,), (0,)), ((), ())), preferred_element_type=f32)


def turned(v):
    return v.astype(f32).T.astype(v.dtype)


def starts_of(seg):
    start = jnp.zeros(seg.shape, jnp.int32)
    for number in range(3):
        count = jnp.sum((seg == number).astype(jnp.int32), axis=1, keepdims=True)
        start = start + jnp.where(seg > number, count, 0)
    return start


def allowed_block(start, first, width):
    place = lax.broadcasted_iota(jnp.int32, (width, QB), 0)
    allowed = place >= start[:, first : first + QB]
    query = lax.broadcasted_iota(jnp.int32, (width, QB), 1) + first
    return allowed & (place <= query)


def dot_t(a, b):
    return lax.dot_general(a, b, (((1,), (1,)), ((), ())), preferred_element_type=f32)


def normalized(v):
    mean = jnp.mean(v, axis=-1, keepdims=True)
    centered = v - mean
    scale = lax.rsqrt(jnp.mean(centered * centered, axis=-1, keepdims=True) + eps)
    return centered * scale, scale


def norm_back(hat, scale, gain, grad):
    scaled = grad * gain
    first = jnp.mean(scaled, axis=-1, keepdims=True)
    second = jnp.mean(scaled * hat, axis=-1, keepdims=True)
    return scale * (scaled - first - hat * second)


def gelu_pair(u):
    slope = math.sqrt(2 / math.pi)
    bent = jnp.tanh(slope * (u + 0.044715 * u * u * u))
    value = 0.5 * u * (1 + bent)
    rate = 0.5 * (1 + bent) + 0.5 * u * (1 - bent * bent) * slope * (1 + 3 * 0.044715 * u * u)
    return value, rate


def chosen_part(refs, number, index, f):
    if f is None:
        return refs[number][index]
    place = number ^ f
    value = refs[0][index]
    for k in range(1, len(refs)):
        value = jnp.where(place == k, refs[k][index], value)
    return value


def pack_small(w_ref, gains_ref, biases_ref, out_ref_in, up_ref, qv_ref, pack_ref, rows_ref):
    part = w_ref.shape[1]
    width = w_ref.shape[2]
    for c in range(3):
        pack_ref[:part, c * width : (c + 1) * width] = w_ref[c]
    rows_ref[...] = jnp.zeros_like(rows_ref)
    for k, ref in enumerate((gains_ref, biases_ref, out_ref_in)):
        rows_ref[0:2, k * width : k * width + part] = ref[...].astype(f32)
    up_rows, cols = up_ref.shape
    heads = qv_ref.shape[0]
    for lane in (0, HD):
        rows_ref[2 : 2 + up_rows, lane : lane + cols] = up_ref[...].astype(f32)
    for i in range(2):
        low = 2 + up_rows + i * heads
        rows_ref[low : low + heads, 0:cols] = qv_ref[:, i, :].astype(f32)
    pack_ref[part:, :] = rows_ref[...].astype(bf16)


def project(n, ordered, at_ref, own_ref, low_ref, high_ref, seg_ref, *refs):
    packs = refs[:n]
    rows_ref, turned_ref, att_ref, log_ref, hat_turned, params_ref, w_ref, qv_row, normed_ref, hat_ref = refs[n:]
    y = at_ref[0]
    f = at_ref[1] if ordered else None
    half = own_ref.shape[0]
    length = 2 * half
    width = own_ref.shape[1]
    part = width // n
    columns = w_ref.shape[1]
    group = columns // 3
    heads = group // HD
    small_rows = packs[0].shape[0] - part
    cols = HD // n
    up_rows = width // HD
    params_ref[...] = jnp.zeros_like(params_ref)
    qv_row[...] = jnp.zeros_like(qv_row)
    for p in range(n):
        w_ref[p * part : (p + 1) * part, :] = chosen_part(packs, p, (slice(0, part), slice(None)), f)
        small = chosen_part(packs, p, (slice(part, part + small_rows), slice(None)), f).astype(f32)
        for k in range(3):
            params_ref[2 * k : 2 * k + 2, p * part : (p + 1) * part] = small[
                0:2, k * group : k * group + part
            ]
        for r in range(up_rows):
            low = r * HD + p * cols
            params_ref[6:7, low : low + cols] = small[2 + r : 3 + r, 0:cols]
            params_ref[7:8, low : low + cols] = small[2 + r : 3 + r, HD : HD + cols]
        for i in range(2):
            for h in range(heads):
                low = 2 * i * group + h * HD + p * cols
                r = 2 + up_rows + i * heads + h
                qv_row[0:1, low : low + cols] = small[r : r + 1, 0:cols]
    gain = params_ref[0:1, :]
    shift = params_ref[2:3, :]
    middle = half // 2
    for rows, place in (
        (own_ref[:middle, :], 2 * y),
        (own_ref[middle:, :], 2 * y + 1),
        (low_ref[:middle, :], 2 - 2 * y),
        (high_ref[...], 3 - 2 * y),
    ):
        hat, _ = normalized(rows.astype(f32))
        here = pl.ds(pl.multiple_of(place * middle, middle), middle)
        hat_ref[here, :] = hat.astype(bf16)
        normed_ref[here, :] = (hat * gain + shift).astype(bf16)
    got_row = low_ref[middle : middle + 1, 0:half].astype(f32).astype(jnp.int32)
    own_row = seg_ref[...]
    first = y == 0
    seg = jnp.concatenate(
        [jnp.where(first, own_row, got_row), jnp.where(first, got_row, own_row)], axis=1
    )
    for low in range(0, length, QB):
        rows = slice(low, low + QB)
        block_rows = (dot(normed_ref[rows, :], w_ref[...]) + qv_row[...]).astype(bf16)
        hat_turned[:, rows] = turned(hat_ref[rows, :])
        rows_ref[rows, :] = block_rows
        turned_ref[:, rows] = turned(block_rows)
    start = starts_of(seg)
    for head in range(heads):
        rows = slice(head * HD, (head + 1) * HD)
        keys = rows_ref[:, group + head * HD : group + (head + 1) * HD]
        for low in range(0, length, QB):
            reach = low + QB
            at_cols = slice(low, reach)
            scores = dot(keys[:reach], turned_ref[rows, at_cols]) * score_scale
            scores = jnp.where(allowed_block(start, low, reach), scores, masked_score)
            top = jnp.max(scores, axis=0, keepdims=True)
            weight = jnp.exp2(scores - top)
            total = jnp.sum(weight, axis=0, keepdims=True)
            mixed = dot(
                turned_ref[2 * group + head * HD : 2 * group + (head + 1) * HD, :reach],
                weight.astype(bf16),
            )
            inside = low % half
            att_ref[low // half, rows, inside : inside + QB] = (mixed / total).astype(bf16)
            log_ref[head : head + 1, at_cols] = top + jnp.log2(total)
    log_ref[heads : heads + 1, :] = start.astype(f32)


def out_project(n, ordered, at_ref, att_ref, z_ref, y_ref, yz_ref, own_ref, params_ref, *refs):
    parts = refs[:n]
    hidden_ref, normed_ref, att_own_ref, out_ref, att_all = refs[n:]
    y, member = at_ref[0], at_ref[2]
    f = at_ref[1] if ordered else None
    group = z_ref.shape[0]
    half, width = own_ref.shape
    part = width // n
    att_all[0:group, :] = att_ref[y]
    for k, ref in enumerate((z_ref, y_ref, yz_ref)):
        att_all[(k + 1) * group : (k + 2) * group, :] = ref[...]
    for p in range(n):
        out_ref[p * part : (p + 1) * part, :] = chosen_part(parts, p, (slice(None), slice(None)), f)
    everything = att_all[...]
    att_own_ref[...] = jnp.where(member == 0, everything[:, : half // 2], everything[:, half // 2 :])
    for low in range(0, half, QB):
        rows = slice(low, low + QB)
        branch = dot_t(turned(everything[:, rows]), out_ref[...])
        hidden = own_ref[rows, :].astype(f32) + branch + params_ref[4:5, :]
        hidden_ref[rows, :] = hidden
        hat, _ = normalized(hidden)
        normed_ref[rows, :] = (hat * params_ref[1:2, :] + params_ref[3:4, :]).astype(bf16)


def feed_near(n, ordered, at_ref, normed_ref, params_ref, *refs):
    parts = refs[:n]
    act_ref, rate_ref, up_all, down_all, down_ref = refs[n:]
    f = at_ref[1] if ordered else None
    half, width = normed_ref.shape
    arrange(parts, f, up_all, down_all)
    shift = jnp.where(at_ref[3] == 1, params_ref[6:7, :], params_ref[7:8, :])
    for low in range(0, half, QB):
        rows = slice(low, low + QB)
        value, rate = gelu_pair(dot(normed_ref[rows, :], up_all[...]) + shift)
        act = value.astype(bf16)
        act_ref[rows, :] = act
        rate_ref[rows, :] = rate
        down_ref[rows, :] = dot_t(act, down_all[...])


def arrange(parts, f, up_all, down_all):
    part = parts[0].shape[0] // 2
    for p in range(len(parts)):
        here = slice(p * part, (p + 1) * part)
        up_all[here, :] = chosen_part(parts, p, (slice(0, part), slice(None)), f)
        down_all[here, :] = chosen_part(parts, p, (slice(part, 2 * part), slice(None)), f)


def feed_far(n, ordered, at_ref, normed_ref, cot_ref, params_ref, rate_one, up_one, down_one, down_in, *refs):
    parts = refs[:n]
    act_two, pre_one, pre_two, back_ref, back_send, down_ref, down_send, sum_ref, up_two, down_two = refs[n:]
    f = at_ref[1] if ordered else None
    member = at_ref[2]
    piece = normed_ref.shape[0] // 2
    arrange(parts, f, up_two, down_two)
    shift = jnp.where(at_ref[3] == 0, params_ref[6:7, :], params_ref[7:8, :])
    sum_ref[...] = jnp.zeros_like(sum_ref)
    for owner, back_out, down_out in ((1 - member, back_send, down_send), (member, back_ref, down_ref)):
        rows = pl.ds(pl.multiple_of(owner * piece, piece), piece)
        value, rate = gelu_pair(dot(normed_ref[rows, :], up_two[...]) + shift)
        act = value.astype(bf16)
        act_two[rows, :] = act
        down_out[...] = (down_in[rows, :] + dot_t(act, down_two[...])).astype(down_out.dtype)
        cot = cot_ref[rows, :]
        back = jnp.zeros((piece, back_ref.shape[1]), f32)
        for k, (slope, up, down, pre) in enumerate(
            ((rate_one[rows, :], up_one, down_one, pre_one), (rate, up_two, down_two, pre_two))
        ):
            grad_act = dot(cot, down[...]).astype(bf16)
            grad = (grad_act.astype(f32) * slope).astype(bf16)
            pre[rows, :] = grad
            sum_ref[k : k + 1, :] += jnp.sum(grad.astype(f32), axis=0, keepdims=True)
            back = back + dot_t(grad, up[...])
        back_out[...] = back.astype(back_out.dtype)


def feed_grads(ordered, at_ref, normed_ref, cot_ref, act_one, pre_one, act_two, pre_two, *refs):
    outs, whole = refs[:-1], refs[-1]
    normed_turned = turned(normed_ref[...])
    cot_turned = turned(cot_ref[...])
    for k, (act, pre) in enumerate(((act_one, pre_one), (act_two, pre_two))):
        for side, (left, right) in enumerate(((normed_turned, pre), (cot_turned, act))):
            whole[...] = dot(left, right[...]).astype(bf16)
            cut_rows(ordered, at_ref[1], whole, [ref.at[2 * k + side] for ref in outs])


def cut_rows(ordered, f, whole, outs):
    if not ordered:
        outs[0][...] = whole[...]
        return
    part = whole.shape[0] // 4
    for ref, core in zip(outs, (f & 1, 1 - (f & 1))):
        for x in range(2):
            ref[x] = whole[pl.ds(pl.multiple_of((2 * x + core) * part, part), part), :]


def core_sum(at_ref, kept_ref, got_ref, own_ref, *sends):
    x = at_ref[1] >> 1
    count = kept_ref.shape[0]
    each = count // len(sends)
    for k in range(count):
        own_ref[k] = kept_ref[k, x].astype(f32) + got_ref[k, x].astype(f32)
        sends[k // each][k % each] = (
            kept_ref[k, 1 - x].astype(f32) + got_ref[k, 1 - x].astype(f32)
        ).astype(bf16)


def x_sum(k, at_ref, own_ref, *refs):
    for side in range(2):
        total = own_ref[2 * k + side]
        for ref in refs[:-1]:
            total = total + ref[side].astype(f32)
        refs[-1][side] = total.astype(bf16)


def branch_back(
    at_ref, back_ref, got_ref, hidden_ref, cot_ref, out_ref, params_ref,
    grad_ref, branch_ref, g0, g1, g2, g3, sum_ref,
):
    piece = got_ref.shape[0]
    group = g0.shape[0]
    here = pl.ds(pl.multiple_of(at_ref[2] * piece, piece), piece)
    grad_two = back_ref[...] + got_ref[...].astype(f32)
    hat, scale = normalized(hidden_ref[here, :])
    cot = cot_ref[here, :].astype(f32)
    grad = cot + norm_back(hat, scale, params_ref[1:2, :], grad_two)
    grad_ref[...] = grad
    low = grad.astype(bf16)
    branch_ref[...] = low
    for k, ref in enumerate((g0, g1, g2, g3)):
        ref[...] = turned(dot(low, out_ref[:, k * group : (k + 1) * group]).astype(bf16))
    sum_ref[...] = jnp.zeros_like(sum_ref)
    sum_ref[0:1, :] = jnp.sum(grad_two * hat, axis=0, keepdims=True)
    sum_ref[1:2, :] = jnp.sum(grad_two, axis=0, keepdims=True)
    sum_ref[2:3, :] = jnp.sum(low.astype(f32), axis=0, keepdims=True)
    sum_ref[3:4, :] = jnp.sum(cot, axis=0, keepdims=True)


def attention_backward(
    ordered, at_ref, rows_in, turned_ref, g0, g1, g2, g3, log_ref, w_ref,
    hat_turned, columns_ref, branch_ref, att_ref, two_ref, up_ref, n0, n1, n2, n3, sum_ref, *refs
):
    outs, (out_ref, whole, key_sum, value_sum) = refs[:-4], refs[-4:]
    at = at_ref[4]
    length = rows_in.shape[0]
    group = turned_ref.shape[0] // 3
    heads = group // HD
    piece = n0.shape[0]
    start = log_ref[heads : heads + 1, :].astype(jnp.int32)
    for head in range(heads):
        rows = slice(head * HD, (head + 1) * HD)
        key_cols = slice(group + head * HD, group + (head + 1) * HD)
        value_cols = slice(2 * group + head * HD, 2 * group + (head + 1) * HD)
        keys = rows_in[:, key_cols]
        values = rows_in[:, value_cols]
        key_sum[...] = jnp.zeros_like(key_sum)
        value_sum[...] = jnp.zeros_like(value_sum)
        for low in range(0, length, QB):
            reach = low + QB
            cols = slice(low, reach)
            place = at ^ (low // QB)
            grad = g0[rows, :]
            for k, ref in ((1, g1), (2, g2), (3, g3)):
                grad = jnp.where(place == k, ref[rows, :], grad)
            scores = dot(keys[:reach], turned_ref[rows, cols]) * score_scale
            prob = jnp.exp2(scores - log_ref[head : head + 1, cols])
            prob = jnp.where(allowed_block(start, low, reach), prob, 0.0)
            grad_prob = dot(values[:reach], grad)
            inner = jnp.sum(prob * grad_prob, axis=0, keepdims=True)
            grad_scores = (prob * (grad_prob - inner) * 0.125).astype(bf16)
            grad_query = dot(turned_ref[key_cols, :reach], grad_scores)
            out_ref[cols, rows] = grad_query.T.astype(bf16)
            key_sum[:reach] += dot(grad_scores, rows_in[cols, rows])
            value_sum[:reach] += dot(prob.astype(bf16), turned(grad))
        out_ref[:, key_cols] = key_sum[...].astype(bf16)
        out_ref[:, value_cols] = value_sum[...].astype(bf16)
    for k, ref in ((3, n3), (2, n2), (1, n1), (0, n0)):
        here = pl.ds(pl.multiple_of((at ^ k) * piece, piece), piece)
        ref[...] = dot_t(out_ref[here, :], w_ref[...]).astype(ref.dtype)
    gain, shift = columns_ref[:, 0:1], columns_ref[:, 2:3]
    rows = out_ref[...]
    row_sum = jnp.sum(rows.astype(f32), axis=0, keepdims=True)
    base = dot(hat_turned[...], rows)
    whole[:, 2 * group : 5 * group] = (gain * base + shift * row_sum).astype(bf16)
    out_grad = dot_t(turned(branch_ref[...]), att_ref[...]).astype(bf16)
    for place, k in ((0, 1), (1, 3), (5, 0), (6, 2)):
        whole[:, place * group : (place + 1) * group] = out_grad[:, k * group : (k + 1) * group]
    cut_rows(ordered, at_ref[1], whole, [ref.at[0] for ref in outs])
    weights = w_ref[...]
    products = (weights.astype(f32) * base).astype(bf16)
    first = dot_t(jnp.ones((8, 3 * group), bf16), products)[0:1]
    high = jnp.broadcast_to(row_sum, (8, 3 * group)).astype(bf16)
    low = (jnp.broadcast_to(row_sum, (8, 3 * group)) - high.astype(f32)).astype(bf16)
    second = (dot_t(high, weights) + dot_t(low, weights))[0:1]
    sum_ref[...] = jnp.zeros_like(sum_ref)
    sum_ref[0:1, :] = first
    sum_ref[1:2, :] = two_ref[0:1, :]
    sum_ref[2:3, :] = second
    sum_ref[3:6, :] = two_ref[1:4, :]
    z = at_ref[5]
    query = row_sum[:, :group]
    value = row_sum[:, 2 * group :]
    for k in range(4):
        row = slice(6 + k, 7 + k)
        sum_ref[row, :] = jnp.where(z == k, up_ref[0:1, :], jnp.where((z ^ 2) == k, up_ref[1:2, :], 0.0))
        row = slice(10 + k, 11 + k)
        sum_ref[row, :group] = jnp.where(at_ref[4] == k, query, 0.0)
        sum_ref[row, group : 2 * group] = jnp.where(at_ref[4] == k, value, 0.0)


def token_back(at_ref, n0, second_ref, near_ref, own_ref, params_ref, grad_ref, out_ref):
    piece = n0.shape[0]
    here = pl.ds(pl.multiple_of(at_ref[2] * piece, piece), piece)
    grad_normed = n0[...].astype(f32) + second_ref[...].astype(f32) + near_ref[...].astype(f32)
    hat, scale = normalized(own_ref[here, :].astype(f32))
    rows = grad_ref[...] + norm_back(hat, scale, params_ref[0:1, :], grad_normed)
    out_ref[...] = rows.astype(bf16)


def place_rows(at_ref, p0, p1, p2, p3, out_ref):
    for k, ref in enumerate((p0, p1, p2, p3)):
        out_ref[at_ref[0] ^ k] = ref[...].astype(out_ref.dtype)


def pick(v, index, axis):
    return lax.dynamic_index_in_dim(v, index, axis, keepdims=False)


def struct(shape, dtype=bf16):
    return jax.ShapeDtypeStruct(shape, dtype)


def call(body, name, scalars, arrays, outs, scratch=(), us=1):
    vmem = pl.BlockSpec(memory_space=pltpu.VMEM)
    specs = [vmem] * len(arrays)
    if scalars is not None:
        specs = [pl.BlockSpec(memory_space=pltpu.SMEM)] + specs
        arrays = (scalars,) + tuple(arrays)
    return pl.pallas_call(
        body, out_shape=outs, in_specs=specs, scratch_shapes=list(scratch), name=name,
        cost_estimate=pl.CostEstimate(flops=0, transcendentals=0, bytes_accessed=us * 3000000),
    )(*arrays)


def block(
    tokens,
    segments,
    ln_gains,
    ln_biases,
    w_qkv,
    bias_qv,
    w_out,
    out_biases,
    w_up,
    up_bias,
    w_down,
    cotangent,
    *,
    fsdp,
    ctx,
    tp,
):
    seq_count, half, width = tokens.shape
    part = w_up.shape[0]
    group = w_qkv.shape[2]
    head_count = group // HD
    hidden_part = w_up.shape[1]
    length = 2 * half
    piece = half // 2
    bias_rows, bias_cols = up_bias.shape
    assert ctx == 2 and seq_count == 2 and tp == 4
    f = lax.axis_index("fsdp")
    y = lax.axis_index("ctx")
    z = lax.axis_index("tp")
    seq = z >> 1
    member = z & 1
    same = seq == y
    at = 2 * y + member
    ordered = fsdp == 4
    scalars = jnp.stack([y, f, member, same.astype(jnp.int32), at, z]).astype(jnp.int32)

    def after(v, *others):
        return lax.optimization_barrier((v,) + others)[0]

    def swap_y(v):
        return swap(v, "ctx", 1, ctx)

    def swap_z(v, bit):
        return swap(v, "tp", bit, tp)

    def swap_yz(v, bit):
        pairs = [(a * tp + b, (1 - a) * tp + (b ^ bit)) for a in range(2) for b in range(tp)]
        return lax.ppermute(v, ("ctx", "tp"), pairs)

    def gather_parts(v, far=None):
        if not ordered:
            got = lax.all_gather(v, "fsdp", axis=0, tiled=False)
            return [got[i] for i in range(fsdp)]
        if far is None:
            far = swap(v, "fsdp", 2, fsdp)
        near = swap(v, "fsdp", 1, fsdp)
        cross = swap(far, "fsdp", 1, fsdp)
        return [v, near, far, cross]

    small_rows = 24
    pack = call(
        pack_small,
        "pack_small",
        None,
        (w_qkv, ln_gains, ln_biases, out_biases, up_bias, jnp.swapaxes(bias_qv, 0, 1)),
        struct((part + small_rows, 3 * group)),
        [pltpu.VMEM((small_rows, 3 * group), f32)],
    )
    pack_far = swap_z(pack, 2)
    out_turned = w_out.T
    out_near = swap_z(after(out_turned, pack), 1)
    tok_own = pick(after(tokens, out_near), seq, 0)
    seg_own = pick(after(segments, out_near), seq, 0)
    seg_row = jnp.pad(seg_own.astype(bf16), (0, width - half)).reshape(1, width)
    tok_low = swap_y(jnp.concatenate([tok_own[:piece], seg_row], axis=0))
    tok_high = swap_y(after(tok_own[piece:], tok_low))
    mlp_pack = jnp.concatenate([after(w_up, pack), w_down.T], axis=0)
    place = lax.broadcasted_iota(jnp.int32, pack.shape, 0)
    lane = lax.broadcasted_iota(jnp.int32, pack.shape, 1)
    turned_choice = (place >= part + 2) & (lane >= HD) & (lane < 2 * HD)
    chosen = jnp.where(turned_choice ^ same, pack, pack_far)
    packs = gather_parts(chosen)
    out_two = jnp.concatenate([out_turned, out_near], axis=1)
    out_far = swap_z(after(out_two, pack_far), 2)
    mlp_far = swap_z(after(mlp_pack, out_far, tok_low), 2)
    near_x = swap(after(mlp_pack, packs[2], out_far), "fsdp", 2, fsdp) if ordered else mlp_pack

    qkv_rows, qkv_turned, attended, logs, hat_turned, params, proj_rows = call(
        functools.partial(project, fsdp, ordered),
        "project",
        scalars,
        (tok_own, tok_low, tok_high, seg_own.reshape(1, half), *packs),
        (
            struct((length, 3 * group)),
            struct((3 * group, length)),
            struct((2, group, half)),
            struct((head_count + 1, length), f32),
            struct((width, length)),
            struct((8, width), f32),
            struct((width, 3 * group)),
        ),
        [pltpu.VMEM((1, 3 * group), f32)] + [pltpu.VMEM((length, width), bf16)] * 2,
        12,
    )

    att_here, att_there = pick(attended, y, 0), pick(attended, 1 - y, 0)
    attended, out_two, out_far = lax.optimization_barrier((attended, out_two, out_far, near_x))[:3]
    out_four = jnp.concatenate(
        [jnp.where(same, out_two, out_far), jnp.where(same, out_far, out_two)], axis=1
    )
    out_x = swap(out_four, "fsdp", 2, fsdp) if ordered else None
    att_y, att_yz, att_z = swap_y(att_there), swap_yz(att_there, 1), swap_z(att_here, 1)
    if ordered:
        out_four, out_x, near_own, near_x = lax.optimization_barrier(
            (out_four, out_x, mlp_pack, near_x, att_z, att_y, att_yz)
        )[:4]
    else:
        near_own = mlp_pack
    out_parts = gather_parts(out_four, out_x)
    near_parts = gather_parts(near_own, near_x)
    hidden, normed_two, att_own, out_proj = call(
        functools.partial(out_project, fsdp, ordered),
        "out_project",
        scalars,
        (attended, att_z, att_y, att_yz, tok_own, params, *out_parts),
        (
            struct((half, width), f32),
            struct((half, width)),
            struct((4 * group, piece)),
            struct((width, 4 * group)),
        ),
        [pltpu.VMEM((4 * group, half), bf16)],
        4,
    )

    cot = pick(cotangent, seq, 0)
    rows_f, rows_b = struct((half, width), f32), struct((half, hidden_part))
    rate_f, square = struct((half, hidden_part), f32), struct((width, hidden_part))
    half_b = struct((piece, width))
    act_one, rate_one, up_one, down_one, down_sum = call(
        functools.partial(feed_near, fsdp, ordered),
        "feed_near",
        scalars,
        (normed_two, params, *near_parts),
        (rows_b, rate_f, square, square, rows_f),
        us=4,
    )
    if ordered:
        far_x = swap(after(mlp_far, att_z, att_y, att_yz), "fsdp", 2, fsdp)
        far_own, far_x = lax.optimization_barrier((mlp_far, far_x, act_one))[:2]
        far_parts = gather_parts(far_own, far_x)
    else:
        far_parts = gather_parts(mlp_far)
    piece_f, sum_f = struct((piece, width), f32), struct((8, hidden_part), f32)
    act_two, pre_one, pre_two, back, back_send, down_own, down_send, up_sums = call(
        functools.partial(feed_far, fsdp, ordered),
        "feed_far",
        scalars,
        (normed_two, cot, params, rate_one, up_one, down_one, down_sum, *far_parts),
        (rows_b, rows_b, rows_b, piece_f, half_b, piece_f, half_b, sum_f),
        [pltpu.VMEM((width, hidden_part), bf16)] * 2,
        us=9,
    )
    back_got = swap_z(back_send, 1)
    cut = (2, part) if ordered else (width,)
    grad_outs = [struct((4,) + cut + (hidden_part,))] * (2 if ordered else 1)
    mlp_grads = call(
        functools.partial(feed_grads, ordered),
        "feed_grads",
        scalars,
        (normed_two, cot, act_one, pre_one, act_two, pre_two),
        tuple(grad_outs),
        [pltpu.VMEM((width, hidden_part), bf16)],
        us=8,
    )

    def scatter(parts, name, count, gate, later):
        if not ordered:
            v = lax.psum_scatter(parts[0], "fsdp", scatter_dimension=1, tiled=True)
            each = v.shape[0] // count
            zeros = [jnp.zeros_like(v[:each])] * count
            return v.astype(f32), zeros, zeros[-1:]
        kept, sent = parts
        got = swap(after(sent, *gate), "fsdp", 1, fsdp)
        shape = kept.shape[:1] + kept.shape[2:]
        each = (shape[0] // count,) + shape[1:]
        kept, *sent = call(
            core_sum, name, scalars, (after(kept, later), got), (struct(shape, f32), *[struct(each)] * count), us=2
        )
        return kept, sent, [swap_x(v) for v in sent[-1:]]

    def swap_x(v, *gate):
        return swap(after(v, *gate), "fsdp", 2, fsdp) if ordered else v

    def mine(v):
        return pick(v.reshape((2, piece) + v.shape[1:]), member, 0)

    def spread(rows, dtype, gate=()):
        far = swap_z(rows, 2)
        near = swap_z(rows, 1)
        cross = swap_z(after(far, near, *gate), 1)

        def placed(name, *others):
            parts = (after(rows, *others), near, far, cross)
            return call(
                place_rows, name, z.reshape(1), parts, struct((tp, piece, width), dtype)
            ).reshape(seq_count, half, width)

        return placed, (near, far), cross

    grad_hidden, grad_branch, g0, g1, g2, g3, sums_two = call(
        branch_back,
        "branch_back",
        scalars,
        (back, back_got, hidden, cot, out_proj, params),
        (
            struct((piece, width), f32),
            struct((piece, width)),
            *[struct((group, piece))] * 4,
            struct((8, width), f32),
        ),
    )
    down_got = swap_z(after(down_send, g0), 1)
    g_y, g_yz, g_z = swap_y(g2), swap_yz(g3, 1), swap_z(g1, 1)
    grads_kept, grads_sent, (far_x,) = scatter(mlp_grads, "core_sum_feed", 2, (g0,), g_y)
    result_rows = (mine(hidden) + down_own + down_got.astype(f32) + params[5:6]).astype(bf16)
    result_rows = after(result_rows, g_y, g_yz, g_z)
    place_result, result_gate, result_cross = spread(result_rows, bf16)
    late_outs = [struct((1,) + cut + (7 * group,))] * (2 if ordered else 1)
    n0, n1, n2, n3, sums, *late = call(
        functools.partial(attention_backward, ordered),
        "attention_backward",
        scalars,
        (
            qkv_rows, qkv_turned, after(g0, result_rows, *grads_sent), g_z, g_y, g_yz, logs, proj_rows,
            hat_turned, params.T, grad_branch, att_own, sums_two, up_sums,
        ),
        (*[struct((piece, width))] * 4, struct((16, width), f32), *late_outs),
        [
            pltpu.VMEM((length, 3 * group), bf16),
            pltpu.VMEM((width, 7 * group), bf16),
            pltpu.VMEM((length, HD), f32),
            pltpu.VMEM((length, HD), f32),
        ],
        us=16,
    )
    first_got = swap_y(after(n3, *result_gate, far_x))
    late_kept, late_sent, _ = scatter(
        late, "core_sum_late", 1, (*result_gate, far_x), first_got
    )
    late_first = late_sent[0]
    two_b = struct((2, part, hidden_part))
    far_sum = call(
        functools.partial(x_sum, 1), "x_sum_far", scalars, (after(grads_kept, n3), far_x), two_b, us=2
    )
    far_far = swap_z(far_sum, 2)
    near_x_got = swap_x(grads_sent[0], n3)
    share = n1.astype(f32) + first_got.astype(f32)
    near_got = swap_z(after(share.astype(bf16), result_cross), 1)
    second_got = swap_y(after(n2, first_got))
    token_rows = call(
        token_back,
        "token_back",
        scalars,
        (after(n0, late_first, far_far), second_got, near_got, tok_own, params, grad_hidden),
        struct((piece, width)),
        us=3,
    )
    late_got = swap_x(late_sent[0], first_got)
    near_sum = call(
        functools.partial(x_sum, 0),
        "x_sum_near",
        scalars,
        (after(grads_kept, token_rows), near_x_got, far_far),
        two_b,
        us=2,
    )
    near_other = swap_y(near_sum)
    place_tokens, token_gate, token_cross = spread(
        token_rows, f32, (late_got, near_other)
    )
    sums = after(sums, *token_gate)
    sums = sums + swap_y(sums)
    if ordered:
        sums = sums + swap(sums, "fsdp", 1, fsdp)
        sums = sums + swap(sums, "fsdp", 2, fsdp)
    else:
        sums = lax.psum(sums, "fsdp")
    grad_both = near_sum.astype(f32) + near_other.astype(f32)
    grad_up, grad_down = grad_both[0], grad_both[1].T

    late = late_kept[0] + late_got[0].astype(f32)
    out_got = swap_z(after(late[:, : 2 * group].astype(bf16), *token_gate), 1).astype(f32)
    grad_qkv = late[:, 2 * group : 5 * group].astype(bf16)
    out_first = late[:, 5 * group : 6 * group] + out_got[:, :group]
    out_second = late[:, 6 * group :] + out_got[:, group:]
    out_here = jnp.where(same, out_first, out_second).astype(bf16)
    out_there = jnp.where(same, out_second, out_first).astype(bf16)
    kept = jnp.concatenate([grad_qkv, out_here], axis=1).astype(f32)
    both = (
        kept + swap_z(jnp.concatenate([grad_qkv, out_there], axis=1), 2).astype(f32)
    ).astype(bf16)
    both_got = swap_y(both)
    result = place_result("place_result", token_rows)
    grad_tokens = place_tokens("place_tokens", both)
    grad_qkv = jnp.where(same, both, both_got)[:, : 3 * group].astype(f32)
    grad_qkv = jnp.moveaxis(grad_qkv.reshape(part, 3, group), 1, 0)
    grad_out = (both[:, 3 * group :].astype(f32) + both_got[:, 3 * group :].astype(f32)).T

    sums = after(sums, out_got, token_cross)
    sums = sums + swap_z(sums, 1)
    sums = sums + swap_z(sums, 2)
    norm_sums = pick(sums[:6].reshape(6, fsdp, part), f, 1)
    up_total = pick(sums[6 : 6 + tp], z, 0)
    grad_up_bias = pick(up_total.reshape(bias_rows, fsdp, bias_cols), f, 1)
    qv_total = pick(sums[6 + tp : 6 + 2 * tp, : 2 * group], z, 0)
    grad_qv = pick(qv_total.reshape(2, head_count, fsdp, bias_cols), f, 2)
    return (
        result,
        grad_tokens,
        norm_sums[0:2],
        norm_sums[2:4],
        grad_qkv,
        grad_qv,
        grad_out,
        norm_sums[4:6],
        grad_up,
        grad_up_bias,
        grad_down,
    )


def solution(mesh):
    in_specs = (
        P("fsdp", "ctx", None),
        P("fsdp", "ctx"),
        P(None, "fsdp"),
        P(None, "fsdp"),
        P(None, "fsdp", "tp"),
        P(None, "tp", "fsdp"),
        P("tp", "fsdp"),
        P(None, "fsdp"),
        P("fsdp", "tp"),
        P("tp", "fsdp"),
        P("tp", "fsdp"),
        P("fsdp", "ctx", None),
    )
    out_specs = (
        P("fsdp", "ctx", None),
        P("fsdp", "ctx", None),
        P(None, "fsdp"),
        P(None, "fsdp"),
        P(None, "fsdp", "tp"),
        P(None, "tp", "fsdp"),
        P("tp", "fsdp"),
        P(None, "fsdp"),
        P("fsdp", "tp"),
        P("tp", "fsdp"),
        P("tp", "fsdp"),
    )
    local = functools.partial(
        block, fsdp=mesh.shape["fsdp"], ctx=mesh.shape["ctx"], tp=mesh.shape["tp"]
    )
    return jax.shard_map(local, mesh=mesh, in_specs=in_specs, out_specs=out_specs, check_vma=False)
```
